32 devices in a mesh: gx: 4 (over z), gy: 8 (over y, x, core).
Axes of the slice: x: 2, y: 2, z: 4, core: 2. Of those that a mesh axis runs over, the one named last changes fastest.
Arguments:
- source: float32 [64, 256, 512], P('gx', 'gy')
- voxel_phase: int32 [64, 256, 512], P('gx', 'gy'), may hold values from 0 to 2
- lin_potential: float32 [64, 256, 512], P('gx', 'gy'), may hold values from -1 to 1
- link_voxel: int32 [4, 8, 2048], P('gx', 'gy'), may hold values from 0 to 262143
- link_count: int32 [4, 8, 8], P('gx', 'gy'), may hold values from 1 to 256, as said below
- link_target: int32 [4, 8, 2048], P('gx', 'gy'), may hold values from 0 to 511
Outputs:
- solution: float32 [64, 256, 512], P('gx', 'gy')
- particle_current: float32 [4, 8, 512], P('gx', 'gy')
The draws below stay inside these ranges and needn't reach their ends.
Inputs may be any that keep to these rules, and one draw needn't show every extreme that they name: `link_count`: every device has exactly 256 live links to at least one gy peer.
All inputs are finite; a program needn't handle non-finite values.
Results may differ from the reference program's by a relative error of at most 0.00012.
Values sent between devices are 32-bit elements; how exact they have to be, the bound alone decides.
A program may use at most 128 MiB of HBM per device.

```python
import jax
import jax.numpy as jnp

CX = 16
CY = 32
CZ = 512
ITERS = 12
CAP = 256
PART_DEV = 512
VOX = 262144
NX = 64
NY = 256
NZ = 512
N_GX = 4
N_GY = 8


def draw_source(key, part):
    first_key = jax.random.fold_in(key, 0)
    xcoord = jnp.arange(NX).astype(jnp.float32) / NX
    ycoord = jnp.arange(NY).astype(jnp.float32) / NY
    ramp = (1.0 + 2.0 * xcoord)[:, None, None] * (1.0 + ycoord)[None, :, None]
    rough = jax.random.normal(first_key, (NX, NY, NZ), jnp.float32)
    return ramp * rough


def draw_link_count(key, part):
    load_key, count_key, full_key = jax.random.split(key, 3)
    load = jax.random.randint(load_key, (N_GX, N_GY, 1), 2, 5)
    highest = CAP * load // 4
    counts = jax.random.randint(count_key, (N_GX, N_GY, N_GY), highest // 2, highest + 1)
    full_peer = jax.random.randint(full_key, (N_GX, N_GY, 1), 0, N_GY)
    peer_ids = jnp.arange(N_GY)[None, None, :]
    return jnp.where(peer_ids == full_peer, CAP, counts).astype(jnp.int32)


def touch_ends(values, key, low, top_value):
    spot = [jax.random.randint(jax.random.fold_in(key, axis), (), 0, length) for axis, length in enumerate(values.shape)]
    longest = values.shape.index(max(values.shape))
    next_to = spot[:longest] + [(spot[longest] + 1) % values.shape[longest]] + spot[longest + 1:]
    return values.at[tuple(spot)].set(low).at[tuple(next_to)].set(top_value)


def level_of(stream_key, dims, cuts, smallest, high):
    level, own = 1.0, jax.random.fold_in(stream_key, 6)
    for axis_at, blocks in cuts:
        steps = jnp.exp(jax.random.uniform(jax.random.fold_in(own, axis_at), (blocks,), jnp.float32, smallest / len(cuts), high / len(cuts)))
        level = level * jnp.repeat(steps, dims[axis_at] // blocks).reshape([-1 if axis == axis_at else 1 for axis in range(len(dims))])
    return level


def setup_inputs(seed: int = 0) -> dict:
    keys = jax.random.split(jax.random.key(seed), 7)
    source = draw_source(jax.random.fold_in(keys[6], 71), 0)
    voxel_phase = touch_ends(jax.random.randint(keys[1], (NX, NY, NZ), 0, 3), jax.random.fold_in(keys[1], 1), 0, 2).astype(jnp.int32)
    lin_potential = jnp.clip(jax.random.uniform(keys[2], (NX, NY, NZ), jnp.float32, -1.0, 1.0) * level_of(keys[2], (NX, NY, NZ), ((0, 4), (1, 8)), -0.4, 0.0), -1.0, 1.0)
    link_voxel = touch_ends(jax.random.randint(keys[3], (N_GX, N_GY, N_GY * CAP), 0, VOX), jax.random.fold_in(keys[3], 1), 0, VOX - 1).astype(jnp.int32)
    link_count = draw_link_count(jax.random.fold_in(keys[6], 71), 0)
    link_target = touch_ends(jax.random.randint(keys[5], (N_GX, N_GY, N_GY * CAP), 0, PART_DEV), jax.random.fold_in(keys[5], 1), 0, PART_DEV - 1).astype(jnp.int32)
    return dict(source=source, voxel_phase=voxel_phase, lin_potential=lin_potential, link_voxel=link_voxel, link_count=link_count, link_target=link_target)


def rate_of(voxel_phase):
    return jnp.where(voxel_phase == 1, 0.3, jnp.where(voxel_phase == 2, 0.08, 0.02)).astype(jnp.float32)


def butler(lin_potential):
    rising = jnp.exp(0.4 * lin_potential)
    falling = jnp.exp(-0.6 * lin_potential)
    return rising - falling, 0.4 * rising + 0.6 * falling


def operate_whole(values, diagonal):
    padded = jnp.pad(values, 1)
    beside = padded[2:, 1:-1, 1:-1] + padded[:-2, 1:-1, 1:-1]
    beside = beside + padded[1:-1, 2:, 1:-1] + padded[1:-1, :-2, 1:-1]
    beside = beside + padded[1:-1, 1:-1, 2:] + padded[1:-1, 1:-1, :-2]
    return diagonal * values - beside


def reference(source, voxel_phase, lin_potential, link_voxel, link_count, link_target):
    base, slope = butler(lin_potential)
    diagonal = 6.0 + rate_of(voxel_phase) * slope
    solution = jnp.zeros_like(source)
    residual = source
    precond = residual / diagonal
    direction = precond
    norm_now = jnp.sum(residual * precond)
    for iteration in range(ITERS):
        image = operate_whole(direction, diagonal)
        alpha = norm_now / jnp.sum(direction * image)
        solution = solution + alpha * direction
        residual = residual - alpha * image
        precond = residual / diagonal
        norm_next = jnp.sum(residual * precond)
        direction = precond + (norm_next / norm_now) * direction
        norm_now = norm_next
    current = base + slope * solution
    blocks = current.reshape(N_GX, CX, N_GY, CY, CZ).transpose(0, 2, 1, 3, 4).reshape(N_GX, N_GY, CX * CY * CZ)
    picked = jnp.take_along_axis(blocks, link_voxel.astype(jnp.int32), axis=2)
    slot_ids = jnp.arange(N_GY * CAP).astype(jnp.int32)
    peer_ids = slot_ids // CAP
    within = slot_ids % CAP
    live = within[None, None, :] < link_count[:, :, peer_ids]
    sent = jnp.where(live, 0.5 * picked, jnp.float32(0.0))
    received = sent.reshape(N_GX, N_GY, N_GY, CAP).transpose(0, 2, 1, 3).reshape(N_GX, N_GY, N_GY * CAP)

    def owner_sum(values, targets):
        return jax.ops.segment_sum(values, targets, num_segments=PART_DEV)

    particle_current = jax.vmap(jax.vmap(owner_sum))(received, link_target)
    return solution, particle_current
```

```python
import functools

import jax
import jax.numpy as jnp
import numpy as np
from jax import lax
from jax.experimental import pallas as pl
from jax.experimental.pallas import tpu as pltpu
from jax.sharding import PartitionSpec as P

ITERS = 12
PART_DEV = 512
ROWS = 16
RHS = 15
PAD = 8
LOW = 64
F32 = jnp.float32


def gram_map():
    s = ITERS
    n = 2 * s

    def unit(at):
        out = np.zeros(n)
        out[at] = 1.0
        return out

    m = []
    for k in range(s):
        m.append(2 * unit(2 * k) - unit(0))
        m.append(2 * unit(2 * k + 1) - unit(1))

    def entry(j, k):
        a, b = j + k, abs(j - k)
        return 0.5 * (
            m[a] - 0.5 * (m[a + 1] + m[abs(a - 1)]) + m[b] - 0.5 * (m[b + 1] + m[abs(b - 1)])
        )

    table = np.zeros((n, ROWS, 128))
    for j in range(s):
        table[:, j, RHS] = m[j]
        for k in range(s):
            table[:, j, k] = entry(j, k)
    return table.astype(np.float32)


def two_sum(a, b):
    s = a + b
    t = s - a
    return s, (a - (s - t)) + (b - t)


def quick_two_sum(a, b):
    s = a + b
    return s, b - (s - a)


def split(a):
    c = 4097.0 * a
    hi = c - (c - a)
    return hi, a - hi


def two_prod(a, b):
    p = a * b
    ah, al = split(a)
    bh, bl = split(b)
    return p, ((ah * bh - p) + ah * bl + al * bh) + al * bl


def dd_add(a, b):
    s, e = two_sum(a[0], b[0])
    return quick_two_sum(s, e + (a[1] + b[1]))


def dd_mul(a, b):
    p, e = two_prod(a[0], b[0])
    return quick_two_sum(p, e + (a[0] * b[1] + a[1] * b[0]))


def dd_inverse(a):
    x = 1.0 / a[0]
    p, e = two_prod(a[0], x)
    r = (1.0 - p) - e - a[1] * x
    return quick_two_sum(x, x * r)


def dd_solve(matrix):
    count = ITERS
    rows = lax.broadcasted_iota(jnp.int32, (ROWS, 128), 0)
    lanes = lax.broadcasted_iota(jnp.int32, (ROWS, 128), 1)
    shape = (ROWS, 128)
    for j in range(count):
        column = tuple(jnp.broadcast_to(m[:, j : j + 1], shape) for m in matrix)
        pivot = tuple(c[j : j + 1, :] for c in column)
        row = tuple(m[j : j + 1, :] for m in matrix)
        row = dd_mul(row, dd_inverse(pivot))
        row = tuple(jnp.broadcast_to(r, shape) for r in row)
        step = dd_mul(column, row)
        less = dd_add(matrix, (-step[0], -step[1]))
        matrix = tuple(jnp.where(rows == j, r, m) for r, m in zip(row, less))
    answer = matrix[0][:, RHS : RHS + 1]
    return [jnp.broadcast_to(answer[j : j + 1, :], (8, 128)) for j in range(count)]


def kernel(
    sizes, source_hbm, phase_hbm, potential_hbm, map_hbm, voxel_hbm, count, target_hbm, out, particle,
    source, phase, potential, table, voxel, target, vecs, diag, inv, base, slope, ybuf, yhalo,
    dots, mine, parts, pick, flat, sent, got, stage,
    isem, osem, xsend, xrecv, ysend, yrecv, rsend, rrecv, lsend, lrecv,
):
    n_gx, n_gy = sizes
    total = n_gx * n_gy
    cx, cy, cz = source_hbm.shape
    tiles = cz // 128
    pitch = cy + PAD
    plane = tiles * pitch
    s = ITERS
    gx, gy = lax.axis_index("gx"), lax.axis_index("gy")
    me = gx * n_gy + gy
    mesh_id = pl.DeviceIdType.MESH

    barrier = pltpu.get_barrier_semaphore()

    @pl.loop(1, total)
    def _(step):
        t = lax.rem(me + step, total)
        pl.semaphore_signal(
            barrier, inc=1, device_id=(t // n_gy, lax.rem(t, n_gy)), device_id_type=mesh_id
        )

    loads = []
    for c in range(tiles):
        for i, (src, dst) in enumerate(
            ((potential_hbm, potential), (phase_hbm, phase), (source_hbm, source))
        ):
            loads.append(
                pltpu.make_async_copy(
                    src.at[:, :, pl.ds(128 * c, 128)], dst.at[c], isem.at[c, i]
                )
            )
    extra = [
        pltpu.make_async_copy(voxel_hbm, voxel, isem.at[tiles, 0]),
        pltpu.make_async_copy(target_hbm, target, isem.at[tiles, 1]),
        pltpu.make_async_copy(map_hbm, table, isem.at[tiles, 2]),
    ]
    for copy in loads + extra:
        copy.start()

    has_up, has_down = gx < n_gx - 1, gx > 0
    has_right, has_left = gy < n_gy - 1, gy > 0

    def row(x, c, y):
        return ((x + 1) * tiles + c) * pitch + PAD + y

    def flat_row(x, c, y):
        return (x * tiles + c) * cy + y

    zeros8 = jnp.zeros((8, 128), F32)

    @pl.loop(0, cx)
    def _(x):
        for c in range(tiles):
            for y in range(0, cy, 8):
                vecs[0, pl.ds(row(x, c, y), 8), :] = zeros8

    @pl.when(gx == 0)
    def _():
        @pl.loop(1, s + 1)
        def _(k):
            for c in range(tiles):
                for y in range(0, cy, 8):
                    vecs[k, pl.ds(row(-1, c, y), 8), :] = zeros8

    @pl.when(gx == n_gx - 1)
    def _():
        @pl.loop(1, s + 1)
        def _(k):
            for c in range(tiles):
                for y in range(0, cy, 8):
                    vecs[k, pl.ds(row(cx, c, y), 8), :] = zeros8

    for side, at_edge in ((0, gy == 0), (1, gy == n_gy - 1)):
        @pl.when(at_edge)
        def _():
            @pl.loop(1, s + 1)
            def _(k):
                for c in range(tiles):
                    yhalo[k, c, side] = jnp.zeros((cx, 128), F32)

    dots[...] = jnp.zeros(dots.shape, F32)

    def pack_rows(k, c):
        for side, y in ((0, 0), (1, cy - 1)):
            for x in range(0, cx, 8):
                ybuf[k, c, side, pl.ds(x, 8), :] = vecs[k, pl.ds(row(x, c, y), 8, stride=plane), :]

    def unpack_rows(k, c):
        for side, y in ((0, -1), (1, cy)):
            for x in range(0, cx, 8):
                vecs[k, pl.ds(row(x, c, y), 8, stride=plane), :] = yhalo[k, c, side, pl.ds(x, 8), :]

    def xcopy(k, c, way):
        up = way == 0
        there = jnp.minimum(gx + 1, n_gx - 1) if up else jnp.maximum(gx - 1, 0)
        return pltpu.make_async_remote_copy(
            src_ref=vecs.at[k, pl.ds(row(cx - 1 if up else 0, c, 0), cy), :],
            dst_ref=vecs.at[k, pl.ds(row(-1 if up else cx, c, 0), cy), :],
            send_sem=xsend.at[way], recv_sem=xrecv.at[k, c, way],
            device_id=(there, gy), device_id_type=mesh_id,
        )

    def ycopy(k, c, way):
        right = way == 0
        there = jnp.minimum(gy + 1, n_gy - 1) if right else jnp.maximum(gy - 1, 0)
        return pltpu.make_async_remote_copy(
            src_ref=ybuf.at[k, c, 1 if right else 0],
            dst_ref=yhalo.at[k, c, 0 if right else 1],
            send_sem=ysend.at[way], recv_sem=yrecv.at[k, c, way],
            device_id=(gx, there), device_id_type=mesh_id,
        )

    for copy in extra[:1]:
        copy.wait()

    for c in range(tiles):
        for copy in loads[3 * c : 3 * c + 3]:
            copy.wait()

        @pl.loop(0, cx)
        def _(x):
            for y in range(0, cy, 8):
                at = potential[c, x, y : y + 8, :]
                rising = jnp.exp(0.4 * at)
                falling = jnp.exp(-0.6 * at)
                label = phase[c, x, y : y + 8, :]
                rate = jnp.where(label == 1, 0.3, jnp.where(label == 2, 0.08, 0.02)).astype(F32)
                bend = 0.4 * rising + 0.6 * falling
                d = 6.0 + rate * bend
                i = 1.0 / d
                f = pl.ds(flat_row(x, c, y), 8)
                base[f, :] = rising - falling
                slope[f, :] = bend
                diag[f, :] = d
                inv[f, :] = i
                vecs[1, pl.ds(row(x, c, y), 8), :] = source[c, x, y : y + 8, :] * i

        pack_rows(1, c)

    def launch_x(k, c):
        pl.when(has_up)(xcopy(k, c, 0).start)
        pl.when(has_down)(xcopy(k, c, 1).start)

    def launch_y(k, c):
        pl.when(has_right)(ycopy(k, c, 0).start)
        pl.when(has_left)(ycopy(k, c, 1).start)

    with jax.named_scope("barrier"):
        pl.semaphore_wait(barrier, total - 1)

    for c in range(tiles):
        launch_x(1, c)
        launch_y(1, c)

    lane8 = lax.broadcasted_iota(jnp.int32, (8, 128), 1)
    first_lane, last_lane = lane8 == 0, lane8 == 127

    def chunk(k, c, xs, scale, carry):
        own, cross = carry
        found = []
        for x in xs:
            for y in range(0, cy, 8):
                r = row(x, c, y)
                f = pl.ds(flat_row(x, c, y), 8)
                v = vecs[k, pl.ds(r, 8), :]
                before = vecs[k, pl.ds(r - pitch, 8), :] if c > 0 else 0.0
                after = vecs[k, pl.ds(r + pitch, 8), :] if c < tiles - 1 else 0.0
                z = pltpu.roll(jnp.where(last_lane, before, v), 1, 1)
                z = z + pltpu.roll(jnp.where(first_lane, after, v), 127, 1)
                n = vecs[k, pl.ds(r - 1, 8), :] + vecs[k, pl.ds(r + 1, 8), :]
                n = n + (vecs[k, pl.ds(r - plane, 8), :] + vecs[k, pl.ds(r + plane, 8), :])
                new = (scale * inv[f, :]) * (n + z) - vecs[k - 1, pl.ds(r, 8), :]
                w = diag[f, :] * v
                own = own + w * v
                cross = cross + w * new
                found.append((r, new))
        for r, new in found:
            vecs[k + 1, pl.ds(r, 8), :] = new
        return own, cross

    group = 7 if (cx - 2) % 7 == 0 else 1

    @pl.loop(1, s + 1)
    def _(k):
      with jax.named_scope("chainstep"):
        scale = jnp.where(k == 1, 1.0, 2.0).astype(F32)
        for c in range(tiles):
            pl.when(has_left)(ycopy(k, c, 0).wait_recv)
            pl.when(has_right)(ycopy(k, c, 1).wait_recv)
            unpack_rows(k, c)
            pl.when(has_down)(xcopy(k, c, 0).wait_recv)
            pl.when(has_up)(xcopy(k, c, 1).wait_recv)
            carry = (zeros8, zeros8)
            carry = chunk(k, c, (0, cx - 1), scale, carry)

            @pl.when(k < s)
            def _():
                launch_x(k + 1, c)

            def some(i, a):
                return chunk(k, c, [group * i + 1 + x for x in range(group)], scale, a)

            carry = lax.fori_loop(0, (cx - 2) // group, some, carry)
            at = pl.ds(pl.multiple_of(16 * (k - 1), 8), 8)
            dots[at, :] = dots[at, :] + carry[0]
            at = pl.ds(pl.multiple_of(16 * (k - 1) + 8, 8), 8)
            dots[at, :] = dots[at, :] + carry[1]

            @pl.when(k < s)
            def _():
                pack_rows(k + 1, c)
                launch_y(k + 1, c)

    for copy in extra[1:]:
        copy.wait()

    with jax.named_scope("reduce"):
        sums = []
        for g in range(2 * s // 8):
            level = [dots[pl.ds(64 * g + i, 8, stride=8), :] for i in range(8)]
            level = [two_sum(level[2 * i], level[2 * i + 1]) for i in range(4)]
            while len(level) > 1:
                level = [dd_add(level[2 * i], level[2 * i + 1]) for i in range(len(level) // 2)]
            sums.append(level[0])
        for shift in (64, 32, 16, 8, 4, 2, 1):
            sums = [
                dd_add(a, tuple(pltpu.roll(p, shift, 1) for p in a)) for a in sums
            ]
        sub8 = lax.broadcasted_iota(jnp.int32, (8, 128), 0)
        spread = zeros8
        for g, (hi, lo) in enumerate(sums):
            spread = jnp.where(lane8 == sub8 + 8 * g, hi, spread)
            spread = jnp.where(lane8 == sub8 + 8 * g + LOW, lo, spread)
        line = jnp.sum(spread, axis=0, keepdims=True)
        mine[...] = line
        parts[pl.ds(me, 1), :] = line

        def move(owner, there):
            return pltpu.make_async_remote_copy(
                src_ref=mine, dst_ref=parts.at[pl.ds(owner, 1), :],
                send_sem=rsend, recv_sem=rrecv.at[owner],
                device_id=(there // n_gy, lax.rem(there, n_gy)), device_id_type=mesh_id,
            )

        @pl.loop(1, total)
        def _(step):
            move(me, lax.rem(me + step, total)).start()

        def drained(ref, sem):
            pltpu.make_async_copy(ref, ref, sem).wait()

        bulk = s * tiles * cy
        for way, there in ((0, has_up), (1, has_down)):
            @pl.when(there)
            def _():
                drained(stage.at[pl.ds(0, bulk), :], xsend.at[way])
        bulk = s * tiles * cx
        for way, there in ((0, has_right), (1, has_left)):
            @pl.when(there)
            def _():
                drained(stage.at[pl.ds(0, bulk), :], ysend.at[way])

        @pl.loop(1, total)
        def _(step):
            other = lax.rem(me + step, total)
            move(other, other).wait_recv()

    with jax.named_scope("solve"):
        level = [parts[8 * i : 8 * i + 8, :] for i in range(total // 8)]
        level = [(a, pltpu.roll(a, 128 - LOW, 1)) for a in level]
        while len(level) > 1:
            level = [dd_add(level[2 * i], level[2 * i + 1]) for i in range(len(level) // 2)]
        every = level[0]
        for shift in (4, 2, 1):
            every = dd_add(every, tuple(pltpu.roll(p, shift, 0) for p in every))
        terms = []
        for m in range(2 * s):
            hi, lo = (jnp.broadcast_to(p[0:1, m : m + 1], (ROWS, 128)) for p in every)
            terms.append((table[m] * hi, table[m] * lo))
        while len(terms) > 1:
            terms = [
                dd_add(terms[i], terms[i + 1]) if i + 1 < len(terms) else terms[i]
                for i in range(0, len(terms), 2)
            ]
        weights = dd_solve(terms[0])

    with jax.named_scope("combine"):
        @pl.loop(0, cx)
        def _(x):
            for c in range(tiles):
                for y in range(0, cy, 8):
                    pieces = [
                        w * vecs[1 + k, pl.ds(row(x, c, y), 8), :] for k, w in enumerate(weights)
                    ]
                    while len(pieces) > 1:
                        pieces = [sum(pieces[i : i + 2]) for i in range(0, len(pieces), 2)]
                    out[x, y : y + 8, 128 * c : 128 * (c + 1)] = pieces[0]
                    f = pl.ds(flat_row(x, c, y), 8)
                    at = (x * cy + y) * tiles + c
                    flat[pl.ds(at, 8, stride=tiles), :] = base[f, :] + slope[f, :] * pieces[0]

    groups = target.shape[0]
    wide = groups // n_gy
    lane = lax.broadcasted_iota(jnp.int32, (1, 128), 1)

    with jax.named_scope("gather"):
        @pl.loop(0, n_gy)
        def _(peer):
            live = count[peer]
            for part in range(wide):
                group = peer * wide + part

                @pl.loop(0, 128, step=32)
                def _(start):
                    for i in range(32):
                        at = group * 128 + start + i
                        v = voxel[at]
                        line = flat[pl.ds(v >> 7, 1), :]
                        pick[pl.ds(start + i, 1), :] = jnp.where(lane == (v & 127), line, 0.0)

                current = jnp.sum(pick[...].T, axis=0, keepdims=True)
                sent[peer, part : part + 1, :] = jnp.where(
                    lane + 128 * part < live, 0.5 * current, 0.0
                )

    def link(owner, peer):
        return pltpu.make_async_remote_copy(
            src_ref=sent.at[peer], dst_ref=got.at[owner], send_sem=lsend.at[peer],
            recv_sem=lrecv.at[owner], device_id=(gx, peer), device_id_type=mesh_id,
        )

    with jax.named_scope("links"):
        @pl.loop(1, n_gy)
        def _(step):
            link(gy, lax.rem(gy + step, n_gy)).start()

        got[gy] = sent[gy]

        @pl.loop(1, total)
        def _(step):
            move(me, lax.rem(me + step, total)).wait_send()

        @pl.loop(1, n_gy)
        def _(step):
            other = lax.rem(gy + step, n_gy)
            link(other, other).wait_recv()

    with jax.named_scope("scatter"):
        own = particle.shape[2]
        sub = lax.broadcasted_iota(jnp.int32, (128, 128), 0)
        for start in range(0, own, 128):
            def add(peer, acc):
                for part in range(wide):
                    spot = target[pl.ds(peer * wide + part, 1), :]
                    acc = acc + jnp.where(spot - start == sub, got[peer, part : part + 1, :], 0.0)
                return acc

            acc = lax.fori_loop(0, n_gy, add, jnp.zeros((128, 128), F32))
            particle[0, :, start : start + 128] = jnp.sum(acc.T, axis=0, keepdims=True)

        @pl.loop(1, n_gy)
        def _(step):
            link(gy, lax.rem(gy + step, n_gy)).wait_send()


def kept(x):
    return pltpu.with_memory_space_constraint(x, pltpu.HBM)


def shards(sizes, source, voxel_phase, lin_potential, link_voxel, link_count, link_target):
    cx, cy, cz = source.shape
    total = sizes[0] * sizes[1]
    s = ITERS
    tiles = cz // 128
    voxels = cx * cy * tiles
    padded = (cx + 2) * tiles * (cy + PAD) + 8
    peers = link_count.shape[2]
    slots = link_voxel.shape[2]
    groups = slots // 128
    whole = pl.BlockSpec(memory_space=pltpu.VMEM)
    far = pl.BlockSpec(memory_space=pltpu.HBM)
    scalars = pl.BlockSpec(memory_space=pltpu.SMEM)
    return pl.pallas_call(
        functools.partial(kernel, sizes),
        out_shape=(
            jax.ShapeDtypeStruct(source.shape, F32),
            jax.ShapeDtypeStruct((1, 1, PART_DEV), F32),
        ),
        in_specs=[far] * 5 + [scalars, far],
        out_specs=(whole, whole),
        scratch_shapes=[
            pltpu.VMEM((tiles, cx, cy, 128), F32),
            pltpu.VMEM((tiles, cx, cy, 128), jnp.int32),
            pltpu.VMEM((tiles, cx, cy, 128), F32),
            pltpu.VMEM((2 * s, ROWS, 128), F32),
            pltpu.SMEM((slots,), jnp.int32),
            pltpu.VMEM((groups, 128), jnp.int32),
            pltpu.VMEM((s + 2, padded, 128), F32),
            pltpu.VMEM((voxels, 128), F32),
            pltpu.VMEM((voxels, 128), F32),
            pltpu.VMEM((voxels, 128), F32),
            pltpu.VMEM((voxels, 128), F32),
            pltpu.VMEM((s + 1, tiles, 2, cx, 128), F32),
            pltpu.VMEM((s + 1, tiles, 2, cx, 128), F32),
            pltpu.VMEM((2 * s * 8, 128), F32),
            pltpu.VMEM((1, 128), F32),
            pltpu.VMEM((total, 128), F32),
            pltpu.VMEM((128, 128), F32),
            pltpu.VMEM((voxels, 128), F32),
            pltpu.VMEM((peers, groups // peers, 128), F32),
            pltpu.VMEM((peers, groups // peers, 128), F32),
            pltpu.VMEM((s * tiles * max(cx, cy), 128), F32),
            pltpu.SemaphoreType.DMA((tiles + 1, 3)),
            pltpu.SemaphoreType.DMA,
            pltpu.SemaphoreType.DMA((2,)),
            pltpu.SemaphoreType.DMA((s + 1, tiles, 2)),
            pltpu.SemaphoreType.DMA((2,)),
            pltpu.SemaphoreType.DMA((s + 1, tiles, 2)),
            pltpu.SemaphoreType.DMA,
            pltpu.SemaphoreType.DMA((total,)),
            pltpu.SemaphoreType.DMA((peers,)),
            pltpu.SemaphoreType.DMA((peers,)),
        ],
        compiler_params=pltpu.CompilerParams(
            collective_id=0, has_side_effects=True, vmem_limit_bytes=48 * 2**20
        ),
    )(
        kept(source), kept(voxel_phase), kept(lin_potential), kept(jnp.asarray(gram_map())),
        kept(link_voxel[0, 0]), kept(link_count[0, 0]), kept(link_target[0, 0].reshape(groups, 128)),
    )


def solution(mesh):
    spec = P("gx", "gy", None)
    return jax.shard_map(
        functools.partial(shards, (mesh.shape["gx"], mesh.shape["gy"])),
        mesh=mesh,
        in_specs=(spec,) * 6,
        out_specs=(spec, spec),
        check_vma=False,
    )
```

```python
import functools

import jax
import jax.numpy as jnp
import numpy as np
from jax import lax
from jax.experimental import pallas as pl
from jax.experimental.pallas import tpu as pltpu
from jax.sharding import PartitionSpec as P

ITERS = 12
PART_DEV = 512
ROWS = 16
RHS = 15
PAD = 8
LOW = 64
F32 = jnp.float32


def gram_map():
    s = ITERS
    n = 2 * s

    def unit(at):
        out = np.zeros(n)
        out[at] = 1.0
        return out

    m = []
    for k in range(s):
        m.append(2 * unit(2 * k) - unit(0))
        m.append(2 * unit(2 * k + 1) - unit(1))

    def entry(j, k):
        a, b = j + k, abs(j - k)
        return 0.5 * (
            m[a] - 0.5 * (m[a + 1] + m[abs(a - 1)]) + m[b] - 0.5 * (m[b + 1] + m[abs(b - 1)])
        )

    table = np.zeros((n, ROWS, 128))
    for j in range(s):
        table[:, j, RHS] = m[j]
        for k in range(s):
            table[:, j, k] = entry(j, k)
    return table.astype(np.float32)


def two_sum(a, b):
    s = a + b
    t = s - a
    return s, (a - (s - t)) + (b - t)


def quick_two_sum(a, b):
    s = a + b
    return s, b - (s - a)


def split(a):
    c = 4097.0 * a
    hi = c - (c - a)
    return hi, a - hi


def two_prod(a, b):
    p = a * b
    ah, al = split(a)
    bh, bl = split(b)
    return p, ((ah * bh - p) + ah * bl + al * bh) + al * bl


def dd_add(a, b):
    s, e = two_sum(a[0], b[0])
    return quick_two_sum(s, e + (a[1] + b[1]))


def dd_mul(a, b):
    p, e = two_prod(a[0], b[0])
    return quick_two_sum(p, e + (a[0] * b[1] + a[1] * b[0]))


def dd_inverse(a):
    x = 1.0 / a[0]
    p, e = two_prod(a[0], x)
    r = (1.0 - p) - e - a[1] * x
    return quick_two_sum(x, x * r)


def dd_solve(matrix):
    count = ITERS
    rows = lax.broadcasted_iota(jnp.int32, (ROWS, 128), 0)
    lanes = lax.broadcasted_iota(jnp.int32, (ROWS, 128), 1)
    shape = (ROWS, 128)
    for j in range(count):
        column = tuple(jnp.broadcast_to(m[:, j : j + 1], shape) for m in matrix)
        pivot = tuple(c[j : j + 1, :] for c in column)
        row = tuple(m[j : j + 1, :] for m in matrix)
        row = dd_mul(row, dd_inverse(pivot))
        row = tuple(jnp.broadcast_to(r, shape) for r in row)
        step = dd_mul(column, row)
        less = dd_add(matrix, (-step[0], -step[1]))
        matrix = tuple(jnp.where(rows == j, r, m) for r, m in zip(row, less))
    answer = matrix[0][:, RHS : RHS + 1]
    return [jnp.broadcast_to(answer[j : j + 1, :], (8, 128)) for j in range(count)]


def kernel(
    sizes, source_hbm, phase_hbm, potential_hbm, map_hbm, voxel_hbm, places_hbm, count, target_hbm,
    out, particle,
    source, phase, potential, table, voxel, places, target, vecs, diag, inv, base, slope, ybuf, hin,
    pinv, hinv, hodd, mask, dots, mine, parts, pick, flat, sent, got,
    isem, xsend, xrecv, ysend, yrecv, csend, crecv, vsend, vrecv, rsend, rrecv, lsend, lrecv,
):
    n_gx, n_gy = sizes
    total = n_gx * n_gy
    cx, cy, cz = source_hbm.shape
    tiles = cz // 128
    pitch = cy + PAD
    block = (cx + 4) * pitch
    s = ITERS
    cycles = s // 2
    gx, gy = lax.axis_index("gx"), lax.axis_index("gy")
    me = gx * n_gy + gy
    mesh_id = pl.DeviceIdType.MESH

    barrier = pltpu.get_barrier_semaphore()

    @pl.loop(1, total)
    def _(step):
        t = lax.rem(me + step, total)
        pl.semaphore_signal(
            barrier, inc=1, device_id=(t // n_gy, lax.rem(t, n_gy)), device_id_type=mesh_id
        )

    loads = []
    for c in range(tiles):
        for i, (src, dst) in enumerate(
            ((potential_hbm, potential), (phase_hbm, phase), (source_hbm, source))
        ):
            loads.append(
                pltpu.make_async_copy(
                    src.at[:, :, pl.ds(128 * c, 128)], dst.at[c], isem.at[c, i]
                )
            )
    extra = [
        pltpu.make_async_copy(voxel_hbm, voxel, isem.at[tiles, 0]),
        pltpu.make_async_copy(target_hbm, target, isem.at[tiles, 1]),
        pltpu.make_async_copy(map_hbm, table, isem.at[tiles, 2]),
        pltpu.make_async_copy(places_hbm, places, isem.at[tiles + 1, 0]),
    ]
    for copy in loads + extra:
        copy.start()

    has_up, has_down = gx < n_gx - 1, gx > 0
    has_right, has_left = gy < n_gy - 1, gy > 0
    up_gx, down_gx = jnp.minimum(gx + 1, n_gx - 1), jnp.maximum(gx - 1, 0)
    right_gy, left_gy = jnp.minimum(gy + 1, n_gy - 1), jnp.maximum(gy - 1, 0)

    def row(x, c, y):
        return c * block + (x + 2) * pitch + PAD + y

    def inv_row(x, c, y):
        return (c * (cx + 2) + x + 1) * cy + y

    def flat_row(x, c, y):
        return (c * cx + x) * cy + y

    near, low_corner, high_corner = cx, 2 * cx + 1, 2 * cx
    zeros8 = jnp.zeros((8, 128), F32)
    zero_row = jnp.zeros((1, 128), F32)

    @pl.loop(-1, cx + 1)
    def _(x):
        for c in range(tiles):
            for y in range(0, cy, 8):
                vecs[0, pl.ds(row(x, c, y), 8), :] = zeros8

    @pl.loop(0, cycles)
    def _(j):
        @pl.loop(0, cx + 1)
        def _(x):
            for c in range(tiles):
                vecs[2 * j + 1, pl.ds(row(x, c, -PAD), 8), :] = zeros8

    hodd[...] = jnp.zeros(hodd.shape, F32)
    for beyond, x in ((gx == 0, -1), (gx == n_gx - 1, cx)):
        @pl.when(beyond)
        def _():
            for c in range(tiles):
                for y in range(0, cy, 8):
                    inv[pl.ds(inv_row(x, c, y), 8), :] = zeros8

            @pl.loop(0, cycles)
            def _(j):
                for c in range(tiles):
                    first = row(-2 if x < 0 else cx, c, 0)
                    for y in range(0, pitch + cy, 8):
                        vecs[2 * j + 1, pl.ds(first + y, 8), :] = zeros8
                    for side in range(2):
                        hin[j, c, side, pl.ds(low_corner if x < 0 else high_corner, 1), :] = zero_row

    for beyond, side in ((gy == 0, 0), (gy == n_gy - 1, 1)):
        @pl.when(beyond)
        def _():
            hinv[side] = jnp.zeros(hinv.shape[1:], F32)

            @pl.loop(0, cycles)
            def _(j):
                for c in range(tiles):
                    hin[j, c, side] = jnp.zeros(hin.shape[3:], F32)

    sides = ((0, 0, 1), (1, cy - 1, cy - 2))

    def pack_rows(j, c):
        k = 2 * j + 1
        for side, y1, y2 in sides:
            for x in range(0, cx, 8):
                ybuf[j, c, side, pl.ds(near + x, 8), :] = (
                    vecs[k, pl.ds(row(x, c, y1), 8, stride=pitch), :]
                )
                ybuf[j, c, side, pl.ds(x, 8), :] = vecs[k, pl.ds(row(x, c, y2), 8, stride=pitch), :]

    def xcopy(j, c, way):
        up = way == 0
        return pltpu.make_async_remote_copy(
            src_ref=vecs.at[2 * j + 1, pl.ds(row(cx - 2 if up else 0, c, 0), pitch + cy), :],
            dst_ref=vecs.at[2 * j + 1, pl.ds(row(-2 if up else cx, c, 0), pitch + cy), :],
            send_sem=xsend.at[way], recv_sem=xrecv.at[lax.rem(j, 2), c, way],
            device_id=(up_gx if up else down_gx, gy), device_id_type=mesh_id,
        )

    def ycopy(j, c, way):
        right = way == 0
        return pltpu.make_async_remote_copy(
            src_ref=ybuf.at[j, c, 1 if right else 0],
            dst_ref=hin.at[j, c, 0 if right else 1, pl.ds(0, 2 * cx), :],
            send_sem=ysend.at[way], recv_sem=yrecv.at[lax.rem(j, 2), c, way],
            device_id=(gx, right_gy if right else left_gy), device_id_type=mesh_id,
        )

    def ccopy(j, c, xway, yway):
        up, right = xway == 0, yway == 0
        q = 2 * xway + yway
        return pltpu.make_async_remote_copy(
            src_ref=vecs.at[
                2 * j + 1, pl.ds(row(cx - 1 if up else 0, c, cy - 1 if right else 0), 1), :
            ],
            dst_ref=hin.at[j, c, 0 if right else 1, pl.ds(low_corner if up else high_corner, 1), :],
            send_sem=csend.at[q], recv_sem=crecv.at[lax.rem(j, 2), c, q],
            device_id=(up_gx if up else down_gx, right_gy if right else left_gy),
            device_id_type=mesh_id,
        )

    def vcopies(way):
        up = way == 0
        return [
            pltpu.make_async_remote_copy(
                src_ref=inv.at[pl.ds(inv_row(cx - 1 if up else 0, c, 0), cy), :],
                dst_ref=inv.at[pl.ds(inv_row(-1 if up else cx, c, 0), cy), :],
                send_sem=vsend.at[way], recv_sem=vrecv.at[way],
                device_id=(up_gx if up else down_gx, gy), device_id_type=mesh_id,
            )
            for c in range(tiles)
        ]

    def hcopy(way):
        right = way == 0
        return pltpu.make_async_remote_copy(
            src_ref=pinv.at[1 if right else 0], dst_ref=hinv.at[0 if right else 1],
            send_sem=vsend.at[2 + way], recv_sem=vrecv.at[2 + way],
            device_id=(gx, right_gy if right else left_gy), device_id_type=mesh_id,
        )

    for c in range(tiles):
        for copy in loads[3 * c : 3 * c + 3]:
            copy.wait()

        @pl.loop(0, cx)
        def _(x):
            found = []
            for y in range(0, cy, 8):
                at = potential[c, x, y : y + 8, :]
                rising = jnp.exp(0.4 * at)
                falling = jnp.exp(-0.6 * at)
                label = phase[c, x, y : y + 8, :]
                rate = jnp.where(label == 1, 0.3, jnp.where(label == 2, 0.08, 0.02)).astype(F32)
                bend = 0.4 * rising + 0.6 * falling
                d = 6.0 + rate * bend
                i = 1.0 / d
                found.append((y, rising - falling, bend, d, i, source[c, x, y : y + 8, :] * i))
            for y, level, bend, d, i, v in found:
                f = pl.ds(flat_row(x, c, y), 8)
                base[f, :] = level
                slope[f, :] = bend
                diag[f, :] = d
                inv[pl.ds(inv_row(x, c, y), 8), :] = i
                vecs[1, pl.ds(row(x, c, y), 8), :] = v

        pack_rows(0, c)
        for side, y, _ in sides:
            for x in range(0, cx, 8):
                pinv[side, c, pl.ds(x, 8), :] = inv[pl.ds(inv_row(x, c, y), 8, stride=cy), :]

    def launch_x(j, c, more):
        @pl.when(has_up & more)
        def _():
            xcopy(j, c, 0).start()
            pl.when(has_right)(ccopy(j, c, 0, 0).start)
            pl.when(has_left)(ccopy(j, c, 0, 1).start)

        @pl.when(has_down & more)
        def _():
            xcopy(j, c, 1).start()
            pl.when(has_right)(ccopy(j, c, 1, 0).start)
            pl.when(has_left)(ccopy(j, c, 1, 1).start)

    def launch_y(j, c, more):
        pl.when(has_right & more)(ycopy(j, c, 0).start)
        pl.when(has_left & more)(ycopy(j, c, 1).start)

    def landed(j, c):
        @pl.when(has_left)
        def _():
            ycopy(j, c, 0).wait_recv()
            pl.when(has_down)(ccopy(j, c, 0, 0).wait_recv)
            pl.when(has_up)(ccopy(j, c, 1, 0).wait_recv)

        @pl.when(has_right)
        def _():
            ycopy(j, c, 1).wait_recv()
            pl.when(has_down)(ccopy(j, c, 0, 1).wait_recv)
            pl.when(has_up)(ccopy(j, c, 1, 1).wait_recv)

        pl.when(has_down)(xcopy(j, c, 0).wait_recv)
        pl.when(has_up)(xcopy(j, c, 1).wait_recv)

    def drained(rows, sem):
        ref = vecs.at[0, pl.ds(0, rows), :]
        pltpu.make_async_copy(ref, ref, sem).wait()

    with jax.named_scope("barrier"):
        pl.semaphore_wait(barrier, total - 1)

    always = gx >= 0
    for c in range(tiles):
        launch_x(0, c, always)
        launch_y(0, c, always)
    for way, there in ((0, has_up), (1, has_down)):
        @pl.when(there)
        def _():
            for copy in vcopies(way):
                copy.start()
    pl.when(has_right)(hcopy(0).start)
    pl.when(has_left)(hcopy(1).start)

    groups = target.shape[0]
    wide = groups // n_gy
    for copy in extra:
        copy.wait()

    @pl.loop(0, n_gy)
    def _(peer):
        live = count[peer]
        lanes = lax.broadcasted_iota(jnp.int32, (128, 128), 1)
        rows = lax.broadcasted_iota(jnp.int32, (128, 128), 0)
        for part in range(wide):
            at = (places[pl.ds(peer * wide + part, 1), :] & 127).astype(F32)
            at = jnp.broadcast_to(at, (128, 128)).T
            mask[peer * wide + part] = jnp.where(
                (lanes.astype(F32) == at) & (rows + 128 * part < live), 0.5, 0.0
            )

    lane8 = lax.broadcasted_iota(jnp.int32, (8, 128), 1)
    sub8 = lax.broadcasted_iota(jnp.int32, (8, 128), 0)
    first_lane, last_lane = lane8 == 0, lane8 == 127

    def beside(v, before, after):
        z = pltpu.roll(jnp.where(last_lane, before, v), 1, 1)
        return z + pltpu.roll(jnp.where(first_lane, after, v), 127, 1)

    def sweep(k, c, start, offsets, scale, carry=None):
        centers = {}

        def center(o, y):
            if (o, y) not in centers:
                centers[o, y] = vecs[k, pl.ds(row(start + o, c, y), 8), :]
            return centers[o, y]

        found = []
        for y in range(0, cy, 8):
            for o in offsets:
                r = row(start + o, c, y)
                v = center(o, y)
                before = vecs[k, pl.ds(r - block, 8), :] if c > 0 else 0.0
                after = vecs[k, pl.ds(r + block, 8), :] if c < tiles - 1 else 0.0
                n = vecs[k, pl.ds(r - 1, 8), :] + vecs[k, pl.ds(r + 1, 8), :]
                n = (n + beside(v, before, after)) + (center(o - 1, y) + center(o + 1, y))
                i = inv[pl.ds(inv_row(start + o, c, y), 8), :]
                new = (scale * i) * n - vecs[k - 1, pl.ds(r, 8), :]
                if carry is not None:
                    w = diag[pl.ds(flat_row(start + o, c, y), 8), :] * v
                    carry = (carry[0] + w * v, carry[1] + w * new)
                found.append((r, new))
        for r, new in found:
            vecs[k + 1, pl.ds(r, 8), :] = new
        return carry

    def inner(k, c, first, last, scale, carry):
        group = max(g for g in range(1, 8) if (last - first) % g == 0)

        def some(i, a):
            return sweep(k, c, group * i + first, range(group), scale, a)

        return lax.fori_loop(0, (last - first) // group, some, carry)

    def edges(j, c, scale, carry):
        k = 2 * j + 1
        carry = sweep(k, c, 0, (0,), scale, carry)
        carry = sweep(k, c, cx - 1, (0,), scale, carry)
        for side, y in ((0, -1), (1, cy)):
            for x, at in ((-1, low_corner), (cx, high_corner)):
                vecs[k, pl.ds(row(x, c, y), 1), :] = hin[j, c, side, pl.ds(at, 1), :]
        sweep(k, c, -1, (0,), scale)
        sweep(k, c, cx, (0,), scale)
        own, cross = carry
        found = []
        for side, y, beyond in ((0, 0, -1), (1, cy - 1, cy)):
            for x in range(0, cx, 8):
                at = pl.ds(near + x, 8)
                h = hin[j, c, side, at, :]
                mine_ = ybuf[j, c, side, at, :]
                before = hin[j, c - 1, side, at, :] if c > 0 else 0.0
                after = hin[j, c + 1, side, at, :] if c < tiles - 1 else 0.0
                lower = hin[j, c, side, pl.ds(near + x - 1, 8), :]
                if x == 0:
                    corner = hin[j, c, side, pl.ds(low_corner, 1), :]
                    lower = jnp.where(sub8 == 0, corner, lower)
                upper = hin[j, c, side, pl.ds(near + x + 1, 8), :]
                n = (lower + upper) + (hin[j, c, side, pl.ds(x, 8), :] + mine_)
                n = n + beside(h, before, after)
                old = pl.ds(x, 8)
                new = (scale * hinv[side, c, old, :]) * n - hodd[side, c, old, :]
                line = pl.ds(row(x, c, y), 8, stride=pitch)
                fixed = vecs[k + 1, line, :] + (scale * pinv[side, c, old, :]) * h
                cross = cross + (scale * mine_) * h
                found.append((side, old, new, line, fixed, pl.ds(row(x, c, beyond), 8, stride=pitch)))
        for side, old, new, line, fixed, outer in found:
            hodd[side, c, old, :] = new
            vecs[k + 1, line, :] = fixed
            vecs[k + 1, outer, :] = new
        return own, cross

    def finish(j, c, carry):
        k = 2 * j + 2
        more = j < cycles - 1
        carry = sweep(k, c, 0, (0, 1), 2.0, carry)
        carry = sweep(k, c, cx - 2, (0, 1), 2.0, carry)
        launch_x(j + 1, c, more)
        carry = inner(k, c, 2, cx - 2, 2.0, carry)

        @pl.when(more)
        def _():
            pack_rows(j + 1, c)
            launch_y(j + 1, c, always)

        return carry

    @pl.loop(0, cycles)
    def _(j):
        with jax.named_scope("cycle"):
            scale = jnp.where(j == 0, 1.0, 2.0).astype(F32)
            first = second = (zeros8, zeros8)
            with jax.named_scope("ainner"):
                for c in range(tiles):
                    first = inner(2 * j + 1, c, 1, cx - 1, scale, first)

            @pl.when(j == 0)
            def _():
                for way, there in ((0, has_down), (1, has_up)):
                    @pl.when(there)
                    def _():
                        pltpu.make_async_copy(
                            inv.at[pl.ds(0, tiles * cy), :], inv.at[pl.ds(0, tiles * cy), :],
                            vrecv.at[way],
                        ).wait()

                pl.when(has_left)(hcopy(0).wait_recv)
                pl.when(has_right)(hcopy(1).wait_recv)

            with jax.named_scope("landed"):
                landed(j, 0)
            for c in range(tiles):
                if c + 1 < tiles:
                    with jax.named_scope("landed"):
                        landed(j, c + 1)
                first = edges(j, c, scale, first)
                if c > 0:
                    second = finish(j, c - 1, second)
            second = finish(j, tiles - 1, second)
            for i, value in enumerate((*first, *second)):
                dots[pl.ds(pl.multiple_of(32 * j + 8 * i, 8), 8), :] = value

    with jax.named_scope("reduce"):
        sums = []
        for g in range(2 * s // 8):
            level = [dots[pl.ds(64 * g + i, 8, stride=8), :] for i in range(8)]
            level = [two_sum(level[2 * i], level[2 * i + 1]) for i in range(4)]
            while len(level) > 1:
                level = [dd_add(level[2 * i], level[2 * i + 1]) for i in range(len(level) // 2)]
            sums.append(level[0])
        for shift in (64, 32, 16, 8, 4, 2, 1):
            sums = [
                dd_add(a, tuple(pltpu.roll(p, shift, 1) for p in a)) for a in sums
            ]
        spread = zeros8
        for g, (hi, lo) in enumerate(sums):
            spread = jnp.where(lane8 == sub8 + 8 * g, hi, spread)
            spread = jnp.where(lane8 == sub8 + 8 * g + LOW, lo, spread)
        line = jnp.sum(spread, axis=0, keepdims=True)
        mine[...] = line
        parts[pl.ds(me, 1), :] = line

        def move(owner, there):
            return pltpu.make_async_remote_copy(
                src_ref=mine, dst_ref=parts.at[pl.ds(owner, 1), :],
                send_sem=rsend, recv_sem=rrecv,
                device_id=(there // n_gy, lax.rem(there, n_gy)), device_id_type=mesh_id,
            )

        @pl.loop(1, total)
        def _(step):
            move(me, lax.rem(me + step, total)).start()

        for way, there in ((0, has_up), (1, has_down)):
            @pl.when(there)
            def _():
                drained(cycles * tiles * (pitch + cy), xsend.at[way])
                drained(tiles * cy, vsend.at[way])
                for q, also in ((0, has_right), (1, has_left)):
                    @pl.when(also)
                    def _():
                        drained(cycles * tiles, csend.at[2 * way + q])

        for way, there in ((0, has_right), (1, has_left)):
            @pl.when(there)
            def _():
                drained(cycles * tiles * 2 * cx, ysend.at[way])
                drained(tiles * cx, vsend.at[2 + way])

        drained(total - 1, rrecv)

    with jax.named_scope("solve"):
        level = [parts[8 * i : 8 * i + 8, :] for i in range(total // 8)]
        level = [(a, pltpu.roll(a, 128 - LOW, 1)) for a in level]
        while len(level) > 1:
            level = [dd_add(level[2 * i], level[2 * i + 1]) for i in range(len(level) // 2)]
        every = level[0]
        for shift in (4, 2, 1):
            every = dd_add(every, tuple(pltpu.roll(p, shift, 0) for p in every))
        terms = []
        for m in range(2 * s):
            hi, lo = (jnp.broadcast_to(p[0:1, m : m + 1], (ROWS, 128)) for p in every)
            terms.append((table[m] * hi, table[m] * lo))
        while len(terms) > 1:
            terms = [
                dd_add(terms[i], terms[i + 1]) if i + 1 < len(terms) else terms[i]
                for i in range(0, len(terms), 2)
            ]
        weights = dd_solve(terms[0])

    with jax.named_scope("combine"):
        @pl.loop(0, cx)
        def _(x):
            for c in range(tiles):
                for y in range(0, cy, 8):
                    pieces = [
                        w * vecs[1 + k, pl.ds(row(x, c, y), 8), :] for k, w in enumerate(weights)
                    ]
                    while len(pieces) > 1:
                        pieces = [sum(pieces[i : i + 2]) for i in range(0, len(pieces), 2)]
                    out[x, y : y + 8, 128 * c : 128 * (c + 1)] = pieces[0]
                    f = pl.ds(flat_row(x, c, y), 8)
                    at = (x * cy + y) * tiles + c
                    flat[pl.ds(at, 8, stride=tiles), :] = base[f, :] + slope[f, :] * pieces[0]

    with jax.named_scope("gather"):
        @pl.loop(0, n_gy)
        def _(peer):
            for part in range(wide):
                group = peer * wide + part

                @pl.loop(0, 128, step=64)
                def _(start):
                    for i in range(64):
                        v = voxel[group * 128 + start + i]
                        pick[pl.ds(start + i, 1), :] = flat[pl.ds(v >> 7, 1), :]

                found = pick[...] * mask[group]
                sent[peer, part : part + 1, :] = jnp.sum(found.T, axis=0, keepdims=True)

    def link(owner, peer):
        return pltpu.make_async_remote_copy(
            src_ref=sent.at[peer], dst_ref=got.at[owner], send_sem=lsend,
            recv_sem=lrecv, device_id=(gx, peer), device_id_type=mesh_id,
        )

    with jax.named_scope("links"):
        @pl.loop(1, n_gy)
        def _(step):
            link(gy, lax.rem(gy + step, n_gy)).start()

        got[gy] = sent[gy]
        drained(total - 1, rsend)
        drained((n_gy - 1) * wide, lsend)
        drained((n_gy - 1) * wide, lrecv)

    with jax.named_scope("scatter"):
        own = particle.shape[2]
        sub = lax.broadcasted_iota(jnp.int32, (128, 128), 0)
        for start in range(0, own, 128):
            def add(peer, acc):
                for part in range(wide):
                    spot = target[pl.ds(peer * wide + part, 1), :]
                    acc = acc + jnp.where(spot - start == sub, got[peer, part : part + 1, :], 0.0)
                return acc

            acc = lax.fori_loop(0, n_gy, add, jnp.zeros((128, 128), F32))
            particle[0, :, start : start + 128] = jnp.sum(acc.T, axis=0, keepdims=True)


def kept(x):
    return pltpu.with_memory_space_constraint(x, pltpu.HBM)


def shards(sizes, source, voxel_phase, lin_potential, link_voxel, link_count, link_target):
    cx, cy, cz = source.shape
    total = sizes[0] * sizes[1]
    s = ITERS
    tiles = cz // 128
    voxels = cx * cy * tiles
    padded = (cx + 4) * tiles * (cy + PAD) + 8
    cycles = s // 2
    places = link_voxel[0, 0].reshape(-1, 128)
    peers = link_count.shape[2]
    slots = link_voxel.shape[2]
    groups = slots // 128
    whole = pl.BlockSpec(memory_space=pltpu.VMEM)
    far = pl.BlockSpec(memory_space=pltpu.HBM)
    scalars = pl.BlockSpec(memory_space=pltpu.SMEM)
    return pl.pallas_call(
        functools.partial(kernel, sizes),
        out_shape=(
            jax.ShapeDtypeStruct(source.shape, F32),
            jax.ShapeDtypeStruct((1, 1, PART_DEV), F32),
        ),
        in_specs=[far] * 6 + [scalars, far],
        out_specs=(whole, whole),
        scratch_shapes=[
            pltpu.VMEM((tiles, cx, cy, 128), F32),
            pltpu.VMEM((tiles, cx, cy, 128), jnp.int32),
            pltpu.VMEM((tiles, cx, cy, 128), F32),
            pltpu.VMEM((2 * s, ROWS, 128), F32),
            pltpu.SMEM((slots,), jnp.int32),
            pltpu.VMEM((groups, 128), jnp.int32),
            pltpu.VMEM((groups, 128), jnp.int32),
            pltpu.VMEM((s + 2, padded, 128), F32),
            pltpu.VMEM((voxels, 128), F32),
            pltpu.VMEM((tiles * (cx + 2) * cy, 128), F32),
            pltpu.VMEM((voxels, 128), F32),
            pltpu.VMEM((voxels, 128), F32),
            pltpu.VMEM((cycles, tiles, 2, 2 * cx, 128), F32),
            pltpu.VMEM((cycles, tiles, 2, 2 * cx + 8, 128), F32),
            pltpu.VMEM((2, tiles, cx, 128), F32),
            pltpu.VMEM((2, tiles, cx, 128), F32),
            pltpu.VMEM((2, tiles, cx, 128), F32),
            pltpu.VMEM((groups, 128, 128), F32),
            pltpu.VMEM((2 * s * 8, 128), F32),
            pltpu.VMEM((1, 128), F32),
            pltpu.VMEM((total, 128), F32),
            pltpu.VMEM((128, 128), F32),
            pltpu.VMEM((voxels, 128), F32),
            pltpu.VMEM((peers, groups // peers, 128), F32),
            pltpu.VMEM((peers, groups // peers, 128), F32),
            pltpu.SemaphoreType.DMA((tiles + 2, 3)),
            pltpu.SemaphoreType.DMA((2,)),
            pltpu.SemaphoreType.DMA((2, tiles, 2)),
            pltpu.SemaphoreType.DMA((2,)),
            pltpu.SemaphoreType.DMA((2, tiles, 2)),
            pltpu.SemaphoreType.DMA((4,)),
            pltpu.SemaphoreType.DMA((2, tiles, 4)),
            pltpu.SemaphoreType.DMA((4,)),
            pltpu.SemaphoreType.DMA((4,)),
            pltpu.SemaphoreType.DMA,
            pltpu.SemaphoreType.DMA,
            pltpu.SemaphoreType.DMA,
            pltpu.SemaphoreType.DMA,
        ],
        compiler_params=pltpu.CompilerParams(
            collective_id=0, has_side_effects=True, vmem_limit_bytes=52 * 2**20
        ),
    )(
        kept(source), kept(voxel_phase), kept(lin_potential), kept(jnp.asarray(gram_map())),
        kept(link_voxel[0, 0]), kept(places), kept(link_count[0, 0]), kept(link_target[0, 0].reshape(groups, 128)),
    )


def solution(mesh):
    spec = P("gx", "gy", None)
    return jax.shard_map(
        functools.partial(shards, (mesh.shape["gx"], mesh.shape["gy"])),
        mesh=mesh,
        in_specs=(spec,) * 6,
        out_specs=(spec, spec),
        check_vma=False,
    )
```

```python
import functools

import jax
import jax.numpy as jnp
import numpy as np
from jax import lax
from jax.experimental import pallas as pl
from jax.experimental.pallas import tpu as pltpu
from jax.sharding import PartitionSpec as P

ITERS = 12
PART_DEV = 512
ROWS = 16
RHS = 15
PAD = 8
LOW = 64
F32 = jnp.float32


def gram_map():
    s = ITERS
    n = 2 * s

    def unit(at):
        out = np.zeros(n)
        out[at] = 1.0
        return out

    m = []
    for k in range(s):
        m.append(2 * unit(2 * k) - unit(0))
        m.append(2 * unit(2 * k + 1) - unit(1))

    def entry(j, k):
        a, b = j + k, abs(j - k)
        return 0.5 * (
            m[a] - 0.5 * (m[a + 1] + m[abs(a - 1)]) + m[b] - 0.5 * (m[b + 1] + m[abs(b - 1)])
        )

    table = np.zeros((n, ROWS, 128))
    for j in range(s):
        table[:, j, RHS] = m[j]
        for k in range(s):
            table[:, j, k] = entry(j, k)
    return table.astype(np.float32)


def two_sum(a, b):
    s = a + b
    t = s - a
    return s, (a - (s - t)) + (b - t)


def quick_two_sum(a, b):
    s = a + b
    return s, b - (s - a)


def split(a):
    c = 4097.0 * a
    hi = c - (c - a)
    return hi, a - hi


def two_prod(a, b):
    p = a * b
    ah, al = split(a)
    bh, bl = split(b)
    return p, ((ah * bh - p) + ah * bl + al * bh) + al * bl


def dd_add(a, b):
    s, e = two_sum(a[0], b[0])
    return quick_two_sum(s, e + (a[1] + b[1]))


def dd_mul(a, b):
    p, e = two_prod(a[0], b[0])
    return quick_two_sum(p, e + (a[0] * b[1] + a[1] * b[0]))


def dd_inverse(a):
    x = 1.0 / a[0]
    p, e = two_prod(a[0], x)
    r = (1.0 - p) - e - a[1] * x
    return quick_two_sum(x, x * r)


def dd_solve(matrix):
    count = ITERS
    rows = lax.broadcasted_iota(jnp.int32, (ROWS, 128), 0)
    lanes = lax.broadcasted_iota(jnp.int32, (ROWS, 128), 1)
    shape = (ROWS, 128)
    for j in range(count):
        column = tuple(jnp.broadcast_to(m[:, j : j + 1], shape) for m in matrix)
        pivot = tuple(c[j : j + 1, :] for c in column)
        row = tuple(m[j : j + 1, :] for m in matrix)
        row = dd_mul(row, dd_inverse(pivot))
        row = tuple(jnp.broadcast_to(r, shape) for r in row)
        step = dd_mul(column, row)
        less = dd_add(matrix, (-step[0], -step[1]))
        matrix = tuple(jnp.where(rows == j, r, m) for r, m in zip(row, less))
    answer = matrix[0][:, RHS : RHS + 1]
    return [jnp.broadcast_to(answer[j : j + 1, :], (8, 128)) for j in range(count)]


def kernel(
    sizes, source_hbm, phase_hbm, potential_hbm, map_hbm, voxel_hbm, places_hbm, count, target_hbm,
    out, particle,
    source, phase, potential, table, voxel, places, target, vecs, diag, inv, base, slope, ybuf, hin,
    pinv, hinv, hodd, mask, dots, mine, parts, pick, flat, sent, got,
    isem, xsend, xrecv, ysend, yrecv, csend, crecv, vsend, vrecv, hrecv, rsend, rrecv, lsend, lrecv,
):
    n_gx, n_gy = sizes
    total = n_gx * n_gy
    cx, cy, cz = source_hbm.shape
    tiles = cz // 128
    pitch = cy + PAD
    block = (cx + 4) * pitch
    s = ITERS
    cycles = s // 2
    gx, gy = lax.axis_index("gx"), lax.axis_index("gy")
    me = gx * n_gy + gy
    mesh_id = pl.DeviceIdType.MESH

    barrier = pltpu.get_barrier_semaphore()

    @pl.loop(1, total)
    def _(step):
        t = lax.rem(me + step, total)
        pl.semaphore_signal(
            barrier, inc=1, device_id=(t // n_gy, lax.rem(t, n_gy)), device_id_type=mesh_id
        )

    loads = []
    for c in range(tiles):
        for i, (src, dst) in enumerate(
            ((potential_hbm, potential), (phase_hbm, phase), (source_hbm, source))
        ):
            loads.append(
                pltpu.make_async_copy(
                    src.at[:, :, pl.ds(128 * c, 128)], dst.at[c], isem.at[c, i]
                )
            )
    extra = [
        pltpu.make_async_copy(voxel_hbm, voxel, isem.at[tiles, 0]),
        pltpu.make_async_copy(target_hbm, target, isem.at[tiles, 1]),
        pltpu.make_async_copy(map_hbm, table, isem.at[tiles, 2]),
        pltpu.make_async_copy(places_hbm, places, isem.at[tiles + 1, 0]),
    ]
    for copy in loads + extra:
        copy.start()

    has_up, has_down = gx < n_gx - 1, gx > 0
    has_right, has_left = gy < n_gy - 1, gy > 0
    up_gx, down_gx = jnp.minimum(gx + 1, n_gx - 1), jnp.maximum(gx - 1, 0)
    right_gy, left_gy = jnp.minimum(gy + 1, n_gy - 1), jnp.maximum(gy - 1, 0)

    def row(x, c, y):
        return c * block + (x + 2) * pitch + PAD + y

    def inv_row(x, c, y):
        return (c * (cx + 2) + x + 1) * cy + y

    def flat_row(x, c, y):
        return (c * cx + x) * cy + y

    near, low_corner, high_corner = cx, 2 * cx + 1, 2 * cx
    zeros8 = jnp.zeros((8, 128), F32)
    zero_row = jnp.zeros((1, 128), F32)

    @pl.loop(-1, cx + 1)
    def _(x):
        for c in range(tiles):
            for y in range(0, cy, 8):
                vecs[0, pl.ds(row(x, c, y), 8), :] = zeros8

    @pl.loop(0, cycles)
    def _(j):
        @pl.loop(0, cx + 1)
        def _(x):
            for c in range(tiles):
                vecs[2 * j + 1, pl.ds(row(x, c, -PAD), 8), :] = zeros8

    hodd[...] = jnp.zeros(hodd.shape, F32)
    for beyond, x in ((gx == 0, -1), (gx == n_gx - 1, cx)):
        @pl.when(beyond)
        def _():
            for c in range(tiles):
                for y in range(0, cy, 8):
                    inv[pl.ds(inv_row(x, c, y), 8), :] = zeros8

            @pl.loop(0, cycles)
            def _(j):
                for c in range(tiles):
                    first = row(-2 if x < 0 else cx, c, 0)
                    for y in range(0, pitch + cy, 8):
                        vecs[2 * j + 1, pl.ds(first + y, 8), :] = zeros8
                    for side in range(2):
                        hin[j, c, side, pl.ds(low_corner if x < 0 else high_corner, 1), :] = zero_row

    for beyond, side in ((gy == 0, 0), (gy == n_gy - 1, 1)):
        @pl.when(beyond)
        def _():
            hinv[side] = jnp.zeros(hinv.shape[1:], F32)

            @pl.loop(0, cycles)
            def _(j):
                for c in range(tiles):
                    hin[j, c, side] = jnp.zeros(hin.shape[3:], F32)

    sides = ((0, 0, 1), (1, cy - 1, cy - 2))

    def pack_rows(j, c):
        k = 2 * j + 1
        for side, y1, y2 in sides:
            for x in range(0, cx, 8):
                ybuf[j, c, side, pl.ds(near + x, 8), :] = (
                    vecs[k, pl.ds(row(x, c, y1), 8, stride=pitch), :]
                )
                ybuf[j, c, side, pl.ds(x, 8), :] = vecs[k, pl.ds(row(x, c, y2), 8, stride=pitch), :]

    def xcopy(j, c, way, layer):
        up = way == 0
        return pltpu.make_async_remote_copy(
            src_ref=vecs.at[2 * j + 1, pl.ds(row(cx - 1 - layer if up else layer, c, 0), cy), :],
            dst_ref=vecs.at[2 * j + 1, pl.ds(row(-1 - layer if up else cx + layer, c, 0), cy), :],
            send_sem=xsend.at[way], recv_sem=xrecv.at[lax.rem(j, 2), c, way, layer],
            device_id=(up_gx if up else down_gx, gy), device_id_type=mesh_id,
        )

    def ycopy(j, c, way):
        right = way == 0
        return pltpu.make_async_remote_copy(
            src_ref=ybuf.at[j, c, 1 if right else 0],
            dst_ref=hin.at[j, c, 0 if right else 1, pl.ds(0, 2 * cx), :],
            send_sem=ysend.at[way], recv_sem=yrecv.at[lax.rem(j, 2), c, way],
            device_id=(gx, right_gy if right else left_gy), device_id_type=mesh_id,
        )

    def ccopy(j, c, xway, yway):
        up, right = xway == 0, yway == 0
        q = 2 * xway + yway
        return pltpu.make_async_remote_copy(
            src_ref=vecs.at[
                2 * j + 1, pl.ds(row(cx - 1 if up else 0, c, cy - 1 if right else 0), 1), :
            ],
            dst_ref=hin.at[j, c, 0 if right else 1, pl.ds(low_corner if up else high_corner, 1), :],
            send_sem=csend.at[q], recv_sem=crecv.at[lax.rem(j, 2), c, q],
            device_id=(up_gx if up else down_gx, right_gy if right else left_gy),
            device_id_type=mesh_id,
        )

    def vcopy(c, way):
        up = way == 0
        return pltpu.make_async_remote_copy(
            src_ref=inv.at[pl.ds(inv_row(cx - 1 if up else 0, c, 0), cy), :],
            dst_ref=inv.at[pl.ds(inv_row(-1 if up else cx, c, 0), cy), :],
            send_sem=vsend.at[way], recv_sem=vrecv.at[c, way],
            device_id=(up_gx if up else down_gx, gy), device_id_type=mesh_id,
        )

    def hcopy(way):
        right = way == 0
        return pltpu.make_async_remote_copy(
            src_ref=pinv.at[1 if right else 0], dst_ref=hinv.at[0 if right else 1],
            send_sem=vsend.at[2 + way], recv_sem=hrecv.at[way],
            device_id=(gx, right_gy if right else left_gy), device_id_type=mesh_id,
        )

    for c in range(tiles):
        for copy in loads[3 * c : 3 * c + 3]:
            copy.wait()

        @pl.loop(0, cx)
        def _(x):
            found = []
            for y in range(0, cy, 8):
                at = potential[c, x, y : y + 8, :]
                rising = jnp.exp(0.4 * at)
                falling = jnp.exp(-0.6 * at)
                label = phase[c, x, y : y + 8, :]
                rate = jnp.where(label == 1, 0.3, jnp.where(label == 2, 0.08, 0.02)).astype(F32)
                bend = 0.4 * rising + 0.6 * falling
                d = 6.0 + rate * bend
                i = 1.0 / d
                found.append((y, rising - falling, bend, d, i, source[c, x, y : y + 8, :] * i))
            for y, level, bend, d, i, v in found:
                f = pl.ds(flat_row(x, c, y), 8)
                base[f, :] = level
                slope[f, :] = bend
                diag[f, :] = d
                inv[pl.ds(inv_row(x, c, y), 8), :] = i
                vecs[1, pl.ds(row(x, c, y), 8), :] = v

        pack_rows(0, c)
        for side, y, _ in sides:
            for x in range(0, cx, 8):
                pinv[side, c, pl.ds(x, 8), :] = inv[pl.ds(inv_row(x, c, y), 8, stride=cy), :]

    def launch_x(j, c, more):
        for way, there in ((0, has_up), (1, has_down)):
            @pl.when(there & more)
            def _():
                pl.when(has_right)(ccopy(j, c, way, 0).start)
                pl.when(has_left)(ccopy(j, c, way, 1).start)
                xcopy(j, c, way, 0).start()
                xcopy(j, c, way, 1).start()

    def launch_y(j, c, more):
        pl.when(has_right & more)(ycopy(j, c, 0).start)
        pl.when(has_left & more)(ycopy(j, c, 1).start)

    def landed_near(j, c):
        pl.when(has_left)(ycopy(j, c, 0).wait_recv)
        pl.when(has_right)(ycopy(j, c, 1).wait_recv)
        pl.when(has_down)(xcopy(j, c, 0, 0).wait_recv)
        pl.when(has_up)(xcopy(j, c, 1, 0).wait_recv)

    def landed_far(j, c):
        for way, there in ((0, has_down), (1, has_up)):
            @pl.when(there)
            def _():
                pl.when(has_left)(ccopy(j, c, way, 0).wait_recv)
                pl.when(has_right)(ccopy(j, c, way, 1).wait_recv)
                xcopy(j, c, way, 1).wait_recv()
                pl.when(j == 0)(vcopy(c, way).wait_recv)

    def drained(rows, sem):
        ref = vecs.at[0, pl.ds(0, rows), :]
        pltpu.make_async_copy(ref, ref, sem).wait()

    with jax.named_scope("barrier"):
        pl.semaphore_wait(barrier, total - 1)

    always = gx >= 0
    pl.when(has_right)(hcopy(0).start)
    pl.when(has_left)(hcopy(1).start)
    for c in range(tiles):
        launch_x(0, c, always)
        launch_y(0, c, always)
        pl.when(has_up)(vcopy(c, 0).start)
        pl.when(has_down)(vcopy(c, 1).start)

    groups = target.shape[0]
    wide = groups // n_gy
    for copy in extra:
        copy.wait()

    @pl.loop(0, n_gy)
    def _(peer):
        live = count[peer]
        lanes = lax.broadcasted_iota(jnp.int32, (128, 128), 1)
        rows = lax.broadcasted_iota(jnp.int32, (128, 128), 0)
        for part in range(wide):
            at = (places[pl.ds(peer * wide + part, 1), :] & 127).astype(F32)
            at = jnp.broadcast_to(at, (128, 128)).T
            mask[peer * wide + part] = jnp.where(
                (lanes.astype(F32) == at) & (rows + 128 * part < live), 0.5, 0.0
            )

    lane8 = lax.broadcasted_iota(jnp.int32, (8, 128), 1)
    sub8 = lax.broadcasted_iota(jnp.int32, (8, 128), 0)
    first_lane, last_lane = lane8 == 0, lane8 == 127

    def beside(v, before, after):
        z = pltpu.roll(jnp.where(last_lane, before, v), 1, 1)
        return z + pltpu.roll(jnp.where(first_lane, after, v), 127, 1)

    def sweep(k, c, start, offsets, scale, carry=None):
        centers = {}

        def center(o, y):
            if (o, y) not in centers:
                centers[o, y] = vecs[k, pl.ds(row(start + o, c, y), 8), :]
            return centers[o, y]

        found = []
        for y in range(0, cy, 8):
            for o in offsets:
                r = row(start + o, c, y)
                v = center(o, y)
                before = vecs[k, pl.ds(r - block, 8), :] if c > 0 else 0.0
                after = vecs[k, pl.ds(r + block, 8), :] if c < tiles - 1 else 0.0
                n = vecs[k, pl.ds(r - 1, 8), :] + vecs[k, pl.ds(r + 1, 8), :]
                n = (n + beside(v, before, after)) + (center(o - 1, y) + center(o + 1, y))
                i = inv[pl.ds(inv_row(start + o, c, y), 8), :]
                new = (scale * i) * n - vecs[k - 1, pl.ds(r, 8), :]
                if carry is not None:
                    w = diag[pl.ds(flat_row(start + o, c, y), 8), :] * v
                    carry = (carry[0] + w * v, carry[1] + w * new)
                found.append((r, new))
        for r, new in found:
            vecs[k + 1, pl.ds(r, 8), :] = new
        return carry

    def inner(k, c, first, last, scale, carry):
        group = max(g for g in range(1, 8) if (last - first) % g == 0)

        def some(i, a):
            return sweep(k, c, group * i + first, range(group), scale, a)

        return lax.fori_loop(0, (last - first) // group, some, carry)

    def border(j, c, scale, carry):
        k = 2 * j + 1
        carry = sweep(k, c, 0, (0,), scale, carry)
        carry = sweep(k, c, cx - 1, (0,), scale, carry)
        own, cross = carry
        found = []
        for side, y, _ in sides:
            for x in range(0, cx, 8):
                at = pl.ds(near + x, 8)
                h = hin[j, c, side, at, :]
                line = pl.ds(row(x, c, y), 8, stride=pitch)
                fixed = vecs[k + 1, line, :] + (scale * pinv[side, c, pl.ds(x, 8), :]) * h
                cross = cross + (scale * ybuf[j, c, side, at, :]) * h
                found.append((line, fixed))
        for line, fixed in found:
            vecs[k + 1, line, :] = fixed
        return own, cross

    def shell(j, c, scale):
        k = 2 * j + 1
        for side, y in ((0, -1), (1, cy)):
            for x, at in ((-1, low_corner), (cx, high_corner)):
                vecs[k, pl.ds(row(x, c, y), 1), :] = hin[j, c, side, pl.ds(at, 1), :]
        sweep(k, c, -1, (0,), scale)
        sweep(k, c, cx, (0,), scale)
        found = []
        for side, beyond in ((0, -1), (1, cy)):
            for x in range(0, cx, 8):
                at = pl.ds(near + x, 8)
                h = hin[j, c, side, at, :]
                before = hin[j, c - 1, side, at, :] if c > 0 else 0.0
                after = hin[j, c + 1, side, at, :] if c < tiles - 1 else 0.0
                lower = hin[j, c, side, pl.ds(near + x - 1, 8), :]
                if x == 0:
                    corner = hin[j, c, side, pl.ds(low_corner, 1), :]
                    lower = jnp.where(sub8 == 0, corner, lower)
                upper = hin[j, c, side, pl.ds(near + x + 1, 8), :]
                n = (lower + upper) + (hin[j, c, side, pl.ds(x, 8), :] + ybuf[j, c, side, at, :])
                n = n + beside(h, before, after)
                old = pl.ds(x, 8)
                new = (scale * hinv[side, c, old, :]) * n - hodd[side, c, old, :]
                found.append((side, old, new, pl.ds(row(x, c, beyond), 8, stride=pitch)))
        for side, old, new, outer in found:
            hodd[side, c, old, :] = new
            vecs[k + 1, outer, :] = new

    def finish(j, c, carry):
        k = 2 * j + 2
        more = j < cycles - 1
        carry = sweep(k, c, 0, (0, 1), 2.0, carry)
        carry = sweep(k, c, cx - 2, (0, 1), 2.0, carry)
        launch_x(j + 1, c, more)
        carry = inner(k, c, 2, cx - 2, 2.0, carry)

        @pl.when(more)
        def _():
            pack_rows(j + 1, c)
            launch_y(j + 1, c, always)

        return carry

    @pl.loop(0, cycles)
    def _(j):
        with jax.named_scope("cycle"):
            scale = jnp.where(j == 0, 1.0, 2.0).astype(F32)
            first = second = (zeros8, zeros8)
            with jax.named_scope("ainner"):
                for c in range(tiles):
                    first = inner(2 * j + 1, c, 1, cx - 1, scale, first)

            @pl.when(j == 0)
            def _():
                pl.when(has_left)(hcopy(0).wait_recv)
                pl.when(has_right)(hcopy(1).wait_recv)

            for c in range(tiles):
                for d in (0, 1) if c == 0 else (c + 1,):
                    if d < tiles:
                        with jax.named_scope("landed"):
                            landed_near(j, d)
                        first = border(j, d, scale, first)
                with jax.named_scope("landed"):
                    landed_far(j, c)
                shell(j, c, scale)
                second = finish(j, c, second)
            for i, value in enumerate((*first, *second)):
                dots[pl.ds(pl.multiple_of(32 * j + 8 * i, 8), 8), :] = value

    with jax.named_scope("reduce"):
        sums = []
        for g in range(2 * s // 8):
            level = [dots[pl.ds(64 * g + i, 8, stride=8), :] for i in range(8)]
            level = [two_sum(level[2 * i], level[2 * i + 1]) for i in range(4)]
            while len(level) > 1:
                level = [dd_add(level[2 * i], level[2 * i + 1]) for i in range(len(level) // 2)]
            sums.append(level[0])
        for shift in (64, 32, 16, 8, 4, 2, 1):
            sums = [
                dd_add(a, tuple(pltpu.roll(p, shift, 1) for p in a)) for a in sums
            ]
        spread = zeros8
        for g, (hi, lo) in enumerate(sums):
            spread = jnp.where(lane8 == sub8 + 8 * g, hi, spread)
            spread = jnp.where(lane8 == sub8 + 8 * g + LOW, lo, spread)
        line = jnp.sum(spread, axis=0, keepdims=True)
        mine[...] = line
        parts[pl.ds(me, 1), :] = line

        def move(owner, there):
            return pltpu.make_async_remote_copy(
                src_ref=mine, dst_ref=parts.at[pl.ds(owner, 1), :],
                send_sem=rsend, recv_sem=rrecv,
                device_id=(there // n_gy, lax.rem(there, n_gy)), device_id_type=mesh_id,
            )

        @pl.loop(1, total)
        def _(step):
            move(me, lax.rem(me + step, total)).start()

        for way, there in ((0, has_up), (1, has_down)):
            @pl.when(there)
            def _():
                drained(cycles * tiles * 2 * cy, xsend.at[way])
                drained(tiles * cy, vsend.at[way])
                for q, also in ((0, has_right), (1, has_left)):
                    @pl.when(also)
                    def _():
                        drained(cycles * tiles, csend.at[2 * way + q])

        for way, there in ((0, has_right), (1, has_left)):
            @pl.when(there)
            def _():
                drained(cycles * tiles * 2 * cx, ysend.at[way])
                drained(tiles * cx, vsend.at[2 + way])

        drained(total - 1, rrecv)

    with jax.named_scope("solve"):
        level = [parts[8 * i : 8 * i + 8, :] for i in range(total // 8)]
        level = [(a, pltpu.roll(a, 128 - LOW, 1)) for a in level]
        while len(level) > 1:
            level = [dd_add(level[2 * i], level[2 * i + 1]) for i in range(len(level) // 2)]
        every = level[0]
        for shift in (4, 2, 1):
            every = dd_add(every, tuple(pltpu.roll(p, shift, 0) for p in every))
        terms = []
        for m in range(2 * s):
            hi, lo = (jnp.broadcast_to(p[0:1, m : m + 1], (ROWS, 128)) for p in every)
            terms.append((table[m] * hi, table[m] * lo))
        while len(terms) > 1:
            terms = [
                dd_add(terms[i], terms[i + 1]) if i + 1 < len(terms) else terms[i]
                for i in range(0, len(terms), 2)
            ]
        weights = dd_solve(terms[0])

    with jax.named_scope("combine"):
        @pl.loop(0, cx)
        def _(x):
            for c in range(tiles):
                for y in range(0, cy, 8):
                    pieces = [
                        w * vecs[1 + k, pl.ds(row(x, c, y), 8), :] for k, w in enumerate(weights)
                    ]
                    while len(pieces) > 1:
                        pieces = [sum(pieces[i : i + 2]) for i in range(0, len(pieces), 2)]
                    out[x, y : y + 8, 128 * c : 128 * (c + 1)] = pieces[0]
                    f = pl.ds(flat_row(x, c, y), 8)
                    at = (x * cy + y) * tiles + c
                    flat[pl.ds(at, 8, stride=tiles), :] = base[f, :] + slope[f, :] * pieces[0]

    with jax.named_scope("gather"):
        @pl.loop(0, n_gy)
        def _(peer):
            for part in range(wide):
                group = peer * wide + part

                @pl.loop(0, 128, step=64)
                def _(start):
                    for i in range(64):
                        v = voxel[group * 128 + start + i]
                        pick[pl.ds(start + i, 1), :] = flat[pl.ds(v >> 7, 1), :]

                found = pick[...] * mask[group]
                sent[peer, part : part + 1, :] = jnp.sum(found.T, axis=0, keepdims=True)

    def link(owner, peer):
        return pltpu.make_async_remote_copy(
            src_ref=sent.at[peer], dst_ref=got.at[owner], send_sem=lsend,
            recv_sem=lrecv, device_id=(gx, peer), device_id_type=mesh_id,
        )

    with jax.named_scope("links"):
        @pl.loop(1, n_gy)
        def _(step):
            link(gy, lax.rem(gy + step, n_gy)).start()

        got[gy] = sent[gy]
        drained(total - 1, rsend)
        drained((n_gy - 1) * wide, lsend)
        drained((n_gy - 1) * wide, lrecv)

    with jax.named_scope("scatter"):
        own = particle.shape[2]
        sub = lax.broadcasted_iota(jnp.int32, (128, 128), 0)
        for start in range(0, own, 128):
            def add(peer, acc):
                for part in range(wide):
                    spot = target[pl.ds(peer * wide + part, 1), :]
                    acc = acc + jnp.where(spot - start == sub, got[peer, part : part + 1, :], 0.0)
                return acc

            acc = lax.fori_loop(0, n_gy, add, jnp.zeros((128, 128), F32))
            particle[0, :, start : start + 128] = jnp.sum(acc.T, axis=0, keepdims=True)


def kept(x):
    return pltpu.with_memory_space_constraint(x, pltpu.HBM)


def shards(sizes, source, voxel_phase, lin_potential, link_voxel, link_count, link_target):
    cx, cy, cz = source.shape
    total = sizes[0] * sizes[1]
    s = ITERS
    tiles = cz // 128
    voxels = cx * cy * tiles
    padded = (cx + 4) * tiles * (cy + PAD) + 8
    cycles = s // 2
    places = link_voxel[0, 0].reshape(-1, 128)
    peers = link_count.shape[2]
    slots = link_voxel.shape[2]
    groups = slots // 128
    whole = pl.BlockSpec(memory_space=pltpu.VMEM)
    far = pl.BlockSpec(memory_space=pltpu.HBM)
    scalars = pl.BlockSpec(memory_space=pltpu.SMEM)
    return pl.pallas_call(
        functools.partial(kernel, sizes),
        out_shape=(
            jax.ShapeDtypeStruct(source.shape, F32),
            jax.ShapeDtypeStruct((1, 1, PART_DEV), F32),
        ),
        in_specs=[far] * 6 + [scalars, far],
        out_specs=(whole, whole),
        scratch_shapes=[
            pltpu.VMEM((tiles, cx, cy, 128), F32),
            pltpu.VMEM((tiles, cx, cy, 128), jnp.int32),
            pltpu.VMEM((tiles, cx, cy, 128), F32),
            pltpu.VMEM((2 * s, ROWS, 128), F32),
            pltpu.SMEM((slots,), jnp.int32),
            pltpu.VMEM((groups, 128), jnp.int32),
            pltpu.VMEM((groups, 128), jnp.int32),
            pltpu.VMEM((s + 2, padded, 128), F32),
            pltpu.VMEM((voxels, 128), F32),
            pltpu.VMEM((tiles * (cx + 2) * cy, 128), F32),
            pltpu.VMEM((voxels, 128), F32),
            pltpu.VMEM((voxels, 128), F32),
            pltpu.VMEM((cycles, tiles, 2, 2 * cx, 128), F32),
            pltpu.VMEM((cycles, tiles, 2, 2 * cx + 8, 128), F32),
            pltpu.VMEM((2, tiles, cx, 128), F32),
            pltpu.VMEM((2, tiles, cx, 128), F32),
            pltpu.VMEM((2, tiles, cx, 128), F32),
            pltpu.VMEM((groups, 128, 128), F32),
            pltpu.VMEM((2 * s * 8, 128), F32),
            pltpu.VMEM((1, 128), F32),
            pltpu.VMEM((total, 128), F32),
            pltpu.VMEM((128, 128), F32),
            pltpu.VMEM((voxels, 128), F32),
            pltpu.VMEM((peers, groups // peers, 128), F32),
            pltpu.VMEM((peers, groups // peers, 128), F32),
            pltpu.SemaphoreType.DMA((tiles + 2, 3)),
            pltpu.SemaphoreType.DMA((2,)),
            pltpu.SemaphoreType.DMA((2, tiles, 2, 2)),
            pltpu.SemaphoreType.DMA((2,)),
            pltpu.SemaphoreType.DMA((2, tiles, 2)),
            pltpu.SemaphoreType.DMA((4,)),
            pltpu.SemaphoreType.DMA((2, tiles, 4)),
            pltpu.SemaphoreType.DMA((4,)),
            pltpu.SemaphoreType.DMA((tiles, 2)),
            pltpu.SemaphoreType.DMA((2,)),
            pltpu.SemaphoreType.DMA,
            pltpu.SemaphoreType.DMA,
            pltpu.SemaphoreType.DMA,
            pltpu.SemaphoreType.DMA,
        ],
        compiler_params=pltpu.CompilerParams(
            collective_id=0, has_side_effects=True, vmem_limit_bytes=52 * 2**20
        ),
    )(
        kept(source), kept(voxel_phase), kept(lin_potential), kept(jnp.asarray(gram_map())),
        kept(link_voxel[0, 0]), kept(places), kept(link_count[0, 0]), kept(link_target[0, 0].reshape(groups, 128)),
    )


def solution(mesh):
    spec = P("gx", "gy", None)
    return jax.shard_map(
        functools.partial(shards, (mesh.shape["gx"], mesh.shape["gy"])),
        mesh=mesh,
        in_specs=(spec,) * 6,
        out_specs=(spec, spec),
        check_vma=False,
    )
```

```python
import functools

import jax
import jax.numpy as jnp
import numpy as np
from jax import lax
from jax.experimental import pallas as pl
from jax.experimental.pallas import tpu as pltpu
from jax.sharding import PartitionSpec as P

ITERS = 12
PART_DEV = 512
ROWS = 16
RHS = 15
PAD = 8
LOW = 64
F32 = jnp.float32


def gram_map():
    s = ITERS
    n = 2 * s

    def unit(at):
        out = np.zeros(n)
        out[at] = 1.0
        return out

    m = []
    for k in range(s):
        m.append(2 * unit(2 * k) - unit(0))
        m.append(2 * unit(2 * k + 1) - unit(1))

    def entry(j, k):
        a, b = j + k, abs(j - k)
        return 0.5 * (
            m[a] - 0.5 * (m[a + 1] + m[abs(a - 1)]) + m[b] - 0.5 * (m[b + 1] + m[abs(b - 1)])
        )

    table = np.zeros((n, ROWS, 128))
    for j in range(s):
        table[:, j, RHS] = m[j]
        for k in range(s):
            table[:, j, k] = entry(j, k)
    return table.astype(np.float32)


def two_sum(a, b):
    s = a + b
    t = s - a
    return s, (a - (s - t)) + (b - t)


def quick_two_sum(a, b):
    s = a + b
    return s, b - (s - a)


def split(a):
    c = 4097.0 * a
    hi = c - (c - a)
    return hi, a - hi


def two_prod(a, b):
    p = a * b
    ah, al = split(a)
    bh, bl = split(b)
    return p, ((ah * bh - p) + ah * bl + al * bh) + al * bl


def dd_add(a, b):
    s, e = two_sum(a[0], b[0])
    return quick_two_sum(s, e + (a[1] + b[1]))


def dd_mul(a, b):
    p, e = two_prod(a[0], b[0])
    return quick_two_sum(p, e + (a[0] * b[1] + a[1] * b[0]))


def dd_inverse(a):
    x = 1.0 / a[0]
    p, e = two_prod(a[0], x)
    r = (1.0 - p) - e - a[1] * x
    return quick_two_sum(x, x * r)


def dd_solve(matrix):
    count = ITERS
    rows = lax.broadcasted_iota(jnp.int32, (ROWS, 128), 0)
    lanes = lax.broadcasted_iota(jnp.int32, (ROWS, 128), 1)
    shape = (ROWS, 128)
    for j in range(count):
        column = tuple(jnp.broadcast_to(m[:, j : j + 1], shape) for m in matrix)
        pivot = tuple(c[j : j + 1, :] for c in column)
        row = tuple(m[j : j + 1, :] for m in matrix)
        row = dd_mul(row, dd_inverse(pivot))
        row = tuple(jnp.broadcast_to(r, shape) for r in row)
        step = dd_mul(column, row)
        less = dd_add(matrix, (-step[0], -step[1]))
        matrix = tuple(jnp.where(rows == j, r, m) for r, m in zip(row, less))
    answer = matrix[0][:, RHS : RHS + 1]
    return [jnp.broadcast_to(answer[j : j + 1, :], (8, 128)) for j in range(count)]


def flipped(index, mask, size):
    if size & (size - 1):
        return lax.rem(index + mask, size)
    out, bit = 0, 1
    while bit < size:
        out = out + lax.rem(index // bit + mask // bit, 2) * bit
        bit *= 2
    return out


def add_up(shape, peers, wide, target, got, start):
    sub = lax.broadcasted_iota(jnp.int32, shape, 0) + start
    step = max(g for g in (1, 2, 4) if peers % g == 0)

    def some(i, acc):
        for extra in range(step):
            for part in range(wide):
                spot = target[pl.ds((i * step + extra) * wide + part, 1), :]
                value = got[pl.ds((i * step + extra) * wide + part, 1), :]
                acc = acc + jnp.where(spot == sub, value, 0.0)
        return acc

    acc = lax.fori_loop(0, peers // step, some, jnp.zeros(shape, F32))
    return jnp.sum(acc.T, axis=0, keepdims=True)


def last_kernel(peers, found, got_in, target_in, out, particle, got, target, sums, sems):
    whole = pltpu.make_async_copy(found, out, sems.at[0])
    pieces = [
        pltpu.make_async_copy(got_in, got, sems.at[1]),
        pltpu.make_async_copy(target_in, target, sems.at[2]),
    ]
    for copy in pieces:
        copy.start()
    whole.start()
    for copy in pieces:
        copy.wait()
    for start in range(0, sums.shape[2], 128):
        sums[0, :, start : start + 128] = add_up(
            (128, 128), peers, got.shape[0] // peers, target, got, start
        )
    back = pltpu.make_async_copy(sums, particle, sems.at[1])
    back.start()
    back.wait()
    whole.wait()


def kernel(
    sizes, source_hbm, phase_hbm, potential_hbm, map_hbm, places_hbm, count,
    out, got,
    source, phase, potential, table, lines, voxel, places, vecs, diag, inv, base, slope, ybuf, hin,
    pinv, hinv, hodd, mask, dots, mine, parts, pick0, pick1, flat, sent,
    isem, xsend, xrecv, ysend, yrecv, csend, crecv, vsend, vrecv, hrecv, rsend, rrecv, lsend, lrecv,
):
    n_gx, n_gy = sizes
    total = n_gx * n_gy
    cx, cy, cz = source_hbm.shape
    tiles = cz // 128
    pitch = cy + PAD
    block = (cx + 4) * pitch
    s = ITERS
    cycles = s // 2
    gx, gy = lax.axis_index("gx"), lax.axis_index("gy")
    me = gx * n_gy + gy
    mesh_id = pl.DeviceIdType.MESH

    barrier = pltpu.get_barrier_semaphore()

    def everyone(act):
        @pl.loop(0, n_gy)
        def _(step):
            to_gy = flipped(gy, n_gy - 1 - step, n_gy)

            @pl.loop(1, n_gx)
            def _(shift):
                act(lax.rem(gx + shift, n_gx), to_gy)

        @pl.loop(0, n_gy - 1)
        def _(step):
            act(gx, flipped(gy, n_gy - 1 - step, n_gy))

    everyone(
        lambda to_gx, to_gy: pl.semaphore_signal(
            barrier, inc=1, device_id=(to_gx, to_gy), device_id_type=mesh_id
        )
    )

    loads = []
    for c in range(tiles):
        for i, (src, dst) in enumerate(
            ((potential_hbm, potential), (phase_hbm, phase), (source_hbm, source))
        ):
            loads.append(
                pltpu.make_async_copy(
                    src.at[:, :, pl.ds(128 * c, 128)], dst.at[c], isem.at[c, i]
                )
            )
    extra = [
        pltpu.make_async_copy(map_hbm, table, isem.at[tiles, 0]),
        pltpu.make_async_copy(places_hbm, places, isem.at[tiles, 1]),
    ]
    for copy in loads + extra:
        copy.start()

    has_up, has_down = gx < n_gx - 1, gx > 0
    has_right, has_left = gy < n_gy - 1, gy > 0
    up_gx, down_gx = jnp.minimum(gx + 1, n_gx - 1), jnp.maximum(gx - 1, 0)
    right_gy, left_gy = jnp.minimum(gy + 1, n_gy - 1), jnp.maximum(gy - 1, 0)

    def row(x, c, y):
        return c * block + (x + 2) * pitch + PAD + y

    def inv_row(x, c, y):
        return (c * (cx + 2) + x + 1) * cy + y

    def flat_row(x, c, y):
        return (c * cx + x) * cy + y

    near, low_corner, high_corner = cx, 2 * cx + 1, 2 * cx
    zeros8 = jnp.zeros((8, 128), F32)
    zero_row = jnp.zeros((1, 128), F32)

    @pl.loop(-1, cx + 1)
    def _(x):
        for c in range(tiles):
            for y in range(0, cy, 8):
                vecs[0, pl.ds(row(x, c, y), 8), :] = zeros8

    @pl.loop(0, cycles)
    def _(j):
        @pl.loop(0, cx + 1)
        def _(x):
            for c in range(tiles):
                vecs[2 * j + 1, pl.ds(row(x, c, -PAD), 8), :] = zeros8

    hodd[...] = jnp.zeros(hodd.shape, F32)
    for beyond, x in ((gx == 0, -1), (gx == n_gx - 1, cx)):
        @pl.when(beyond)
        def _():
            for c in range(tiles):
                for y in range(0, cy, 8):
                    inv[pl.ds(inv_row(x, c, y), 8), :] = zeros8

            @pl.loop(0, cycles)
            def _(j):
                for c in range(tiles):
                    first = row(-2 if x < 0 else cx, c, 0)
                    for y in range(0, pitch + cy, 8):
                        vecs[2 * j + 1, pl.ds(first + y, 8), :] = zeros8
                    for side in range(2):
                        hin[j, c, side, pl.ds(low_corner if x < 0 else high_corner, 1), :] = zero_row

    for beyond, side in ((gy == 0, 0), (gy == n_gy - 1, 1)):
        @pl.when(beyond)
        def _():
            hinv[side] = jnp.zeros(hinv.shape[1:], F32)

            @pl.loop(0, cycles)
            def _(j):
                for c in range(tiles):
                    hin[j, c, side] = jnp.zeros(hin.shape[3:], F32)

    sides = ((0, 0, 1), (1, cy - 1, cy - 2))

    def pack_rows(j, c):
        k = 2 * j + 1
        for side, y1, y2 in sides:
            for x in range(0, cx, 8):
                ybuf[j, c, side, pl.ds(near + x, 8), :] = (
                    vecs[k, pl.ds(row(x, c, y1), 8, stride=pitch), :]
                )
                ybuf[j, c, side, pl.ds(x, 8), :] = vecs[k, pl.ds(row(x, c, y2), 8, stride=pitch), :]

    def xcopy(j, c, way, layer):
        up = way == 0
        return pltpu.make_async_remote_copy(
            src_ref=vecs.at[2 * j + 1, pl.ds(row(cx - 1 - layer if up else layer, c, 0), cy), :],
            dst_ref=vecs.at[2 * j + 1, pl.ds(row(-1 - layer if up else cx + layer, c, 0), cy), :],
            send_sem=xsend.at[way], recv_sem=xrecv.at[lax.rem(j, 2), c, way, layer],
            device_id=(up_gx if up else down_gx, gy), device_id_type=mesh_id,
        )

    def ycopy(j, c, way):
        right = way == 0
        return pltpu.make_async_remote_copy(
            src_ref=ybuf.at[j, c, 1 if right else 0],
            dst_ref=hin.at[j, c, 0 if right else 1, pl.ds(0, 2 * cx), :],
            send_sem=ysend.at[way], recv_sem=yrecv.at[lax.rem(j, 2), c, way],
            device_id=(gx, right_gy if right else left_gy), device_id_type=mesh_id,
        )

    def ccopy(j, c, xway, yway):
        up, right = xway == 0, yway == 0
        q = 2 * xway + yway
        return pltpu.make_async_remote_copy(
            src_ref=vecs.at[
                2 * j + 1, pl.ds(row(cx - 1 if up else 0, c, cy - 1 if right else 0), 1), :
            ],
            dst_ref=hin.at[j, c, 0 if right else 1, pl.ds(low_corner if up else high_corner, 1), :],
            send_sem=csend.at[q], recv_sem=crecv.at[lax.rem(j, 2), c, q],
            device_id=(up_gx if up else down_gx, right_gy if right else left_gy),
            device_id_type=mesh_id,
        )

    def vcopy(c, way):
        up = way == 0
        return pltpu.make_async_remote_copy(
            src_ref=inv.at[pl.ds(inv_row(cx - 1 if up else 0, c, 0), cy), :],
            dst_ref=inv.at[pl.ds(inv_row(-1 if up else cx, c, 0), cy), :],
            send_sem=vsend.at[way], recv_sem=vrecv.at[c, way],
            device_id=(up_gx if up else down_gx, gy), device_id_type=mesh_id,
        )

    def hcopy(way):
        right = way == 0
        return pltpu.make_async_remote_copy(
            src_ref=pinv.at[1 if right else 0], dst_ref=hinv.at[0 if right else 1],
            send_sem=vsend.at[2 + way], recv_sem=hrecv.at[way],
            device_id=(gx, right_gy if right else left_gy), device_id_type=mesh_id,
        )

    for c in range(tiles):
        for copy in loads[3 * c : 3 * c + 3]:
            copy.wait()

        @pl.loop(0, cx)
        def _(x):
            found = []
            for y in range(0, cy, 8):
                at = potential[c, x, y : y + 8, :]
                rising = jnp.exp(0.4 * at)
                falling = jnp.exp(-0.6 * at)
                label = phase[c, x, y : y + 8, :]
                rate = jnp.where(label == 1, 0.3, jnp.where(label == 2, 0.08, 0.02)).astype(F32)
                bend = 0.4 * rising + 0.6 * falling
                d = 6.0 + rate * bend
                i = 1.0 / d
                found.append((y, rising - falling, bend, d, i, source[c, x, y : y + 8, :] * i))
            for y, level, bend, d, i, v in found:
                f = pl.ds(flat_row(x, c, y), 8)
                base[f, :] = level
                slope[f, :] = bend
                diag[f, :] = d
                inv[pl.ds(inv_row(x, c, y), 8), :] = i
                vecs[1, pl.ds(row(x, c, y), 8), :] = v

        pack_rows(0, c)
        for side, y, _ in sides:
            for x in range(0, cx, 8):
                pinv[side, c, pl.ds(x, 8), :] = inv[pl.ds(inv_row(x, c, y), 8, stride=cy), :]

    def launch_x(j, c, more):
        for way, there in ((0, has_up), (1, has_down)):
            @pl.when(there & more)
            def _():
                pl.when(has_right)(ccopy(j, c, way, 0).start)
                pl.when(has_left)(ccopy(j, c, way, 1).start)
                xcopy(j, c, way, 0).start()
                xcopy(j, c, way, 1).start()

    def launch_y(j, c, more):
        pl.when(has_right & more)(ycopy(j, c, 0).start)
        pl.when(has_left & more)(ycopy(j, c, 1).start)

    def landed_near(j, c):
        pl.when(has_left)(ycopy(j, c, 0).wait_recv)
        pl.when(has_right)(ycopy(j, c, 1).wait_recv)
        pl.when(has_down)(xcopy(j, c, 0, 0).wait_recv)
        pl.when(has_up)(xcopy(j, c, 1, 0).wait_recv)

    def landed_far(j, c):
        for way, there in ((0, has_down), (1, has_up)):
            @pl.when(there)
            def _():
                pl.when(has_left)(ccopy(j, c, way, 0).wait_recv)
                pl.when(has_right)(ccopy(j, c, way, 1).wait_recv)
                xcopy(j, c, way, 1).wait_recv()
                pl.when(j == 0)(vcopy(c, way).wait_recv)

    def drained(rows, sem):
        ref = vecs.at[0, pl.ds(0, rows), :]
        pltpu.make_async_copy(ref, ref, sem).wait()

    with jax.named_scope("barrier"):
        pl.semaphore_wait(barrier, total - 1)

    always = gx >= 0
    pl.when(has_right)(hcopy(0).start)
    pl.when(has_left)(hcopy(1).start)
    for c in range(tiles):
        launch_x(0, c, always)
        launch_y(0, c, always)
        pl.when(has_up)(vcopy(c, 0).start)
        pl.when(has_down)(vcopy(c, 1).start)

    groups = places.shape[0]
    wide = groups // n_gy
    for copy in extra:
        copy.wait()
    lines[...] = places[...] >> 7
    scalar_lines = pltpu.make_async_copy(lines, voxel, isem.at[tiles, 2])
    scalar_lines.start()

    @pl.loop(0, n_gy)
    def _(peer):
        live = count[peer]
        lanes = lax.broadcasted_iota(jnp.int32, (128, 128), 1)
        rows = lax.broadcasted_iota(jnp.int32, (128, 128), 0)
        for part in range(wide):
            at = (places[pl.ds(peer * wide + part, 1), :] & 127).astype(F32)
            at = jnp.broadcast_to(at, (128, 128)).T
            mask[peer * wide + part] = jnp.where(
                (lanes.astype(F32) == at) & (rows + 128 * part < live), 0.5, 0.0
            )

    lane8 = lax.broadcasted_iota(jnp.int32, (8, 128), 1)
    sub8 = lax.broadcasted_iota(jnp.int32, (8, 128), 0)
    first_lane, last_lane = lane8 == 0, lane8 == 127

    def beside(v, before, after):
        z = pltpu.roll(jnp.where(last_lane, before, v), 1, 1)
        return z + pltpu.roll(jnp.where(first_lane, after, v), 127, 1)

    def sweep(k, c, start, offsets, scale, carry=None):
        centers = {}

        def center(o, y):
            if (o, y) not in centers:
                centers[o, y] = vecs[k, pl.ds(row(start + o, c, y), 8), :]
            return centers[o, y]

        found = []
        for y in range(0, cy, 8):
            for o in offsets:
                r = row(start + o, c, y)
                v = center(o, y)
                before = vecs[k, pl.ds(r - block, 8), :] if c > 0 else 0.0
                after = vecs[k, pl.ds(r + block, 8), :] if c < tiles - 1 else 0.0
                n = vecs[k, pl.ds(r - 1, 8), :] + vecs[k, pl.ds(r + 1, 8), :]
                n = (n + beside(v, before, after)) + (center(o - 1, y) + center(o + 1, y))
                i = inv[pl.ds(inv_row(start + o, c, y), 8), :]
                new = (scale * i) * n - vecs[k - 1, pl.ds(r, 8), :]
                if carry is not None:
                    w = diag[pl.ds(flat_row(start + o, c, y), 8), :] * v
                    carry = (carry[0] + w * v, carry[1] + w * new)
                found.append((r, new))
        for r, new in found:
            vecs[k + 1, pl.ds(r, 8), :] = new
        return carry

    def inner(k, c, first, last, scale, carry):
        group = max(g for g in range(1, 8) if (last - first) % g == 0)

        def some(i, a):
            return sweep(k, c, group * i + first, range(group), scale, a)

        return lax.fori_loop(0, (last - first) // group, some, carry)

    def border(j, c, scale, carry):
        k = 2 * j + 1
        carry = sweep(k, c, 0, (0,), scale, carry)
        carry = sweep(k, c, cx - 1, (0,), scale, carry)
        own, cross = carry
        found = []
        for side, y, _ in sides:
            for x in range(0, cx, 8):
                at = pl.ds(near + x, 8)
                h = hin[j, c, side, at, :]
                line = pl.ds(row(x, c, y), 8, stride=pitch)
                fixed = vecs[k + 1, line, :] + (scale * pinv[side, c, pl.ds(x, 8), :]) * h
                cross = cross + (scale * ybuf[j, c, side, at, :]) * h
                found.append((line, fixed))
        for line, fixed in found:
            vecs[k + 1, line, :] = fixed
        return own, cross

    def shell(j, c, scale):
        k = 2 * j + 1
        for side, y in ((0, -1), (1, cy)):
            for x, at in ((-1, low_corner), (cx, high_corner)):
                vecs[k, pl.ds(row(x, c, y), 1), :] = hin[j, c, side, pl.ds(at, 1), :]
        sweep(k, c, -1, (0,), scale)
        sweep(k, c, cx, (0,), scale)
        found = []
        for side, beyond in ((0, -1), (1, cy)):
            for x in range(0, cx, 8):
                at = pl.ds(near + x, 8)
                h = hin[j, c, side, at, :]
                before = hin[j, c - 1, side, at, :] if c > 0 else 0.0
                after = hin[j, c + 1, side, at, :] if c < tiles - 1 else 0.0
                lower = hin[j, c, side, pl.ds(near + x - 1, 8), :]
                if x == 0:
                    corner = hin[j, c, side, pl.ds(low_corner, 1), :]
                    lower = jnp.where(sub8 == 0, corner, lower)
                upper = hin[j, c, side, pl.ds(near + x + 1, 8), :]
                n = (lower + upper) + (hin[j, c, side, pl.ds(x, 8), :] + ybuf[j, c, side, at, :])
                n = n + beside(h, before, after)
                old = pl.ds(x, 8)
                new = (scale * hinv[side, c, old, :]) * n - hodd[side, c, old, :]
                found.append((side, old, new, pl.ds(row(x, c, beyond), 8, stride=pitch)))
        for side, old, new, outer in found:
            hodd[side, c, old, :] = new
            vecs[k + 1, outer, :] = new

    def finish(j, c, carry):
        k = 2 * j + 2
        more = j < cycles - 1
        carry = sweep(k, c, 0, (0, 1), 2.0, carry)
        carry = sweep(k, c, cx - 2, (0, 1), 2.0, carry)
        launch_x(j + 1, c, more)
        carry = inner(k, c, 2, cx - 2, 2.0, carry)

        @pl.when(more)
        def _():
            pack_rows(j + 1, c)
            launch_y(j + 1, c, always)

        return carry

    @pl.loop(0, cycles)
    def _(j):
        with jax.named_scope("cycle"):
            scale = jnp.where(j == 0, 1.0, 2.0).astype(F32)
            first = second = (zeros8, zeros8)
            with jax.named_scope("ainner"):
                for c in range(tiles):
                    first = inner(2 * j + 1, c, 1, cx - 1, scale, first)

            @pl.when(j == 0)
            def _():
                pl.when(has_left)(hcopy(0).wait_recv)
                pl.when(has_right)(hcopy(1).wait_recv)

            for c in range(tiles):
                for d in (0, 1) if c == 0 else (c + 1,):
                    if d < tiles:
                        with jax.named_scope("landed"):
                            landed_near(j, d)
                        first = border(j, d, scale, first)
                with jax.named_scope("landed"):
                    landed_far(j, c)
                shell(j, c, scale)
                second = finish(j, c, second)
            for i, value in enumerate((*first, *second)):
                dots[pl.ds(pl.multiple_of(32 * j + 8 * i, 8), 8), :] = value

    scalar_lines.wait()

    with jax.named_scope("reduce"):
        sums = []
        for g in range(2 * s // 8):
            level = [dots[pl.ds(64 * g + i, 8, stride=8), :] for i in range(8)]
            level = [two_sum(level[2 * i], level[2 * i + 1]) for i in range(4)]
            while len(level) > 1:
                level = [dd_add(level[2 * i], level[2 * i + 1]) for i in range(len(level) // 2)]
            sums.append(level[0])
        for shift in (64, 32, 16, 8, 4, 2, 1):
            sums = [
                dd_add(a, tuple(pltpu.roll(p, shift, 1) for p in a)) for a in sums
            ]
        spread = zeros8
        for g, (hi, lo) in enumerate(sums):
            spread = jnp.where(lane8 == sub8 + 8 * g, hi, spread)
            spread = jnp.where(lane8 == sub8 + 8 * g + LOW, lo, spread)
        line = jnp.sum(spread, axis=0, keepdims=True)
        mine[...] = line
        parts[pl.ds(me, 1), :] = line

        everyone(
            lambda to_gx, to_gy: pltpu.make_async_remote_copy(
                src_ref=mine, dst_ref=parts.at[pl.ds(me, 1), :],
                send_sem=rsend, recv_sem=rrecv,
                device_id=(to_gx, to_gy), device_id_type=mesh_id,
            ).start()
        )

        for way, there in ((0, has_up), (1, has_down)):
            @pl.when(there)
            def _():
                drained(cycles * tiles * 2 * cy, xsend.at[way])
                drained(tiles * cy, vsend.at[way])
                for q, also in ((0, has_right), (1, has_left)):
                    @pl.when(also)
                    def _():
                        drained(cycles * tiles, csend.at[2 * way + q])

        for way, there in ((0, has_right), (1, has_left)):
            @pl.when(there)
            def _():
                drained(cycles * tiles * 2 * cx, ysend.at[way])
                drained(tiles * cx, vsend.at[2 + way])

        drained(total - 1, rrecv)

    with jax.named_scope("solve"):
        level = [parts[8 * i : 8 * i + 8, :] for i in range(total // 8)]
        level = [(a, pltpu.roll(a, 128 - LOW, 1)) for a in level]
        while len(level) > 1:
            level = [dd_add(level[2 * i], level[2 * i + 1]) for i in range(len(level) // 2)]
        every = level[0]
        for shift in (4, 2, 1):
            every = dd_add(every, tuple(pltpu.roll(p, shift, 0) for p in every))
        terms = []
        for m in range(2 * s):
            hi, lo = (jnp.broadcast_to(p[0:1, m : m + 1], (ROWS, 128)) for p in every)
            terms.append((table[m] * hi, table[m] * lo))
        while len(terms) > 1:
            terms = [
                dd_add(terms[i], terms[i + 1]) if i + 1 < len(terms) else terms[i]
                for i in range(0, len(terms), 2)
            ]
        weights = dd_solve(terms[0])

    with jax.named_scope("combine"):
        @pl.loop(0, cx)
        def _(x):
            for c in range(tiles):
                for y in range(0, cy, 8):
                    pieces = [
                        w * vecs[1 + k, pl.ds(row(x, c, y), 8), :] for k, w in enumerate(weights)
                    ]
                    while len(pieces) > 1:
                        pieces = [sum(pieces[i : i + 2]) for i in range(0, len(pieces), 2)]
                    out[x, y : y + 8, 128 * c : 128 * (c + 1)] = pieces[0]
                    f = pl.ds(flat_row(x, c, y), 8)
                    at = (x * cy + y) * tiles + c
                    flat[pl.ds(at, 8, stride=tiles), :] = base[f, :] + slope[f, :] * pieces[0]

    picks = (pick0, pick1)

    def gathered(peer):
        for part in range(wide):
            group = peer * wide + part
            for i in range(128):
                picks[part % 2][pl.ds(i, 1), :] = flat[pl.ds(voxel[group, i], 1), :]
            value = picks[part % 2][...] * mask[group]
            sent[peer, pl.ds(part, 1), :] = jnp.sum(value.T, axis=0, keepdims=True)

    with jax.named_scope("gather"):
        @pl.loop(0, n_gy - 1)
        def _(step):
            peer = flipped(gy, n_gy - 1 - step, n_gy)
            gathered(peer)
            pltpu.make_async_remote_copy(
                src_ref=sent.at[peer], dst_ref=got.at[gy], send_sem=lsend, recv_sem=lrecv,
                device_id=(gx, peer), device_id_type=mesh_id,
            ).start()

        gathered(gy)
        got[gy] = sent[gy]

    with jax.named_scope("links"):
        drained(total - 1, rsend)
        drained((n_gy - 1) * wide, lsend)
        drained((n_gy - 1) * wide, lrecv)


def kept(x):
    return pltpu.with_memory_space_constraint(x, pltpu.HBM)


def shards(sizes, source, voxel_phase, lin_potential, link_voxel, link_count, link_target):
    cx, cy, cz = source.shape
    total = sizes[0] * sizes[1]
    s = ITERS
    tiles = cz // 128
    voxels = cx * cy * tiles
    padded = (cx + 4) * tiles * (cy + PAD) + 8
    cycles = s // 2
    places = link_voxel[0, 0].reshape(-1, 128)
    peers = link_count.shape[2]
    slots = link_voxel.shape[2]
    groups = slots // 128
    whole = pl.BlockSpec(memory_space=pltpu.VMEM)
    far = pl.BlockSpec(memory_space=pltpu.HBM)
    scalars = pl.BlockSpec(memory_space=pltpu.SMEM)
    found, got = pl.pallas_call(
        functools.partial(kernel, sizes),
        out_shape=(
            jax.ShapeDtypeStruct(source.shape, F32),
            jax.ShapeDtypeStruct((peers, groups // peers, 128), F32),
        ),
        in_specs=[far] * 5 + [scalars],
        out_specs=(whole, whole),
        scratch_shapes=[
            pltpu.VMEM((tiles, cx, cy, 128), F32),
            pltpu.VMEM((tiles, cx, cy, 128), jnp.int32),
            pltpu.VMEM((tiles, cx, cy, 128), F32),
            pltpu.VMEM((2 * s, ROWS, 128), F32),
            pltpu.VMEM((groups, 128), jnp.int32),
            pltpu.SMEM((groups, 128), jnp.int32),
            pltpu.VMEM((groups, 128), jnp.int32),
            pltpu.VMEM((s + 2, padded, 128), F32),
            pltpu.VMEM((voxels, 128), F32),
            pltpu.VMEM((tiles * (cx + 2) * cy, 128), F32),
            pltpu.VMEM((voxels, 128), F32),
            pltpu.VMEM((voxels, 128), F32),
            pltpu.VMEM((cycles, tiles, 2, 2 * cx, 128), F32),
            pltpu.VMEM((cycles, tiles, 2, 2 * cx + 8, 128), F32),
            pltpu.VMEM((2, tiles, cx, 128), F32),
            pltpu.VMEM((2, tiles, cx, 128), F32),
            pltpu.VMEM((2, tiles, cx, 128), F32),
            pltpu.VMEM((groups, 128, 128), F32),
            pltpu.VMEM((2 * s * 8, 128), F32),
            pltpu.VMEM((1, 128), F32),
            pltpu.VMEM((total, 128), F32),
            pltpu.VMEM((128, 128), F32),
            pltpu.VMEM((128, 128), F32),
            pltpu.VMEM((voxels, 128), F32),
            pltpu.VMEM((peers, groups // peers, 128), F32),
            pltpu.SemaphoreType.DMA((tiles + 1, 3)),
            pltpu.SemaphoreType.DMA((2,)),
            pltpu.SemaphoreType.DMA((2, tiles, 2, 2)),
            pltpu.SemaphoreType.DMA((2,)),
            pltpu.SemaphoreType.DMA((2, tiles, 2)),
            pltpu.SemaphoreType.DMA((4,)),
            pltpu.SemaphoreType.DMA((2, tiles, 4)),
            pltpu.SemaphoreType.DMA((4,)),
            pltpu.SemaphoreType.DMA((tiles, 2)),
            pltpu.SemaphoreType.DMA((2,)),
            pltpu.SemaphoreType.DMA,
            pltpu.SemaphoreType.DMA,
            pltpu.SemaphoreType.DMA,
            pltpu.SemaphoreType.DMA,
        ],
        compiler_params=pltpu.CompilerParams(
            collective_id=0, has_side_effects=True, vmem_limit_bytes=52 * 2**20
        ),
    )(
        kept(source), kept(voxel_phase), kept(lin_potential), kept(jnp.asarray(gram_map())),
        kept(places), kept(link_count[0, 0]),
    )
    return pl.pallas_call(
        functools.partial(last_kernel, peers),
        out_shape=(
            jax.ShapeDtypeStruct(source.shape, F32),
            jax.ShapeDtypeStruct((1, 1, PART_DEV), F32),
        ),
        in_specs=[pl.BlockSpec(memory_space=pl.ANY)] * 3,
        out_specs=(far, far),
        scratch_shapes=[
            pltpu.VMEM((groups, 128), F32),
            pltpu.VMEM((groups, 128), jnp.int32),
            pltpu.VMEM((1, 1, PART_DEV), F32),
            pltpu.SemaphoreType.DMA((3,)),
        ],
        compiler_params=pltpu.CompilerParams(vmem_limit_bytes=2 * 2**20),
    )(found, got.reshape(groups, 128), kept(link_target[0, 0].reshape(groups, 128)))


def solution(mesh):
    spec = P("gx", "gy", None)
    return jax.shard_map(
        functools.partial(shards, (mesh.shape["gx"], mesh.shape["gy"])),
        mesh=mesh,
        in_specs=(spec,) * 6,
        out_specs=(spec, spec),
        check_vma=False,
    )
```

```python
import functools

import jax
import jax.numpy as jnp
import numpy as np
from jax import lax
from jax.experimental import pallas as pl
from jax.experimental.pallas import tpu as pltpu
from jax.sharding import PartitionSpec as P

ITERS = 12
PART_DEV = 512
ROWS = 16
RHS = 15
PAD = 8
LOW = 64
F32 = jnp.float32


def gram_map():
    s = ITERS
    n = 2 * s

    def unit(at):
        out = np.zeros(n)
        out[at] = 1.0
        return out

    m = []
    for k in range(s):
        m.append(2 * unit(2 * k) - unit(0))
        m.append(2 * unit(2 * k + 1) - unit(1))

    def entry(j, k):
        a, b = j + k, abs(j - k)
        return 0.5 * (
            m[a] - 0.5 * (m[a + 1] + m[abs(a - 1)]) + m[b] - 0.5 * (m[b + 1] + m[abs(b - 1)])
        )

    table = np.zeros((n, ROWS, 128))
    for j in range(s):
        table[:, j, RHS] = m[j]
        for k in range(s):
            table[:, j, k] = entry(j, k)
    return table.astype(np.float32)


def two_sum(a, b):
    s = a + b
    t = s - a
    return s, (a - (s - t)) + (b - t)


def quick_two_sum(a, b):
    s = a + b
    return s, b - (s - a)


def split(a):
    c = 4097.0 * a
    hi = c - (c - a)
    return hi, a - hi


def two_prod(a, b):
    p = a * b
    ah, al = split(a)
    bh, bl = split(b)
    return p, ((ah * bh - p) + ah * bl + al * bh) + al * bl


def dd_add(a, b):
    s, e = two_sum(a[0], b[0])
    return quick_two_sum(s, e + (a[1] + b[1]))


def dd_mul(a, b):
    p, e = two_prod(a[0], b[0])
    return quick_two_sum(p, e + (a[0] * b[1] + a[1] * b[0]))


def dd_inverse(a):
    x = 1.0 / a[0]
    p, e = two_prod(a[0], x)
    r = (1.0 - p) - e - a[1] * x
    return quick_two_sum(x, x * r)


def dd_minus(a, b):
    return dd_add(a, (-b[0], -b[1]))


def dd_solve(matrix):
    rows = lax.broadcasted_iota(jnp.int32, (ROWS, 128), 0)
    shape = (ROWS, 128)

    def column(j):
        return tuple(jnp.broadcast_to(m[:, j : j + 1], shape) for m in matrix)

    def row(a, j):
        return tuple(jnp.broadcast_to(m[j : j + 1, :], shape) for m in a)

    def eliminate(a, j, by, inverse):
        scaled = dd_mul(row(a, j), inverse)
        less = dd_minus(a, dd_mul(by, scaled))
        return tuple(jnp.where(rows == j, r, m) for r, m in zip(scaled, less))

    for j in range(0, ITERS, 2):
        one, two = column(j), column(j + 1)
        inverse = dd_inverse(row(one, j))
        two = eliminate(two, j, one, inverse)
        matrix = eliminate(matrix, j, one, inverse)
        matrix = eliminate(matrix, j + 1, two, dd_inverse(row(two, j + 1)))
    answer = matrix[0][:, RHS : RHS + 1]
    return [jnp.broadcast_to(answer[j : j + 1, :], (8, 128)) for j in range(ITERS)]


def flipped(index, mask, size):
    if size & (size - 1):
        return lax.rem(index + mask, size)
    out, bit = 0, 1
    while bit < size:
        out = out + lax.rem(index // bit + mask // bit, 2) * bit
        bit *= 2
    return out


def last_kernel(found, sums, out, particle, sems):
    pieces = [
        pltpu.make_async_copy(found, out, sems.at[0]),
        pltpu.make_async_copy(sums, particle, sems.at[1]),
    ]
    for copy in pieces:
        copy.start()
    for copy in pieces:
        copy.wait()


def kernel(
    sizes, source_hbm, phase_hbm, potential_hbm, map_hbm, places_hbm, count_hbm, target_hbm,
    out, particle,
    source, phase, potential, table, lines, voxel, places, count, target, vecs, diag, inv, base, slope, ybuf, hin,
    pinv, hinv, hodd, mask, dots, mine, parts, pick0, pick1, flat, sent, got, tally,
    isem, xsend, xrecv, ysend, yrecv, csend, crecv, vsend, vrecv, hrecv, rsend, rrecv, lsend, lrecv,
):
    n_gx, n_gy = sizes
    total = n_gx * n_gy
    cx, cy, cz = source_hbm.shape
    tiles = cz // 128
    pitch = cy + PAD
    block = (cx + 4) * pitch
    s = ITERS
    cycles = s // 2
    gx, gy = lax.axis_index("gx"), lax.axis_index("gy")
    me = gx * n_gy + gy
    mesh_id = pl.DeviceIdType.MESH

    barrier = pltpu.get_barrier_semaphore()

    def everyone(act):
        @pl.loop(0, n_gy)
        def _(step):
            to_gy = flipped(gy, n_gy - 1 - step, n_gy)

            @pl.loop(1, n_gx)
            def _(shift):
                act(lax.rem(gx + shift, n_gx), to_gy)

        @pl.loop(0, n_gy - 1)
        def _(step):
            act(gx, flipped(gy, n_gy - 1 - step, n_gy))

    everyone(
        lambda to_gx, to_gy: pl.semaphore_signal(
            barrier, inc=1, device_id=(to_gx, to_gy), device_id_type=mesh_id
        )
    )

    loads = []
    for c in range(tiles):
        for i, (src, dst) in enumerate(
            ((potential_hbm, potential), (phase_hbm, phase), (source_hbm, source))
        ):
            loads.append(
                pltpu.make_async_copy(
                    src.at[:, :, pl.ds(128 * c, 128)], dst.at[c], isem.at[c, i]
                )
            )
    extra = [
        pltpu.make_async_copy(map_hbm, table, isem.at[tiles, 0]),
        pltpu.make_async_copy(places_hbm, places, isem.at[tiles, 1]),
        pltpu.make_async_copy(count_hbm, count, isem.at[tiles + 1, 0]),
        pltpu.make_async_copy(target_hbm, target, isem.at[tiles + 1, 1]),
    ]
    for copy in loads + extra:
        copy.start()

    has_up, has_down = gx < n_gx - 1, gx > 0
    has_right, has_left = gy < n_gy - 1, gy > 0
    up_gx, down_gx = jnp.minimum(gx + 1, n_gx - 1), jnp.maximum(gx - 1, 0)
    right_gy, left_gy = jnp.minimum(gy + 1, n_gy - 1), jnp.maximum(gy - 1, 0)

    def row(x, c, y):
        return c * block + (x + 2) * pitch + PAD + y

    def inv_row(x, c, y):
        return (c * (cx + 2) + x + 1) * cy + y

    def flat_row(x, c, y):
        return (c * cx + x) * cy + y

    near, low_corner, high_corner = cx, 2 * cx + 1, 2 * cx
    zeros8 = jnp.zeros((8, 128), F32)
    zero_row = jnp.zeros((1, 128), F32)

    @pl.loop(-1, cx + 1)
    def _(x):
        for c in range(tiles):
            for y in range(0, cy, 8):
                vecs[0, pl.ds(row(x, c, y), 8), :] = zeros8

    @pl.loop(0, cycles)
    def _(j):
        @pl.loop(0, cx + 1)
        def _(x):
            for c in range(tiles):
                vecs[2 * j + 1, pl.ds(row(x, c, -PAD), 8), :] = zeros8

    hodd[...] = jnp.zeros(hodd.shape, F32)
    for beyond, x in ((gx == 0, -1), (gx == n_gx - 1, cx)):
        @pl.when(beyond)
        def _():
            for c in range(tiles):
                for y in range(0, cy, 8):
                    inv[pl.ds(inv_row(x, c, y), 8), :] = zeros8

            @pl.loop(0, cycles)
            def _(j):
                for c in range(tiles):
                    first = row(-2 if x < 0 else cx, c, 0)
                    for y in range(0, pitch + cy, 8):
                        vecs[2 * j + 1, pl.ds(first + y, 8), :] = zeros8
                    for side in range(2):
                        hin[j, c, side, pl.ds(low_corner if x < 0 else high_corner, 1), :] = zero_row

    for beyond, side in ((gy == 0, 0), (gy == n_gy - 1, 1)):
        @pl.when(beyond)
        def _():
            hinv[side] = jnp.zeros(hinv.shape[1:], F32)

            @pl.loop(0, cycles)
            def _(j):
                for c in range(tiles):
                    hin[j, c, side] = jnp.zeros(hin.shape[3:], F32)

    sides = ((0, 0, 1), (1, cy - 1, cy - 2))

    def pack_rows(j, c):
        k = 2 * j + 1
        for side, y1, y2 in sides:
            for x in range(0, cx, 8):
                ybuf[j, c, side, pl.ds(near + x, 8), :] = (
                    vecs[k, pl.ds(row(x, c, y1), 8, stride=pitch), :]
                )
                ybuf[j, c, side, pl.ds(x, 8), :] = vecs[k, pl.ds(row(x, c, y2), 8, stride=pitch), :]

    def xcopy(j, c, way, layer):
        up = way == 0
        return pltpu.make_async_remote_copy(
            src_ref=vecs.at[2 * j + 1, pl.ds(row(cx - 1 - layer if up else layer, c, 0), cy), :],
            dst_ref=vecs.at[2 * j + 1, pl.ds(row(-1 - layer if up else cx + layer, c, 0), cy), :],
            send_sem=xsend.at[way], recv_sem=xrecv.at[lax.rem(j, 2), c, way, layer],
            device_id=(up_gx if up else down_gx, gy), device_id_type=mesh_id,
        )

    def ycopy(j, c, way):
        right = way == 0
        return pltpu.make_async_remote_copy(
            src_ref=ybuf.at[j, c, 1 if right else 0],
            dst_ref=hin.at[j, c, 0 if right else 1, pl.ds(0, 2 * cx), :],
            send_sem=ysend.at[way], recv_sem=yrecv.at[lax.rem(j, 2), c, way],
            device_id=(gx, right_gy if right else left_gy), device_id_type=mesh_id,
        )

    def ccopy(j, c, xway, yway):
        up, right = xway == 0, yway == 0
        q = 2 * xway + yway
        return pltpu.make_async_remote_copy(
            src_ref=vecs.at[
                2 * j + 1, pl.ds(row(cx - 1 if up else 0, c, cy - 1 if right else 0), 1), :
            ],
            dst_ref=hin.at[j, c, 0 if right else 1, pl.ds(low_corner if up else high_corner, 1), :],
            send_sem=csend.at[q], recv_sem=crecv.at[lax.rem(j, 2), c, q],
            device_id=(up_gx if up else down_gx, right_gy if right else left_gy),
            device_id_type=mesh_id,
        )

    def vcopy(c, way):
        up = way == 0
        return pltpu.make_async_remote_copy(
            src_ref=inv.at[pl.ds(inv_row(cx - 1 if up else 0, c, 0), cy), :],
            dst_ref=inv.at[pl.ds(inv_row(-1 if up else cx, c, 0), cy), :],
            send_sem=vsend.at[way], recv_sem=vrecv.at[c, way],
            device_id=(up_gx if up else down_gx, gy), device_id_type=mesh_id,
        )

    def hcopy(way):
        right = way == 0
        return pltpu.make_async_remote_copy(
            src_ref=pinv.at[1 if right else 0], dst_ref=hinv.at[0 if right else 1],
            send_sem=vsend.at[2 + way], recv_sem=hrecv.at[way],
            device_id=(gx, right_gy if right else left_gy), device_id_type=mesh_id,
        )

    for c in range(tiles):
        for copy in loads[3 * c : 3 * c + 3]:
            copy.wait()

        @pl.loop(0, cx)
        def _(x):
            found = []
            for y in range(0, cy, 8):
                at = potential[c, x, y : y + 8, :]
                rising = jnp.exp(0.4 * at)
                falling = jnp.exp(-0.6 * at)
                label = phase[c, x, y : y + 8, :]
                rate = jnp.where(label == 1, 0.3, jnp.where(label == 2, 0.08, 0.02)).astype(F32)
                bend = 0.4 * rising + 0.6 * falling
                d = 6.0 + rate * bend
                i = 1.0 / d
                found.append((y, rising - falling, bend, d, i, source[c, x, y : y + 8, :] * i))
            for y, level, bend, d, i, v in found:
                f = pl.ds(flat_row(x, c, y), 8)
                base[f, :] = level
                slope[f, :] = bend
                diag[f, :] = d
                inv[pl.ds(inv_row(x, c, y), 8), :] = i
                vecs[1, pl.ds(row(x, c, y), 8), :] = v

        pack_rows(0, c)
        for side, y, _ in sides:
            for x in range(0, cx, 8):
                pinv[side, c, pl.ds(x, 8), :] = inv[pl.ds(inv_row(x, c, y), 8, stride=cy), :]

    def launch_x(j, c, more):
        for way, there in ((0, has_up), (1, has_down)):
            @pl.when(there & more)
            def _():
                pl.when(has_right)(ccopy(j, c, way, 0).start)
                pl.when(has_left)(ccopy(j, c, way, 1).start)
                xcopy(j, c, way, 0).start()
                xcopy(j, c, way, 1).start()

    def launch_y(j, c, more):
        pl.when(has_right & more)(ycopy(j, c, 0).start)
        pl.when(has_left & more)(ycopy(j, c, 1).start)

    def landed_near(j, c):
        pl.when(has_left)(ycopy(j, c, 0).wait_recv)
        pl.when(has_right)(ycopy(j, c, 1).wait_recv)
        pl.when(has_down)(xcopy(j, c, 0, 0).wait_recv)
        pl.when(has_up)(xcopy(j, c, 1, 0).wait_recv)

    def landed_far(j, c):
        for way, there in ((0, has_down), (1, has_up)):
            @pl.when(there)
            def _():
                pl.when(has_left)(ccopy(j, c, way, 0).wait_recv)
                pl.when(has_right)(ccopy(j, c, way, 1).wait_recv)
                xcopy(j, c, way, 1).wait_recv()
                pl.when(j == 0)(vcopy(c, way).wait_recv)

    def drained(rows, sem):
        ref = vecs.at[0, pl.ds(0, rows), :]
        pltpu.make_async_copy(ref, ref, sem).wait()

    with jax.named_scope("barrier"):
        pl.semaphore_wait(barrier, total - 1)

    always = gx >= 0
    pl.when(has_right)(hcopy(0).start)
    pl.when(has_left)(hcopy(1).start)
    for c in range(tiles):
        launch_x(0, c, always)
        launch_y(0, c, always)
        pl.when(has_up)(vcopy(c, 0).start)
        pl.when(has_down)(vcopy(c, 1).start)

    groups = places.shape[0]
    wide = groups // n_gy
    for copy in extra:
        copy.wait()
    lines[...] = places[...] >> 7
    scalar_lines = pltpu.make_async_copy(lines, voxel, isem.at[tiles, 2])
    scalar_lines.start()

    @pl.loop(0, n_gy)
    def _(peer):
        live = count[peer]
        lanes = lax.broadcasted_iota(jnp.int32, (128, 128), 1)
        rows = lax.broadcasted_iota(jnp.int32, (128, 128), 0)
        for part in range(wide):
            at = (places[pl.ds(peer * wide + part, 1), :] & 127).astype(F32)
            at = jnp.broadcast_to(at, (128, 128)).T
            mask[peer * wide + part] = jnp.where(
                (lanes.astype(F32) == at) & (rows + 128 * part < live), 0.5, 0.0
            )

    lane8 = lax.broadcasted_iota(jnp.int32, (8, 128), 1)
    sub8 = lax.broadcasted_iota(jnp.int32, (8, 128), 0)
    first_lane, last_lane = lane8 == 0, lane8 == 127

    def beside(v, before, after):
        z = pltpu.roll(jnp.where(last_lane, before, v), 1, 1)
        return z + pltpu.roll(jnp.where(first_lane, after, v), 127, 1)

    def sweep(k, c, start, offsets, scale, carry=None):
        centers = {}

        def center(o, y):
            if (o, y) not in centers:
                centers[o, y] = vecs[k, pl.ds(row(start + o, c, y), 8), :]
            return centers[o, y]

        found = []
        for y in range(0, cy, 8):
            for o in offsets:
                r = row(start + o, c, y)
                v = center(o, y)
                before = vecs[k, pl.ds(r - block, 8), :] if c > 0 else 0.0
                after = vecs[k, pl.ds(r + block, 8), :] if c < tiles - 1 else 0.0
                n = vecs[k, pl.ds(r - 1, 8), :] + vecs[k, pl.ds(r + 1, 8), :]
                n = (n + beside(v, before, after)) + (center(o - 1, y) + center(o + 1, y))
                i = inv[pl.ds(inv_row(start + o, c, y), 8), :]
                new = (scale * i) * n - vecs[k - 1, pl.ds(r, 8), :]
                if carry is not None:
                    w = diag[pl.ds(flat_row(start + o, c, y), 8), :] * v
                    carry = (carry[0] + w * v, carry[1] + w * new)
                found.append((r, new))
        for r, new in found:
            vecs[k + 1, pl.ds(r, 8), :] = new
        return carry

    def inner(k, c, first, last, scale, carry):
        group = max(g for g in range(1, 8) if (last - first) % g == 0)

        def some(i, a):
            return sweep(k, c, group * i + first, range(group), scale, a)

        return lax.fori_loop(0, (last - first) // group, some, carry)

    def border(j, c, scale, carry):
        k = 2 * j + 1
        carry = sweep(k, c, 0, (0,), scale, carry)
        carry = sweep(k, c, cx - 1, (0,), scale, carry)
        own, cross = carry
        found = []
        for side, y, _ in sides:
            for x in range(0, cx, 8):
                at = pl.ds(near + x, 8)
                h = hin[j, c, side, at, :]
                line = pl.ds(row(x, c, y), 8, stride=pitch)
                fixed = vecs[k + 1, line, :] + (scale * pinv[side, c, pl.ds(x, 8), :]) * h
                cross = cross + (scale * ybuf[j, c, side, at, :]) * h
                found.append((line, fixed))
        for line, fixed in found:
            vecs[k + 1, line, :] = fixed
        return own, cross

    def shell(j, c, scale):
        k = 2 * j + 1
        for side, y in ((0, -1), (1, cy)):
            for x, at in ((-1, low_corner), (cx, high_corner)):
                vecs[k, pl.ds(row(x, c, y), 1), :] = hin[j, c, side, pl.ds(at, 1), :]
        sweep(k, c, -1, (0,), scale)
        sweep(k, c, cx, (0,), scale)
        found = []
        for side, beyond in ((0, -1), (1, cy)):
            for x in range(0, cx, 8):
                at = pl.ds(near + x, 8)
                h = hin[j, c, side, at, :]
                before = hin[j, c - 1, side, at, :] if c > 0 else 0.0
                after = hin[j, c + 1, side, at, :] if c < tiles - 1 else 0.0
                lower = hin[j, c, side, pl.ds(near + x - 1, 8), :]
                if x == 0:
                    corner = hin[j, c, side, pl.ds(low_corner, 1), :]
                    lower = jnp.where(sub8 == 0, corner, lower)
                upper = hin[j, c, side, pl.ds(near + x + 1, 8), :]
                n = (lower + upper) + (hin[j, c, side, pl.ds(x, 8), :] + ybuf[j, c, side, at, :])
                n = n + beside(h, before, after)
                old = pl.ds(x, 8)
                new = (scale * hinv[side, c, old, :]) * n - hodd[side, c, old, :]
                found.append((side, old, new, pl.ds(row(x, c, beyond), 8, stride=pitch)))
        for side, old, new, outer in found:
            hodd[side, c, old, :] = new
            vecs[k + 1, outer, :] = new

    def finish(j, c, carry):
        k = 2 * j + 2
        more = j < cycles - 1
        carry = sweep(k, c, 0, (0, 1), 2.0, carry)
        carry = sweep(k, c, cx - 2, (0, 1), 2.0, carry)
        launch_x(j + 1, c, more)
        carry = inner(k, c, 2, cx - 2, 2.0, carry)

        @pl.when(more)
        def _():
            pack_rows(j + 1, c)
            launch_y(j + 1, c, always)

        return carry

    @pl.loop(0, cycles)
    def _(j):
        with jax.named_scope("cycle"):
            scale = jnp.where(j == 0, 1.0, 2.0).astype(F32)
            first = second = (zeros8, zeros8)
            with jax.named_scope("ainner"):
                for c in range(tiles):
                    first = inner(2 * j + 1, c, 1, cx - 1, scale, first)

            @pl.when(j == 0)
            def _():
                pl.when(has_left)(hcopy(0).wait_recv)
                pl.when(has_right)(hcopy(1).wait_recv)

            for c in range(tiles):
                for d in (0, 1) if c == 0 else (c + 1,):
                    if d < tiles:
                        with jax.named_scope("landed"):
                            landed_near(j, d)
                        first = border(j, d, scale, first)
                with jax.named_scope("landed"):
                    landed_far(j, c)
                shell(j, c, scale)
                second = finish(j, c, second)
            for i, value in enumerate((*first, *second)):
                dots[pl.ds(pl.multiple_of(32 * j + 8 * i, 8), 8), :] = value

    scalar_lines.wait()

    with jax.named_scope("reduce"):
        sums = []
        for g in range(2 * s // 8):
            level = [dots[pl.ds(64 * g + i, 8, stride=8), :] for i in range(8)]
            level = [two_sum(level[2 * i], level[2 * i + 1]) for i in range(4)]
            while len(level) > 1:
                level = [dd_add(level[2 * i], level[2 * i + 1]) for i in range(len(level) // 2)]
            sums.append(level[0])
        for shift in (64, 32, 16, 8, 4, 2, 1):
            sums = [
                dd_add(a, tuple(pltpu.roll(p, shift, 1) for p in a)) for a in sums
            ]
        spread = zeros8
        for g, (hi, lo) in enumerate(sums):
            spread = jnp.where(lane8 == sub8 + 8 * g, hi, spread)
            spread = jnp.where(lane8 == sub8 + 8 * g + LOW, lo, spread)
        line = jnp.sum(spread, axis=0, keepdims=True)
        mine[...] = line
        parts[pl.ds(me, 1), :] = line

        everyone(
            lambda to_gx, to_gy: pltpu.make_async_remote_copy(
                src_ref=mine, dst_ref=parts.at[pl.ds(me, 1), :],
                send_sem=rsend, recv_sem=rrecv,
                device_id=(to_gx, to_gy), device_id_type=mesh_id,
            ).start()
        )

        for way, there in ((0, has_up), (1, has_down)):
            @pl.when(there)
            def _():
                drained(cycles * tiles * 2 * cy, xsend.at[way])
                drained(tiles * cy, vsend.at[way])
                for q, also in ((0, has_right), (1, has_left)):
                    @pl.when(also)
                    def _():
                        drained(cycles * tiles, csend.at[2 * way + q])

        for way, there in ((0, has_right), (1, has_left)):
            @pl.when(there)
            def _():
                drained(cycles * tiles * 2 * cx, ysend.at[way])
                drained(tiles * cx, vsend.at[2 + way])

        drained(total - 1, rrecv)

    with jax.named_scope("solve"):
        level = [parts[8 * i : 8 * i + 8, :] for i in range(total // 8)]
        level = [(a, pltpu.roll(a, 128 - LOW, 1)) for a in level]
        while len(level) > 1:
            level = [dd_add(level[2 * i], level[2 * i + 1]) for i in range(len(level) // 2)]
        every = level[0]
        for shift in (4, 2, 1):
            every = dd_add(every, tuple(pltpu.roll(p, shift, 0) for p in every))
        terms = []
        for m in range(2 * s):
            hi, lo = (jnp.broadcast_to(p[0:1, m : m + 1], (ROWS, 128)) for p in every)
            terms.append((table[m] * hi, table[m] * lo))
        while len(terms) > 1:
            terms = [
                dd_add(terms[i], terms[i + 1]) if i + 1 < len(terms) else terms[i]
                for i in range(0, len(terms), 2)
            ]
        weights = dd_solve(terms[0])

    with jax.named_scope("combine"):
        @pl.loop(0, cx)
        def _(x):
            for c in range(tiles):
                for y in range(0, cy, 8):
                    pieces = [
                        w * vecs[1 + k, pl.ds(row(x, c, y), 8), :] for k, w in enumerate(weights)
                    ]
                    while len(pieces) > 1:
                        pieces = [sum(pieces[i : i + 2]) for i in range(0, len(pieces), 2)]
                    out[x, y : y + 8, 128 * c : 128 * (c + 1)] = pieces[0]
                    f = pl.ds(flat_row(x, c, y), 8)
                    at = (x * cy + y) * tiles + c
                    flat[pl.ds(at, 8, stride=tiles), :] = base[f, :] + slope[f, :] * pieces[0]

    picks = (pick0, pick1)

    def gathered(peer):
        for part in range(wide):
            group = peer * wide + part
            for i in range(128):
                picks[part % 2][pl.ds(i, 1), :] = flat[pl.ds(voxel[group, i], 1), :]
            value = picks[part % 2][...] * mask[group]
            sent[peer, pl.ds(part, 1), :] = jnp.sum(value.T, axis=0, keepdims=True)

    with jax.named_scope("gather"):
        @pl.loop(0, n_gy - 1)
        def _(step):
            peer = flipped(gy, n_gy - 1 - step, n_gy)
            gathered(peer)
            pltpu.make_async_remote_copy(
                src_ref=sent.at[peer], dst_ref=got.at[gy], send_sem=lsend, recv_sem=lrecv.at[gy],
                device_id=(gx, peer), device_id_type=mesh_id,
            ).start()

        gathered(gy)
        got[gy] = sent[gy]

    own = tally.shape[0]

    def tallied(peer, first):
        spots = [target[pl.ds(peer * wide + part, 1), :] for part in range(wide)]
        values = [got[peer, part : part + 1, :] for part in range(wide)]
        for start in range(0, own, 128):
            found = []
            for r in range(start, start + 128, 8):
                total_ = zeros8 if first else tally[r : r + 8, :]
                for spot, value in zip(spots, values):
                    total_ = total_ + jnp.where(spot == sub8 + r, value, 0.0)
                found.append((r, total_))
            for r, total_ in found:
                tally[r : r + 8, :] = total_

    with jax.named_scope("links"):
        tallied(gy, True)
        drained(total - 1, rsend)

        @pl.loop(0, n_gy - 1)
        def _(step):
            peer = flipped(gy, n_gy - 1 - step, n_gy)
            pltpu.make_async_copy(got.at[peer], got.at[peer], lrecv.at[peer]).wait()
            tallied(peer, False)

        for start in range(0, own, 128):
            particle[0, :, start : start + 128] = jnp.sum(
                tally[start : start + 128, :].T, axis=0, keepdims=True
            )
        drained((n_gy - 1) * wide, lsend)


def kept(x):
    return pltpu.with_memory_space_constraint(x, pltpu.HBM)


def shards(sizes, source, voxel_phase, lin_potential, link_voxel, link_count, link_target):
    cx, cy, cz = source.shape
    total = sizes[0] * sizes[1]
    s = ITERS
    tiles = cz // 128
    voxels = cx * cy * tiles
    padded = (cx + 4) * tiles * (cy + PAD) + 8
    cycles = s // 2
    places = link_voxel[0, 0].reshape(-1, 128)
    peers = link_count.shape[2]
    slots = link_voxel.shape[2]
    groups = slots // 128
    whole = pl.BlockSpec(memory_space=pltpu.VMEM)
    far = pl.BlockSpec(memory_space=pltpu.HBM)
    found, sums = pl.pallas_call(
        functools.partial(kernel, sizes),
        out_shape=(
            jax.ShapeDtypeStruct(source.shape, F32),
            jax.ShapeDtypeStruct((1, 1, PART_DEV), F32),
        ),
        in_specs=[far] * 7,
        out_specs=(whole, whole),
        scratch_shapes=[
            pltpu.VMEM((tiles, cx, cy, 128), F32),
            pltpu.VMEM((tiles, cx, cy, 128), jnp.int32),
            pltpu.VMEM((tiles, cx, cy, 128), F32),
            pltpu.VMEM((2 * s, ROWS, 128), F32),
            pltpu.VMEM((groups, 128), jnp.int32),
            pltpu.SMEM((groups, 128), jnp.int32),
            pltpu.VMEM((groups, 128), jnp.int32),
            pltpu.SMEM((peers,), jnp.int32),
            pltpu.VMEM((groups, 128), jnp.int32),
            pltpu.VMEM((s + 2, padded, 128), F32),
            pltpu.VMEM((voxels, 128), F32),
            pltpu.VMEM((tiles * (cx + 2) * cy, 128), F32),
            pltpu.VMEM((voxels, 128), F32),
            pltpu.VMEM((voxels, 128), F32),
            pltpu.VMEM((cycles, tiles, 2, 2 * cx, 128), F32),
            pltpu.VMEM((cycles, tiles, 2, 2 * cx + 8, 128), F32),
            pltpu.VMEM((2, tiles, cx, 128), F32),
            pltpu.VMEM((2, tiles, cx, 128), F32),
            pltpu.VMEM((2, tiles, cx, 128), F32),
            pltpu.VMEM((groups, 128, 128), F32),
            pltpu.VMEM((2 * s * 8, 128), F32),
            pltpu.VMEM((1, 128), F32),
            pltpu.VMEM((total, 128), F32),
            pltpu.VMEM((128, 128), F32),
            pltpu.VMEM((128, 128), F32),
            pltpu.VMEM((voxels, 128), F32),
            pltpu.VMEM((peers, groups // peers, 128), F32),
            pltpu.VMEM((peers, groups // peers, 128), F32),
            pltpu.VMEM((PART_DEV, 128), F32),
            pltpu.SemaphoreType.DMA((tiles + 2, 3)),
            pltpu.SemaphoreType.DMA((2,)),
            pltpu.SemaphoreType.DMA((2, tiles, 2, 2)),
            pltpu.SemaphoreType.DMA((2,)),
            pltpu.SemaphoreType.DMA((2, tiles, 2)),
            pltpu.SemaphoreType.DMA((4,)),
            pltpu.SemaphoreType.DMA((2, tiles, 4)),
            pltpu.SemaphoreType.DMA((4,)),
            pltpu.SemaphoreType.DMA((tiles, 2)),
            pltpu.SemaphoreType.DMA((2,)),
            pltpu.SemaphoreType.DMA,
            pltpu.SemaphoreType.DMA,
            pltpu.SemaphoreType.DMA,
            pltpu.SemaphoreType.DMA((peers,)),
        ],
        compiler_params=pltpu.CompilerParams(
            collective_id=0, has_side_effects=True, vmem_limit_bytes=52 * 2**20
        ),
    )(
        kept(source), kept(voxel_phase), kept(lin_potential), kept(jnp.asarray(gram_map())),
        kept(places), kept(link_count[0, 0]), kept(link_target[0, 0].reshape(groups, 128)),
    )
    return pl.pallas_call(
        last_kernel,
        out_shape=(
            jax.ShapeDtypeStruct(source.shape, F32),
            jax.ShapeDtypeStruct((1, 1, PART_DEV), F32),
        ),
        in_specs=[pl.BlockSpec(memory_space=pl.ANY)] * 2,
        out_specs=(far, far),
        scratch_shapes=[pltpu.SemaphoreType.DMA((2,))],
        compiler_params=pltpu.CompilerParams(vmem_limit_bytes=2 * 2**20),
    )(found, sums)


def solution(mesh):
    spec = P("gx", "gy", None)
    return jax.shard_map(
        functools.partial(shards, (mesh.shape["gx"], mesh.shape["gy"])),
        mesh=mesh,
        in_specs=(spec,) * 6,
        out_specs=(spec, spec),
        check_vma=False,
    )
```

```python
import functools

import jax
import jax.numpy as jnp
import numpy as np
from jax import lax
from jax.experimental import pallas as pl
from jax.experimental.pallas import tpu as pltpu
from jax.sharding import PartitionSpec as P

ITERS = 12
PART_DEV = 512
ROWS = 16
RHS = 15
PAD = 8
LOW = 64
F32 = jnp.float32


def gram_map():
    s = ITERS
    n = 2 * s

    def unit(at):
        out = np.zeros(n)
        out[at] = 1.0
        return out

    m = []
    for k in range(s):
        m.append(2 * unit(2 * k) - unit(0))
        m.append(2 * unit(2 * k + 1) - unit(1))

    def entry(j, k):
        a, b = j + k, abs(j - k)
        return 0.5 * (
            m[a] - 0.5 * (m[a + 1] + m[abs(a - 1)]) + m[b] - 0.5 * (m[b + 1] + m[abs(b - 1)])
        )

    table = np.zeros((n, ROWS, 128))
    for j in range(s):
        table[:, j, RHS] = m[j]
        for k in range(s):
            table[:, j, k] = entry(j, k)
    return table.astype(np.float32)


def two_sum(a, b):
    s = a + b
    t = s - a
    return s, (a - (s - t)) + (b - t)


def quick_two_sum(a, b):
    s = a + b
    return s, b - (s - a)


def split(a):
    c = 4097.0 * a
    hi = c - (c - a)
    return hi, a - hi


def two_prod(a, b):
    p = a * b
    ah, al = split(a)
    bh, bl = split(b)
    return p, ((ah * bh - p) + ah * bl + al * bh) + al * bl


def dd_add(a, b):
    s, e = two_sum(a[0], b[0])
    return quick_two_sum(s, e + (a[1] + b[1]))


def dd_mul(a, b):
    p, e = two_prod(a[0], b[0])
    return quick_two_sum(p, e + (a[0] * b[1] + a[1] * b[0]))


def dd_inverse(a):
    x = 1.0 / a[0]
    p, e = two_prod(a[0], x)
    r = (1.0 - p) - e - a[1] * x
    return quick_two_sum(x, x * r)


def dd_minus(a, b):
    return dd_add(a, (-b[0], -b[1]))


def dd_solve(matrix):
    rows = lax.broadcasted_iota(jnp.int32, (ROWS, 128), 0)
    shape = (ROWS, 128)

    def column(j):
        return tuple(jnp.broadcast_to(m[:, j : j + 1], shape) for m in matrix)

    def row(a, j):
        return tuple(jnp.broadcast_to(m[j : j + 1, :], shape) for m in a)

    def eliminate(a, j, by, inverse):
        scaled = dd_mul(row(a, j), inverse)
        less = dd_minus(a, dd_mul(by, scaled))
        return tuple(jnp.where(rows == j, r, m) for r, m in zip(scaled, less))

    for j in range(0, ITERS, 2):
        one, two = column(j), column(j + 1)
        inverse = dd_inverse(row(one, j))
        two = eliminate(two, j, one, inverse)
        matrix = eliminate(matrix, j, one, inverse)
        matrix = eliminate(matrix, j + 1, two, dd_inverse(row(two, j + 1)))
    answer = matrix[0][:, RHS : RHS + 1]
    return [jnp.broadcast_to(answer[j : j + 1, :], (8, 128)) for j in range(ITERS)]


def partners(index, size):
    if size & (size - 1):
        return [lax.rem(index + m, size) for m in range(size)]
    out = [0]
    bit = 1
    while bit < size:
        same = lax.rem(index // bit, 2) * bit
        out = [o + same for o in out] + [o + (bit - same) for o in out]
        bit *= 2
    return out


def flipped(index, m, size):
    if size & (size - 1):
        return lax.rem(index + m, size)
    out, bit = 0, 1
    while bit < size:
        out = out + lax.rem(index // bit + m // bit, 2) * bit
        bit *= 2
    return out


def last_kernel(found, sums, out, particle, sems):
    pieces = [
        pltpu.make_async_copy(found, out, sems.at[0]),
        pltpu.make_async_copy(sums, particle, sems.at[1]),
    ]
    for copy in pieces:
        copy.start()
    for copy in pieces:
        copy.wait()


def kernel(
    sizes, source_hbm, phase_hbm, potential_hbm, map_hbm, places_hbm, count_hbm, target_hbm,
    out, particle,
    source, phase, potential, table, lines, voxel, places, count, target, vecs, diag, inv, base, slope, ybuf, hin,
    pinv, hinv, hodd, mask, dots, mine, parts, pick0, pick1, flat, sent, got, tally,
    isem, xsend, ysend, csend, hrecv, vsend, vrecv, rsend, rrecv, lsend, lrecv,
):
    n_gx, n_gy = sizes
    total = n_gx * n_gy
    cx, cy, cz = source_hbm.shape
    tiles = cz // 128
    pitch = cy + PAD
    block = (cx + 4) * pitch
    s = ITERS
    cycles = s // 2
    gx, gy = lax.axis_index("gx"), lax.axis_index("gy")
    me = gx * n_gy + gy
    mesh_id = pl.DeviceIdType.MESH

    barrier = pltpu.get_barrier_semaphore()

    gy_of = partners(gy, n_gy)
    gx_of = partners(gx, n_gx)

    def everyone(act):
        for m in reversed(range(n_gy)):
            for q in reversed(range(n_gx)):
                if m or q:
                    act(gx_of[q], gy_of[m])


    loads = []
    for c in range(tiles):
        for src, dst in (
            (potential_hbm, potential), (phase_hbm, phase), (source_hbm, source)
        ):
            loads.append(
                pltpu.make_async_copy(
                    src.at[:, :, pl.ds(128 * c, 128)], dst.at[c], isem.at[c]
                )
            )
    extra = [
        pltpu.make_async_copy(map_hbm, table, isem.at[tiles]),
        pltpu.make_async_copy(places_hbm, places, isem.at[tiles]),
        pltpu.make_async_copy(count_hbm, count, isem.at[tiles + 1]),
        pltpu.make_async_copy(target_hbm, target, isem.at[tiles]),
    ]
    for copy in loads[:3]:
        copy.start()
    everyone(
        lambda to_gx, to_gy: pl.semaphore_signal(
            barrier, inc=1, device_id=(to_gx, to_gy), device_id_type=mesh_id
        )
    )
    for copy in loads[3:] + extra:
        copy.start()

    has_up, has_down = gx < n_gx - 1, gx > 0
    has_right, has_left = gy < n_gy - 1, gy > 0
    up_gx, down_gx = jnp.minimum(gx + 1, n_gx - 1), jnp.maximum(gx - 1, 0)
    right_gy, left_gy = jnp.minimum(gy + 1, n_gy - 1), jnp.maximum(gy - 1, 0)

    def row(x, c, y):
        return c * block + (x + 2) * pitch + PAD + y

    def inv_row(x, c, y):
        return (c * (cx + 2) + x + 1) * cy + y

    def flat_row(x, c, y):
        return (c * cx + x) * cy + y

    def drained(rows, sem):
        ref = vecs.at[0, pl.ds(0, rows), :]
        pltpu.make_async_copy(ref, ref, sem).wait()

    def counts(one, other, size):
        if size < 3:
            return [(size - 1, None)]
        both = one & other
        return [(1, jnp.logical_not(both)), (2, both)]

    x_counts = counts(has_up, has_down, n_gx)
    y_counts = counts(has_right, has_left, n_gy)

    def taken(sem, rows):
        for a, so_many_x in x_counts:
            for b, so_many_y in y_counts:
                if not rows(a, b):
                    continue
                there = [t for t in (so_many_x, so_many_y) if t is not None]
                if there:
                    pl.when(functools.reduce(jnp.logical_and, there))(
                        functools.partial(drained, rows(a, b), sem)
                    )
                else:
                    drained(rows(a, b), sem)

    near, low_corner, high_corner = cx, 2 * cx + 1, 2 * cx
    zeros8 = jnp.zeros((8, 128), F32)
    zero_row = jnp.zeros((1, 128), F32)

    sides = ((0, 0, 1), (1, cy - 1, cy - 2))

    def pack_rows(j, c):
        k = 2 * j + 1
        for side, y1, y2 in sides:
            for x in range(0, cx, 8):
                ybuf[j, c, side, pl.ds(near + x, 8), :] = (
                    vecs[k, pl.ds(row(x, c, y1), 8, stride=pitch), :]
                )
                ybuf[j, c, side, pl.ds(x, 8), :] = vecs[k, pl.ds(row(x, c, y2), 8, stride=pitch), :]

    def xcopy(j, c, way, layer):
        up = way == 0
        return pltpu.make_async_remote_copy(
            src_ref=vecs.at[2 * j + 1, pl.ds(row(cx - 1 - layer if up else layer, c, 0), cy), :],
            dst_ref=vecs.at[2 * j + 1, pl.ds(row(-1 - layer if up else cx + layer, c, 0), cy), :],
            send_sem=xsend.at[way], recv_sem=hrecv.at[lax.rem(j, 2), c, layer],
            device_id=(up_gx if up else down_gx, gy), device_id_type=mesh_id,
        )

    def ycopy(j, c, way):
        right = way == 0
        return pltpu.make_async_remote_copy(
            src_ref=ybuf.at[j, c, 1 if right else 0],
            dst_ref=hin.at[j, c, 0 if right else 1, pl.ds(0, 2 * cx), :],
            send_sem=ysend.at[way], recv_sem=hrecv.at[lax.rem(j, 2), c, 0],
            device_id=(gx, right_gy if right else left_gy), device_id_type=mesh_id,
        )

    def ccopy(j, c, xway, yway):
        up, right = xway == 0, yway == 0
        q = 2 * xway + yway
        return pltpu.make_async_remote_copy(
            src_ref=vecs.at[
                2 * j + 1, pl.ds(row(cx - 1 if up else 0, c, cy - 1 if right else 0), 1), :
            ],
            dst_ref=hin.at[j, c, 0 if right else 1, pl.ds(low_corner if up else high_corner, 1), :],
            send_sem=csend.at[q], recv_sem=hrecv.at[lax.rem(j, 2), c, 1],
            device_id=(up_gx if up else down_gx, right_gy if right else left_gy),
            device_id_type=mesh_id,
        )

    def vcopy(c, way):
        up = way == 0
        return pltpu.make_async_remote_copy(
            src_ref=inv.at[pl.ds(inv_row(cx - 1 if up else 0, c, 0), cy), :],
            dst_ref=inv.at[pl.ds(inv_row(-1 if up else cx, c, 0), cy), :],
            send_sem=vsend.at[way], recv_sem=vrecv.at[c],
            device_id=(up_gx if up else down_gx, gy), device_id_type=mesh_id,
        )

    def hcopy(way):
        right = way == 0
        return pltpu.make_async_remote_copy(
            src_ref=pinv.at[1 if right else 0], dst_ref=hinv.at[0 if right else 1],
            send_sem=vsend.at[2 + way], recv_sem=vrecv.at[tiles],
            device_id=(gx, right_gy if right else left_gy), device_id_type=mesh_id,
        )

    for c in range(tiles):
        drained(3 * cx * cy, isem.at[c])

        @pl.loop(0, cx)
        def _(x):
            found = []
            for y in range(0, cy, 8):
                at = potential[c, x, y : y + 8, :]
                rising = jnp.exp(0.4 * at)
                falling = jnp.exp(-0.6 * at)
                label = phase[c, x, y : y + 8, :]
                rate = jnp.where(label == 1, 0.3, jnp.where(label == 2, 0.08, 0.02)).astype(F32)
                bend = 0.4 * rising + 0.6 * falling
                d = 6.0 + rate * bend
                i = 1.0 / d
                found.append((y, rising - falling, bend, d, i, source[c, x, y : y + 8, :] * i))
            for y, level, bend, d, i, v in found:
                f = pl.ds(flat_row(x, c, y), 8)
                base[f, :] = level
                slope[f, :] = bend
                diag[f, :] = d
                inv[pl.ds(inv_row(x, c, y), 8), :] = i
                vecs[1, pl.ds(row(x, c, y), 8), :] = v

        pack_rows(0, c)
        for side, y, _ in sides:
            for x in range(0, cx, 8):
                pinv[side, c, pl.ds(x, 8), :] = inv[pl.ds(inv_row(x, c, y), 8, stride=cy), :]

    def launch_x(j, c, more):
        for way, there in ((0, has_up), (1, has_down)):
            @pl.when(there & more)
            def _():
                pl.when(has_right)(ccopy(j, c, way, 0).start)
                pl.when(has_left)(ccopy(j, c, way, 1).start)
                xcopy(j, c, way, 0).start()
                xcopy(j, c, way, 1).start()

    def launch_y(j, c, more):
        pl.when(has_right & more)(ycopy(j, c, 0).start)
        pl.when(has_left & more)(ycopy(j, c, 1).start)

    def landed_near(j, c):
        taken(hrecv.at[lax.rem(j, 2), c, 0], lambda a, b: a * cy + b * 2 * cx)

    def landed_far(j, c):
        taken(hrecv.at[lax.rem(j, 2), c, 1], lambda a, b: a * (cy + b))

        @pl.when(j == 0)
        def _():
            taken(vrecv.at[c], lambda a, b: a * cy)

    with jax.named_scope("barrier"):
        pl.semaphore_wait(barrier, total - 1)

    always = gx >= 0
    pl.when(has_right)(hcopy(0).start)
    pl.when(has_left)(hcopy(1).start)
    for c in range(tiles):
        launch_x(0, c, always)
        launch_y(0, c, always)
        pl.when(has_up)(vcopy(c, 0).start)
        pl.when(has_down)(vcopy(c, 1).start)

    groups = places.shape[0]
    wide = groups // n_gy
    drained(table.shape[0] * ROWS + 2 * groups, isem.at[tiles])
    pltpu.make_async_copy(count_hbm, count, isem.at[tiles + 1]).wait()
    lines[...] = places[...] >> 7
    scalar_lines = pltpu.make_async_copy(lines, voxel, isem.at[tiles + 2])
    scalar_lines.start()

    @pl.loop(-1, cx + 1)
    def _(x):
        for c in range(tiles):
            for y in range(0, cy, 8):
                vecs[0, pl.ds(row(x, c, y), 8), :] = zeros8

    @pl.loop(0, cycles)
    def _(j):
        @pl.loop(0, cx + 1)
        def _(x):
            for c in range(tiles):
                vecs[2 * j + 1, pl.ds(row(x, c, -PAD), 8), :] = zeros8

    hodd[...] = jnp.zeros(hodd.shape, F32)
    for beyond, x in ((gx == 0, -1), (gx == n_gx - 1, cx)):
        @pl.when(beyond)
        def _():
            for c in range(tiles):
                for y in range(0, cy, 8):
                    inv[pl.ds(inv_row(x, c, y), 8), :] = zeros8

            @pl.loop(0, cycles)
            def _(j):
                for c in range(tiles):
                    first = row(-2 if x < 0 else cx, c, 0)
                    for y in range(0, pitch + cy, 8):
                        vecs[2 * j + 1, pl.ds(first + y, 8), :] = zeros8
                    for side in range(2):
                        hin[j, c, side, pl.ds(low_corner if x < 0 else high_corner, 1), :] = zero_row

    for beyond, side in ((gy == 0, 0), (gy == n_gy - 1, 1)):
        @pl.when(beyond)
        def _():
            hinv[side] = jnp.zeros(hinv.shape[1:], F32)

            @pl.loop(0, cycles)
            def _(j):
                for c in range(tiles):
                    hin[j, c, side] = jnp.zeros(hin.shape[3:], F32)

    def build_masks():
        @pl.loop(0, n_gy)
        def _(peer):
            live = count[peer]
            lanes = lax.broadcasted_iota(jnp.int32, (128, 128), 1)
            rows = lax.broadcasted_iota(jnp.int32, (128, 128), 0)
            for part in range(wide):
                at = (places[pl.ds(peer * wide + part, 1), :] & 127).astype(F32)
                at = jnp.broadcast_to(at, (128, 128)).T
                mask[peer * wide + part] = jnp.where(
                    (lanes.astype(F32) == at) & (rows + 128 * part < live), 0.5, 0.0
                )

    lane8 = lax.broadcasted_iota(jnp.int32, (8, 128), 1)
    sub8 = lax.broadcasted_iota(jnp.int32, (8, 128), 0)
    first_lane, last_lane = lane8 == 0, lane8 == 127

    def beside(v, before, after):
        z = pltpu.roll(jnp.where(last_lane, before, v), 1, 1)
        return z + pltpu.roll(jnp.where(first_lane, after, v), 127, 1)

    def sweep(k, c, runs, scale, carry=None, more=lambda: ()):
        centers = {}

        def center(start, o, y):
            at = (start if isinstance(start, int) else None, o, y)
            if at not in centers:
                centers[at] = vecs[k, pl.ds(row(start + o, c, y), 8), :]
            return centers[at]

        found = []
        for start, offsets in runs:
            for y in range(0, cy, 8):
                for o in offsets:
                    r = row(start + o, c, y)
                    v = center(start, o, y)
                    before = vecs[k, pl.ds(r - block, 8), :] if c > 0 else 0.0
                    after = vecs[k, pl.ds(r + block, 8), :] if c < tiles - 1 else 0.0
                    n = vecs[k, pl.ds(r - 1, 8), :] + vecs[k, pl.ds(r + 1, 8), :]
                    n = n + (center(start, o - 1, y) + center(start, o + 1, y))
                    n = n + beside(v, before, after)
                    i = inv[pl.ds(inv_row(start + o, c, y), 8), :]
                    new = (scale * i) * n - vecs[k - 1, pl.ds(r, 8), :]
                    if carry is not None:
                        w = diag[pl.ds(flat_row(start + o, c, y), 8), :] * v
                        carry = (carry[0] + w * v, carry[1] + w * new)
                    found.append((r, new))
        others = more()
        for r, new in found:
            vecs[k + 1, pl.ds(r, 8), :] = new
        for store in others:
            store()
        return carry

    def inner(k, c, first, last, scale, carry):
        group = max(g for g in range(1, 8) if (last - first) % g == 0)

        def some(i, a):
            return sweep(k, c, [(group * i + first, range(group))], scale, a)

        return lax.fori_loop(0, (last - first) // group, some, carry)

    def border(j, c, scale, carry):
        k = 2 * j + 1
        carry = sweep(k, c, [(0, (0,)), (cx - 1, (0,))], scale, carry)
        own, cross = carry
        found = []
        for side, y, _ in sides:
            for x in range(0, cx, 8):
                at = pl.ds(near + x, 8)
                h = hin[j, c, side, at, :]
                line = pl.ds(row(x, c, y), 8, stride=pitch)
                fixed = vecs[k + 1, line, :] + (scale * pinv[side, c, pl.ds(x, 8), :]) * h
                cross = cross + (scale * ybuf[j, c, side, at, :]) * h
                found.append((line, fixed))
        for line, fixed in found:
            vecs[k + 1, line, :] = fixed
        return own, cross

    def shell(j, c, scale):
        k = 2 * j + 1
        for side, y in ((0, -1), (1, cy)):
            for x, at in ((-1, low_corner), (cx, high_corner)):
                vecs[k, pl.ds(row(x, c, y), 1), :] = hin[j, c, side, pl.ds(at, 1), :]

        def rows_beyond():
            stores = []
            for side, beyond in ((0, -1), (1, cy)):
                for x in range(0, cx, 8):
                    at = pl.ds(near + x, 8)
                    h = hin[j, c, side, at, :]
                    before = hin[j, c - 1, side, at, :] if c > 0 else 0.0
                    after = hin[j, c + 1, side, at, :] if c < tiles - 1 else 0.0
                    lower = hin[j, c, side, pl.ds(near + x - 1, 8), :]
                    if x == 0:
                        corner = hin[j, c, side, pl.ds(low_corner, 1), :]
                        lower = jnp.where(sub8 == 0, corner, lower)
                    upper = hin[j, c, side, pl.ds(near + x + 1, 8), :]
                    n = (lower + upper) + (hin[j, c, side, pl.ds(x, 8), :] + ybuf[j, c, side, at, :])
                    n = n + beside(h, before, after)
                    old = pl.ds(x, 8)
                    new = (scale * hinv[side, c, old, :]) * n - hodd[side, c, old, :]

                    def store(side=side, old=old, new=new, line=row(x, c, beyond)):
                        hodd[side, c, old, :] = new
                        vecs[k + 1, pl.ds(line, 8, stride=pitch), :] = new

                    stores.append(store)
            return stores

        sweep(k, c, [(-1, (0,)), (cx, (0,))], scale, None, rows_beyond)

    def finish(j, c, carry):
        k = 2 * j + 2
        more = j < cycles - 1
        carry = sweep(k, c, [(0, (0, 1)), (cx - 2, (0, 1))], 2.0, carry)
        launch_x(j + 1, c, more)
        carry = inner(k, c, 2, cx - 2, 2.0, carry)

        @pl.when(more)
        def _():
            pack_rows(j + 1, c)
            launch_y(j + 1, c, always)

        return carry

    @pl.loop(0, cycles)
    def _(j):
        with jax.named_scope("cycle"):
            scale = jnp.where(j == 0, 1.0, 2.0).astype(F32)
            first = second = (zeros8, zeros8)
            with jax.named_scope("ainner"):
                for c in range(tiles):
                    first = inner(2 * j + 1, c, 1, cx - 1, scale, first)

            @pl.when(j == 0)
            def _():
                taken(vrecv.at[tiles], lambda a, b: b * tiles * cx)

            for c in range(tiles):
                for d in (0, 1) if c == 0 else (c + 1,):
                    if d < tiles:
                        with jax.named_scope("landed"):
                            landed_near(j, d)
                        first = border(j, d, scale, first)
                with jax.named_scope("landed"):
                    landed_far(j, c)
                shell(j, c, scale)
                second = finish(j, c, second)
            for i, value in enumerate((*first, *second)):
                dots[pl.ds(pl.multiple_of(32 * j + 8 * i, 8), 8), :] = value

    scalar_lines.wait()

    with jax.named_scope("reduce"):
        sums = []
        for g in range(2 * s // 8):
            level = [dots[pl.ds(64 * g + i, 8, stride=8), :] for i in range(8)]
            level = [two_sum(level[2 * i], level[2 * i + 1]) for i in range(4)]
            while len(level) > 1:
                level = [dd_add(level[2 * i], level[2 * i + 1]) for i in range(len(level) // 2)]
            sums.append(level[0])
        for shift in (64, 32, 16, 8, 4, 2, 1):
            sums = [
                dd_add(a, tuple(pltpu.roll(p, shift, 1) for p in a)) for a in sums
            ]
        spread = zeros8
        for g, (hi, lo) in enumerate(sums):
            spread = jnp.where(lane8 == sub8 + 8 * g, hi, spread)
            spread = jnp.where(lane8 == sub8 + 8 * g + LOW, lo, spread)
        line = jnp.sum(spread, axis=0, keepdims=True)
        mine[...] = line
        parts[pl.ds(me, 1), :] = line

        everyone(
            lambda to_gx, to_gy: pltpu.make_async_remote_copy(
                src_ref=mine, dst_ref=parts.at[pl.ds(me, 1), :],
                send_sem=rsend, recv_sem=rrecv,
                device_id=(to_gx, to_gy), device_id_type=mesh_id,
            ).start()
        )

        build_masks()
        for way, there in ((0, has_up), (1, has_down)):
            @pl.when(there)
            def _():
                drained(cycles * tiles * 2 * cy, xsend.at[way])
                drained(tiles * cy, vsend.at[way])
                for q, also in ((0, has_right), (1, has_left)):
                    @pl.when(also)
                    def _():
                        drained(cycles * tiles, csend.at[2 * way + q])

        for way, there in ((0, has_right), (1, has_left)):
            @pl.when(there)
            def _():
                drained(cycles * tiles * 2 * cx, ysend.at[way])
                drained(tiles * cx, vsend.at[2 + way])

        drained(total - 1, rrecv)

    with jax.named_scope("solve"):
        level = [parts[8 * i : 8 * i + 8, :] for i in range(total // 8)]
        level = [(a, pltpu.roll(a, 128 - LOW, 1)) for a in level]
        while len(level) > 1:
            level = [dd_add(level[2 * i], level[2 * i + 1]) for i in range(len(level) // 2)]
        every = level[0]
        for shift in (4, 2, 1):
            every = dd_add(every, tuple(pltpu.roll(p, shift, 0) for p in every))
        terms = []
        for m in range(2 * s):
            hi, lo = (jnp.broadcast_to(p[0:1, m : m + 1], (ROWS, 128)) for p in every)
            terms.append((table[m] * hi, table[m] * lo))
        while len(terms) > 1:
            terms = [
                dd_add(terms[i], terms[i + 1]) if i + 1 < len(terms) else terms[i]
                for i in range(0, len(terms), 2)
            ]
        weights = dd_solve(terms[0])

    with jax.named_scope("combine"):
        @pl.loop(0, cx)
        def _(x):
            for c in range(tiles):
                for y in range(0, cy, 8):
                    pieces = [
                        w * vecs[1 + k, pl.ds(row(x, c, y), 8), :] for k, w in enumerate(weights)
                    ]
                    while len(pieces) > 1:
                        pieces = [sum(pieces[i : i + 2]) for i in range(0, len(pieces), 2)]
                    out[x, y : y + 8, 128 * c : 128 * (c + 1)] = pieces[0]
                    f = pl.ds(flat_row(x, c, y), 8)
                    at = (x * cy + y) * tiles + c
                    flat[pl.ds(at, 8, stride=tiles), :] = base[f, :] + slope[f, :] * pieces[0]

    picks = (pick0, pick1)

    def fetch(peer, pick):
        for part in range(wide):
            for i in range(128):
                pick[pl.ds(128 * part + i, 1), :] = flat[pl.ds(voxel[peer * wide + part, i], 1), :]

    def pass_on(peer, pick):
        for part in range(wide):
            value = pick[128 * part : 128 * (part + 1), :] * mask[peer * wide + part]
            sent[peer, pl.ds(part, 1), :] = jnp.sum(value.T, axis=0, keepdims=True)

    def give(peer):
        pltpu.make_async_remote_copy(
            src_ref=sent.at[peer], dst_ref=got.at[gy], send_sem=lsend, recv_sem=lrecv.at[gy],
            device_id=(gx, peer), device_id_type=mesh_id,
        ).start()

    def peer_at(step):
        return flipped(gy, n_gy - 1 - step, n_gy)

    with jax.named_scope("gather"):
        fetch(peer_at(0), picks[0])

        @pl.loop(0, n_gy // 2 - 1)
        def _(i):
            pass_on(peer_at(2 * i), picks[0])
            fetch(peer_at(2 * i + 1), picks[1])
            give(peer_at(2 * i))
            pass_on(peer_at(2 * i + 1), picks[1])
            fetch(peer_at(2 * i + 2), picks[0])
            give(peer_at(2 * i + 1))

        pass_on(peer_at(n_gy - 2), picks[0])
        fetch(gy, picks[1])
        give(peer_at(n_gy - 2))
        pass_on(gy, picks[1])
        got[gy] = sent[gy]

    own = tally.shape[0]

    def tallied(peer, first):
        spots = [target[pl.ds(peer * wide + part, 1), :] for part in range(wide)]
        values = [got[peer, part : part + 1, :] for part in range(wide)]
        for start in range(0, own, 128):
            found = []
            for r in range(start, start + 128, 8):
                total_ = zeros8 if first else tally[r : r + 8, :]
                for spot, value in zip(spots, values):
                    total_ = total_ + jnp.where(spot == sub8 + r, value, 0.0)
                found.append((r, total_))
            for r, total_ in found:
                tally[r : r + 8, :] = total_

    with jax.named_scope("links"):
        tallied(gy, True)
        drained(total - 1, rsend)

        @pl.loop(0, n_gy - 1)
        def _(step):
            peer = flipped(gy, n_gy - 1 - step, n_gy)
            pltpu.make_async_copy(got.at[peer], got.at[peer], lrecv.at[peer]).wait()
            tallied(peer, False)

        for start in range(0, own, 128):
            particle[0, :, start : start + 128] = jnp.sum(
                tally[start : start + 128, :].T, axis=0, keepdims=True
            )
        drained((n_gy - 1) * wide, lsend)


def kept(x):
    return pltpu.with_memory_space_constraint(x, pltpu.HBM)


def shards(sizes, source, voxel_phase, lin_potential, link_voxel, link_count, link_target):
    cx, cy, cz = source.shape
    total = sizes[0] * sizes[1]
    s = ITERS
    tiles = cz // 128
    voxels = cx * cy * tiles
    padded = (cx + 4) * tiles * (cy + PAD) + 8
    cycles = s // 2
    places = link_voxel[0, 0].reshape(-1, 128)
    peers = link_count.shape[2]
    slots = link_voxel.shape[2]
    groups = slots // 128
    whole = pl.BlockSpec(memory_space=pltpu.VMEM)
    far = pl.BlockSpec(memory_space=pltpu.HBM)
    found, sums = pl.pallas_call(
        functools.partial(kernel, sizes),
        out_shape=(
            jax.ShapeDtypeStruct(source.shape, F32),
            jax.ShapeDtypeStruct((1, 1, PART_DEV), F32),
        ),
        in_specs=[far] * 7,
        out_specs=(whole, whole),
        scratch_shapes=[
            pltpu.VMEM((tiles, cx, cy, 128), F32),
            pltpu.VMEM((tiles, cx, cy, 128), jnp.int32),
            pltpu.VMEM((tiles, cx, cy, 128), F32),
            pltpu.VMEM((2 * s, ROWS, 128), F32),
            pltpu.VMEM((groups, 128), jnp.int32),
            pltpu.SMEM((groups, 128), jnp.int32),
            pltpu.VMEM((groups, 128), jnp.int32),
            pltpu.SMEM((peers,), jnp.int32),
            pltpu.VMEM((groups, 128), jnp.int32),
            pltpu.VMEM((s + 2, padded, 128), F32),
            pltpu.VMEM((voxels, 128), F32),
            pltpu.VMEM((tiles * (cx + 2) * cy, 128), F32),
            pltpu.VMEM((voxels, 128), F32),
            pltpu.VMEM((voxels, 128), F32),
            pltpu.VMEM((cycles, tiles, 2, 2 * cx, 128), F32),
            pltpu.VMEM((cycles, tiles, 2, 2 * cx + 8, 128), F32),
            pltpu.VMEM((2, tiles, cx, 128), F32),
            pltpu.VMEM((2, tiles, cx, 128), F32),
            pltpu.VMEM((2, tiles, cx, 128), F32),
            pltpu.VMEM((groups, 128, 128), F32),
            pltpu.VMEM((2 * s * 8, 128), F32),
            pltpu.VMEM((1, 128), F32),
            pltpu.VMEM((total, 128), F32),
            pltpu.VMEM((groups // peers * 128, 128), F32),
            pltpu.VMEM((groups // peers * 128, 128), F32),
            pltpu.VMEM((voxels, 128), F32),
            pltpu.VMEM((peers, groups // peers, 128), F32),
            pltpu.VMEM((peers, groups // peers, 128), F32),
            pltpu.VMEM((PART_DEV, 128), F32),
            pltpu.SemaphoreType.DMA((tiles + 3,)),
            pltpu.SemaphoreType.DMA((2,)),
            pltpu.SemaphoreType.DMA((2,)),
            pltpu.SemaphoreType.DMA((4,)),
            pltpu.SemaphoreType.DMA((2, tiles, 2)),
            pltpu.SemaphoreType.DMA((4,)),
            pltpu.SemaphoreType.DMA((tiles + 1,)),
            pltpu.SemaphoreType.DMA,
            pltpu.SemaphoreType.DMA,
            pltpu.SemaphoreType.DMA,
            pltpu.SemaphoreType.DMA((peers,)),
        ],
        compiler_params=pltpu.CompilerParams(
            collective_id=0, has_side_effects=True, vmem_limit_bytes=52 * 2**20
        ),
    )(
        kept(source), kept(voxel_phase), kept(lin_potential), kept(jnp.asarray(gram_map())),
        kept(places), kept(link_count[0, 0]), kept(link_target[0, 0].reshape(groups, 128)),
    )
    return pl.pallas_call(
        last_kernel,
        out_shape=(
            jax.ShapeDtypeStruct(source.shape, F32),
            jax.ShapeDtypeStruct((1, 1, PART_DEV), F32),
        ),
        in_specs=[pl.BlockSpec(memory_space=pl.ANY)] * 2,
        out_specs=(far, far),
        scratch_shapes=[pltpu.SemaphoreType.DMA((2,))],
        compiler_params=pltpu.CompilerParams(vmem_limit_bytes=2 * 2**20),
    )(found, sums)


def solution(mesh):
    spec = P("gx", "gy", None)
    return jax.shard_map(
        functools.partial(shards, (mesh.shape["gx"], mesh.shape["gy"])),
        mesh=mesh,
        in_specs=(spec,) * 6,
        out_specs=(spec, spec),
        check_vma=False,
    )
```

```python
import functools

import jax
import jax.numpy as jnp
import numpy as np
from jax import lax
from jax.experimental import pallas as pl
from jax.experimental.pallas import tpu as pltpu
from jax.sharding import PartitionSpec as P

ITERS = 12
PART_DEV = 512
ROWS = 16
RHS = 15
LATE = 4
PAD = 8
LOW = 64
F32 = jnp.float32


def gram_map():
    s = ITERS
    n = 2 * s

    def unit(at):
        out = np.zeros(n)
        out[at] = 1.0
        return out

    m = []
    for k in range(s):
        m.append(2 * unit(2 * k) - unit(0))
        m.append(2 * unit(2 * k + 1) - unit(1))

    def entry(j, k):
        a, b = j + k, abs(j - k)
        return 0.5 * (
            m[a] - 0.5 * (m[a + 1] + m[abs(a - 1)]) + m[b] - 0.5 * (m[b + 1] + m[abs(b - 1)])
        )

    table = np.zeros((n, ROWS, 128))
    for j in range(s):
        table[:, j, RHS] = m[j]
        for k in range(s):
            table[:, j, k] = entry(j, k)
    extra = np.zeros((ROWS, 128))
    for i, m in enumerate(range(n - LATE, n)):
        extra[:, RHS + 1 + 2 * i : RHS + 3 + 2 * i] = table[m][:, s - 2 : s]
    return np.concatenate([table, extra[None]]).astype(np.float32)


def two_sum(a, b):
    s = a + b
    t = s - a
    return s, (a - (s - t)) + (b - t)


def quick_two_sum(a, b):
    s = a + b
    return s, b - (s - a)


def split(a):
    c = 4097.0 * a
    hi = c - (c - a)
    return hi, a - hi


def two_prod(a, b):
    p = a * b
    ah, al = split(a)
    bh, bl = split(b)
    return p, ((ah * bh - p) + ah * bl + al * bh) + al * bl


def dd_add(a, b):
    s, e = two_sum(a[0], b[0])
    return quick_two_sum(s, e + (a[1] + b[1]))


def dd_mul(a, b):
    p, e = two_prod(a[0], b[0])
    return quick_two_sum(p, e + (a[0] * b[1] + a[1] * b[0]))


def dd_inverse(a):
    x = 1.0 / a[0]
    p, e = two_prod(a[0], x)
    r = (1.0 - p) - e - a[1] * x
    return quick_two_sum(x, x * r)


def dd_minus(a, b):
    return dd_add(a, (-b[0], -b[1]))


def dd_sum(terms):
    while len(terms) > 1:
        terms = [
            dd_add(terms[i], terms[i + 1]) if i + 1 < len(terms) else terms[i]
            for i in range(0, len(terms), 2)
        ]
    return terms[0]


def lane_column(matrix, j):
    return tuple(jnp.broadcast_to(m[:, j : j + 1], m.shape) for m in matrix)


def full_row(matrix, j, rows=ROWS):
    return tuple(jnp.broadcast_to(m[j : j + 1, :], (rows, 128)) for m in matrix)


def weighted(table, every, numbers):
    terms = []
    for m in numbers:
        hi, lo = (jnp.broadcast_to(p[0:1, m : m + 1], (ROWS, 128)) for p in every)
        terms.append((table[m] * hi, table[m] * lo))
    return terms


def dd_eliminate(matrix, count):
    rows = lax.broadcasted_iota(jnp.int32, (ROWS, 128), 0)

    def eliminate(a, j, by, inverse):
        scaled = dd_mul(full_row(a, j), inverse)
        less = dd_minus(a, dd_mul(by, scaled))
        return tuple(jnp.where(rows == j, r, m) for r, m in zip(scaled, less))

    for j in range(0, count, 2):
        one, two = lane_column(matrix, j), lane_column(matrix, j + 1)
        inverse = dd_inverse(full_row(one, j))
        two = eliminate(two, j, one, inverse)
        matrix = eliminate(matrix, j, one, inverse)
        matrix = eliminate(matrix, j + 1, two, dd_inverse(full_row(two, j + 1)))
    return matrix


def dd_finish(table, early, reduced, every):
    u = ITERS - 2
    rows = lax.broadcasted_iota(jnp.int32, (ROWS, 128), 0)
    lanes = lax.broadcasted_iota(jnp.int32, (ROWS, 128), 1)
    last_two = (lanes == u) | (lanes == u + 1)
    late = range(2 * ITERS - LATE, 2 * ITERS)
    matrix = dd_sum([early] + weighted(table, every, late))
    terms = [reduced]
    for i, m in enumerate(late):
        value = tuple(
            jnp.where(last_two, jnp.broadcast_to(p[0:1, m : m + 1], (ROWS, 128)), 0.0) for p in every
        )
        moved = tuple(pltpu.roll(p, 128 - (RHS + 1 + 2 * i - u), 1) for p in reduced)
        terms.append(dd_mul(value, moved))
    x = dd_sum(terms)
    schur = []
    for a in range(2):
        product = dd_mul(lane_column(matrix, u + a), x)
        product = tuple(jnp.where(rows < u, p, 0.0) for p in product)
        total = dd_add(tuple(p[0:8, :] for p in product), tuple(p[8:16, :] for p in product))
        for shift in (4, 2, 1):
            total = dd_add(total, tuple(pltpu.roll(p, shift, 0) for p in total))
        schur.append(dd_minus(full_row(matrix, u + a, 8), total))
    (s00, s01, r0), (s10, s11, r1) = (
        [lane_column(row, j) for j in (u, u + 1, RHS)] for row in schur
    )
    over = dd_inverse(dd_minus(dd_mul(s00, s11), dd_mul(s01, s10)))
    c0 = dd_mul(dd_minus(dd_mul(r0, s11), dd_mul(r1, s01)), over)
    c1 = dd_mul(dd_minus(dd_mul(r1, s00), dd_mul(r0, s10)), over)
    rest = dd_minus(
        dd_minus(lane_column(x, RHS), dd_mul(lane_column(x, u), full_row(c0, 0))),
        dd_mul(lane_column(x, u + 1), full_row(c1, 0)),
    )
    return [full_row(rest, j, 8)[0] for j in range(u)] + [c0[0], c1[0]]


def partners(index, size):
    if size & (size - 1):
        return [lax.rem(index + m, size) for m in range(size)]
    out = [0]
    bit = 1
    while bit < size:
        same = lax.rem(index // bit, 2) * bit
        out = [o + same for o in out] + [o + (bit - same) for o in out]
        bit *= 2
    return out


def flipped(index, m, size):
    if size & (size - 1):
        return lax.rem(index + m, size)
    out, bit = 0, 1
    while bit < size:
        out = out + lax.rem(index // bit + m // bit, 2) * bit
        bit *= 2
    return out


def last_kernel(found, sums, out, particle, sems):
    pieces = [
        pltpu.make_async_copy(found, out, sems.at[0]),
        pltpu.make_async_copy(sums, particle, sems.at[1]),
    ]
    for copy in pieces:
        copy.start()
    for copy in pieces:
        copy.wait()


def kernel(
    sizes, source_hbm, phase_hbm, potential_hbm, map_hbm, places_hbm, count_hbm, target_hbm,
    out, particle,
    source, phase, potential, table, lines, voxel, places, count, target, vecs, diag, inv, base, slope, ybuf, hin,
    pinv, hinv, hodd, mask, dots, mine, parts, pick0, pick1, flat, sent, got, tally,
    isem, xsend, ysend, csend, hrecv, vsend, vrecv, rsend, rrecv, lsend, lrecv,
):
    n_gx, n_gy = sizes
    total = n_gx * n_gy
    cx, cy, cz = source_hbm.shape
    tiles = cz // 128
    pitch = cy + PAD
    block = (cx + 4) * pitch
    s = ITERS
    cycles = s // 2
    gx, gy = lax.axis_index("gx"), lax.axis_index("gy")
    me = gx * n_gy + gy
    mesh_id = pl.DeviceIdType.MESH

    barrier = pltpu.get_barrier_semaphore()

    gy_of = partners(gy, n_gy)
    gx_of = partners(gx, n_gx)

    def everyone(act):
        for m in reversed(range(n_gy)):
            for q in reversed(range(n_gx)):
                if m or q:
                    act(gx_of[q], gy_of[m])


    loads = []
    for c in range(tiles):
        for src, dst in (
            (potential_hbm, potential), (phase_hbm, phase), (source_hbm, source)
        ):
            loads.append(
                pltpu.make_async_copy(
                    src.at[:, :, pl.ds(128 * c, 128)], dst.at[c], isem.at[c]
                )
            )
    extra = [
        pltpu.make_async_copy(map_hbm, table, isem.at[tiles]),
        pltpu.make_async_copy(places_hbm, places, isem.at[tiles]),
        pltpu.make_async_copy(count_hbm, count, isem.at[tiles + 1]),
        pltpu.make_async_copy(target_hbm, target, isem.at[tiles]),
    ]
    for copy in loads[:3]:
        copy.start()
    everyone(
        lambda to_gx, to_gy: pl.semaphore_signal(
            barrier, inc=1, device_id=(to_gx, to_gy), device_id_type=mesh_id
        )
    )
    for copy in loads[3:] + extra:
        copy.start()

    has_up, has_down = gx < n_gx - 1, gx > 0
    has_right, has_left = gy < n_gy - 1, gy > 0
    up_gx, down_gx = jnp.minimum(gx + 1, n_gx - 1), jnp.maximum(gx - 1, 0)
    right_gy, left_gy = jnp.minimum(gy + 1, n_gy - 1), jnp.maximum(gy - 1, 0)

    def row(x, c, y):
        return c * block + (x + 2) * pitch + PAD + y

    def inv_row(x, c, y):
        return (c * (cx + 2) + x + 1) * cy + y

    def flat_row(x, c, y):
        return (c * cx + x) * cy + y

    def drained(rows, sem):
        ref = vecs.at[0, pl.ds(0, rows), :]
        pltpu.make_async_copy(ref, ref, sem).wait()

    def counts(one, other, size):
        if size < 3:
            return [(size - 1, None)]
        both = one & other
        return [(1, jnp.logical_not(both)), (2, both)]

    x_counts = counts(has_up, has_down, n_gx)
    y_counts = counts(has_right, has_left, n_gy)

    def taken(sem, rows):
        for a, so_many_x in x_counts:
            for b, so_many_y in y_counts:
                if not rows(a, b):
                    continue
                there = [t for t in (so_many_x, so_many_y) if t is not None]
                if there:
                    pl.when(functools.reduce(jnp.logical_and, there))(
                        functools.partial(drained, rows(a, b), sem)
                    )
                else:
                    drained(rows(a, b), sem)

    near, low_corner, high_corner = cx, 2 * cx + 1, 2 * cx
    zeros8 = jnp.zeros((8, 128), F32)
    zero_row = jnp.zeros((1, 128), F32)

    sides = ((0, 0, 1), (1, cy - 1, cy - 2))

    def pack_rows(j, c):
        k = 2 * j + 1
        for side, y1, y2 in sides:
            for x in range(0, cx, 8):
                ybuf[j, c, side, pl.ds(near + x, 8), :] = (
                    vecs[k, pl.ds(row(x, c, y1), 8, stride=pitch), :]
                )
                ybuf[j, c, side, pl.ds(x, 8), :] = vecs[k, pl.ds(row(x, c, y2), 8, stride=pitch), :]

    def xcopy(j, c, way, layer):
        up = way == 0
        return pltpu.make_async_remote_copy(
            src_ref=vecs.at[2 * j + 1, pl.ds(row(cx - 1 - layer if up else layer, c, 0), cy), :],
            dst_ref=vecs.at[2 * j + 1, pl.ds(row(-1 - layer if up else cx + layer, c, 0), cy), :],
            send_sem=xsend.at[way], recv_sem=hrecv.at[lax.rem(j, 2), c, layer],
            device_id=(up_gx if up else down_gx, gy), device_id_type=mesh_id,
        )

    def ycopy(j, c, way):
        right = way == 0
        return pltpu.make_async_remote_copy(
            src_ref=ybuf.at[j, c, 1 if right else 0],
            dst_ref=hin.at[j, c, 0 if right else 1, pl.ds(0, 2 * cx), :],
            send_sem=ysend.at[way], recv_sem=hrecv.at[lax.rem(j, 2), c, 0],
            device_id=(gx, right_gy if right else left_gy), device_id_type=mesh_id,
        )

    def ccopy(j, c, xway, yway):
        up, right = xway == 0, yway == 0
        q = 2 * xway + yway
        return pltpu.make_async_remote_copy(
            src_ref=vecs.at[
                2 * j + 1, pl.ds(row(cx - 1 if up else 0, c, cy - 1 if right else 0), 1), :
            ],
            dst_ref=hin.at[j, c, 0 if right else 1, pl.ds(low_corner if up else high_corner, 1), :],
            send_sem=csend.at[q], recv_sem=hrecv.at[lax.rem(j, 2), c, 1],
            device_id=(up_gx if up else down_gx, right_gy if right else left_gy),
            device_id_type=mesh_id,
        )

    def vcopy(c, way):
        up = way == 0
        return pltpu.make_async_remote_copy(
            src_ref=inv.at[pl.ds(inv_row(cx - 1 if up else 0, c, 0), cy), :],
            dst_ref=inv.at[pl.ds(inv_row(-1 if up else cx, c, 0), cy), :],
            send_sem=vsend.at[way], recv_sem=vrecv.at[c],
            device_id=(up_gx if up else down_gx, gy), device_id_type=mesh_id,
        )

    def hcopy(way):
        right = way == 0
        return pltpu.make_async_remote_copy(
            src_ref=pinv.at[1 if right else 0], dst_ref=hinv.at[0 if right else 1],
            send_sem=vsend.at[2 + way], recv_sem=vrecv.at[tiles],
            device_id=(gx, right_gy if right else left_gy), device_id_type=mesh_id,
        )

    for c in range(tiles):
        drained(3 * cx * cy, isem.at[c])

        @pl.loop(0, cx)
        def _(x):
            found = []
            for y in range(0, cy, 8):
                at = potential[c, x, y : y + 8, :]
                rising = jnp.exp(0.4 * at)
                falling = jnp.exp(-0.6 * at)
                label = phase[c, x, y : y + 8, :]
                rate = jnp.where(label == 1, 0.3, jnp.where(label == 2, 0.08, 0.02)).astype(F32)
                bend = 0.4 * rising + 0.6 * falling
                d = 6.0 + rate * bend
                i = 1.0 / d
                found.append((y, rising - falling, bend, d, i, source[c, x, y : y + 8, :] * i))
            for y, level, bend, d, i, v in found:
                f = pl.ds(flat_row(x, c, y), 8)
                base[f, :] = level
                slope[f, :] = bend
                diag[f, :] = d
                inv[pl.ds(inv_row(x, c, y), 8), :] = i
                vecs[1, pl.ds(row(x, c, y), 8), :] = v

        pack_rows(0, c)
        for side, y, _ in sides:
            for x in range(0, cx, 8):
                pinv[side, c, pl.ds(x, 8), :] = inv[pl.ds(inv_row(x, c, y), 8, stride=cy), :]

    def launch_x(j, c, more):
        for way, there in ((0, has_up), (1, has_down)):
            @pl.when(there & more)
            def _():
                pl.when(has_right)(ccopy(j, c, way, 0).start)
                pl.when(has_left)(ccopy(j, c, way, 1).start)
                xcopy(j, c, way, 0).start()
                xcopy(j, c, way, 1).start()

    def launch_y(j, c, more):
        pl.when(has_right & more)(ycopy(j, c, 0).start)
        pl.when(has_left & more)(ycopy(j, c, 1).start)

    def landed_near(j, c):
        taken(hrecv.at[lax.rem(j, 2), c, 0], lambda a, b: a * cy + b * 2 * cx)

    def landed_far(j, c):
        taken(hrecv.at[lax.rem(j, 2), c, 1], lambda a, b: a * (cy + b))

        @pl.when(j == 0)
        def _():
            taken(vrecv.at[c], lambda a, b: a * cy)

    with jax.named_scope("barrier"):
        pl.semaphore_wait(barrier, total - 1)

    always = gx >= 0
    pl.when(has_right)(hcopy(0).start)
    pl.when(has_left)(hcopy(1).start)
    for c in range(tiles):
        launch_x(0, c, always)
        launch_y(0, c, always)
        pl.when(has_up)(vcopy(c, 0).start)
        pl.when(has_down)(vcopy(c, 1).start)

    groups = places.shape[0]
    wide = groups // n_gy
    drained(table.shape[0] * ROWS + 2 * groups, isem.at[tiles])
    pltpu.make_async_copy(count_hbm, count, isem.at[tiles + 1]).wait()
    lines[...] = places[...] >> 7
    scalar_lines = pltpu.make_async_copy(lines, voxel, isem.at[tiles + 2])
    scalar_lines.start()

    @pl.loop(-1, cx + 1)
    def _(x):
        for c in range(tiles):
            for y in range(0, cy, 8):
                vecs[0, pl.ds(row(x, c, y), 8), :] = zeros8

    @pl.loop(0, cycles)
    def _(j):
        @pl.loop(0, cx + 1)
        def _(x):
            for c in range(tiles):
                vecs[2 * j + 1, pl.ds(row(x, c, -PAD), 8), :] = zeros8

    hodd[...] = jnp.zeros(hodd.shape, F32)
    for beyond, x in ((gx == 0, -1), (gx == n_gx - 1, cx)):
        @pl.when(beyond)
        def _():
            for c in range(tiles):
                for y in range(0, cy, 8):
                    inv[pl.ds(inv_row(x, c, y), 8), :] = zeros8

            @pl.loop(0, cycles)
            def _(j):
                for c in range(tiles):
                    first = row(-2 if x < 0 else cx, c, 0)
                    for y in range(0, pitch + cy, 8):
                        vecs[2 * j + 1, pl.ds(first + y, 8), :] = zeros8
                    for side in range(2):
                        hin[j, c, side, pl.ds(low_corner if x < 0 else high_corner, 1), :] = zero_row

    for beyond, side in ((gy == 0, 0), (gy == n_gy - 1, 1)):
        @pl.when(beyond)
        def _():
            hinv[side] = jnp.zeros(hinv.shape[1:], F32)

            @pl.loop(0, cycles)
            def _(j):
                for c in range(tiles):
                    hin[j, c, side] = jnp.zeros(hin.shape[3:], F32)

    def build_masks():
        @pl.loop(0, n_gy)
        def _(peer):
            live = count[peer]
            lanes = lax.broadcasted_iota(jnp.int32, (128, 128), 1)
            rows = lax.broadcasted_iota(jnp.int32, (128, 128), 0)
            for part in range(wide):
                at = (places[pl.ds(peer * wide + part, 1), :] & 127).astype(F32)
                at = jnp.broadcast_to(at, (128, 128)).T
                mask[peer * wide + part] = jnp.where(
                    (lanes.astype(F32) == at) & (rows + 128 * part < live), 0.5, 0.0
                )

    lane8 = lax.broadcasted_iota(jnp.int32, (8, 128), 1)
    sub8 = lax.broadcasted_iota(jnp.int32, (8, 128), 0)
    first_lane, last_lane = lane8 == 0, lane8 == 127

    def beside(v, before, after):
        z = pltpu.roll(jnp.where(last_lane, before, v), 1, 1)
        return z + pltpu.roll(jnp.where(first_lane, after, v), 127, 1)

    def sweep(k, c, runs, scale, carry=None, more=lambda: ()):
        centers = {}

        def center(start, o, y):
            at = (start if isinstance(start, int) else None, o, y)
            if at not in centers:
                centers[at] = vecs[k, pl.ds(row(start + o, c, y), 8), :]
            return centers[at]

        found = []
        for start, offsets in runs:
            for y in range(0, cy, 8):
                for o in offsets:
                    r = row(start + o, c, y)
                    v = center(start, o, y)
                    before = vecs[k, pl.ds(r - block, 8), :] if c > 0 else 0.0
                    after = vecs[k, pl.ds(r + block, 8), :] if c < tiles - 1 else 0.0
                    n = vecs[k, pl.ds(r - 1, 8), :] + vecs[k, pl.ds(r + 1, 8), :]
                    n = n + (center(start, o - 1, y) + center(start, o + 1, y))
                    n = n + beside(v, before, after)
                    i = inv[pl.ds(inv_row(start + o, c, y), 8), :]
                    new = (scale * i) * n - vecs[k - 1, pl.ds(r, 8), :]
                    if carry is not None:
                        w = diag[pl.ds(flat_row(start + o, c, y), 8), :] * v
                        carry = (carry[0] + w * v, carry[1] + w * new)
                    found.append((r, new))
        others = more()
        for r, new in found:
            vecs[k + 1, pl.ds(r, 8), :] = new
        for store in others:
            store()
        return carry

    def inner(k, c, first, last, scale, carry):
        group = max(g for g in range(1, 8) if (last - first) % g == 0)

        def some(i, a):
            return sweep(k, c, [(group * i + first, range(group))], scale, a)

        return lax.fori_loop(0, (last - first) // group, some, carry)

    def border(j, c, scale, carry):
        k = 2 * j + 1
        carry = sweep(k, c, [(0, (0,)), (cx - 1, (0,))], scale, carry)
        own, cross = carry
        found = []
        for side, y, _ in sides:
            for x in range(0, cx, 8):
                at = pl.ds(near + x, 8)
                h = hin[j, c, side, at, :]
                line = pl.ds(row(x, c, y), 8, stride=pitch)
                fixed = vecs[k + 1, line, :] + (scale * pinv[side, c, pl.ds(x, 8), :]) * h
                cross = cross + (scale * ybuf[j, c, side, at, :]) * h
                found.append((line, fixed))
        for line, fixed in found:
            vecs[k + 1, line, :] = fixed
        return own, cross

    def shell(j, c, scale):
        k = 2 * j + 1
        for side, y in ((0, -1), (1, cy)):
            for x, at in ((-1, low_corner), (cx, high_corner)):
                vecs[k, pl.ds(row(x, c, y), 1), :] = hin[j, c, side, pl.ds(at, 1), :]

        def rows_beyond():
            stores = []
            for side, beyond in ((0, -1), (1, cy)):
                for x in range(0, cx, 8):
                    at = pl.ds(near + x, 8)
                    h = hin[j, c, side, at, :]
                    before = hin[j, c - 1, side, at, :] if c > 0 else 0.0
                    after = hin[j, c + 1, side, at, :] if c < tiles - 1 else 0.0
                    lower = hin[j, c, side, pl.ds(near + x - 1, 8), :]
                    if x == 0:
                        corner = hin[j, c, side, pl.ds(low_corner, 1), :]
                        lower = jnp.where(sub8 == 0, corner, lower)
                    upper = hin[j, c, side, pl.ds(near + x + 1, 8), :]
                    n = (lower + upper) + (hin[j, c, side, pl.ds(x, 8), :] + ybuf[j, c, side, at, :])
                    n = n + beside(h, before, after)
                    old = pl.ds(x, 8)
                    new = (scale * hinv[side, c, old, :]) * n - hodd[side, c, old, :]

                    def store(side=side, old=old, new=new, line=row(x, c, beyond)):
                        hodd[side, c, old, :] = new
                        vecs[k + 1, pl.ds(line, 8, stride=pitch), :] = new

                    stores.append(store)
            return stores

        sweep(k, c, [(-1, (0,)), (cx, (0,))], scale, None, rows_beyond)

    def finish(j, c, carry):
        k = 2 * j + 2
        more = j < cycles - 1
        carry = sweep(k, c, [(0, (0, 1)), (cx - 2, (0, 1))], 2.0, carry)
        launch_x(j + 1, c, more)
        carry = inner(k, c, 2, cx - 2, 2.0, carry)

        @pl.when(more)
        def _():
            pack_rows(j + 1, c)
            launch_y(j + 1, c, always)

        return carry

    def local_sums(numbers):
        sums = []
        for g in numbers:
            level = [dots[pl.ds(64 * g + i, 8, stride=8), :] for i in range(8)]
            level = [two_sum(level[2 * i], level[2 * i + 1]) for i in range(4)]
            sums.append(dd_sum(level))
        for shift in (64, 32, 16, 8, 4, 2, 1):
            sums = [
                dd_add(a, tuple(pltpu.roll(p, shift, 1) for p in a)) for a in sums
            ]
        spread = zeros8
        for g, (hi, lo) in zip(numbers, sums):
            spread = jnp.where(lane8 == sub8 + 8 * g, hi, spread)
            spread = jnp.where(lane8 == sub8 + 8 * g + LOW, lo, spread)
        return jnp.sum(spread, axis=0, keepdims=True)

    def share(which, line):
        mine[which] = line
        parts[which, pl.ds(me, 1), :] = line
        everyone(
            lambda to_gx, to_gy: pltpu.make_async_remote_copy(
                src_ref=mine.at[which], dst_ref=parts.at[which, pl.ds(me, 1), :],
                send_sem=rsend, recv_sem=rrecv.at[which],
                device_id=(to_gx, to_gy), device_id_type=mesh_id,
            ).start()
        )

    def shared(which):
        drained(total - 1, rrecv.at[which])
        level = [parts[which, 8 * i : 8 * i + 8, :] for i in range(total // 8)]
        every = dd_sum([(a, pltpu.roll(a, 128 - LOW, 1)) for a in level])
        for shift in (4, 2, 1):
            every = dd_add(every, tuple(pltpu.roll(p, shift, 0) for p in every))
        return every

    numbers = range(2 * s // 8)
    late_group = (2 * s - LATE) // 8
    dots[pl.ds(8 * (2 * s - LATE), 8 * LATE), :] = jnp.zeros((8 * LATE, 128), F32)

    @pl.loop(0, cycles)
    def _(j):
        with jax.named_scope("cycle"):
            scale = jnp.where(j == 0, 1.0, 2.0).astype(F32)
            first = second = (zeros8, zeros8)
            with jax.named_scope("ainner"):
                for c in range(tiles):
                    first = inner(2 * j + 1, c, 1, cx - 1, scale, first)

            @pl.when(j == cycles - 1)
            def _():
                share(0, local_sums(numbers))

            @pl.when(j == 0)
            def _():
                taken(vrecv.at[tiles], lambda a, b: b * tiles * cx)

            for c in range(tiles):
                for d in (0, 1) if c == 0 else (c + 1,):
                    if d < tiles:
                        with jax.named_scope("landed"):
                            landed_near(j, d)
                        first = border(j, d, scale, first)
                with jax.named_scope("landed"):
                    landed_far(j, c)
                shell(j, c, scale)
                second = finish(j, c, second)
            for i, value in enumerate((*first, *second)):
                dots[pl.ds(pl.multiple_of(32 * j + 8 * i, 8), 8), :] = value

    scalar_lines.wait()

    with jax.named_scope("reduce"):
        share(1, local_sums(numbers[late_group:]))

        build_masks()
        for way, there in ((0, has_up), (1, has_down)):
            @pl.when(there)
            def _():
                drained(cycles * tiles * 2 * cy, xsend.at[way])
                drained(tiles * cy, vsend.at[way])
                for q, also in ((0, has_right), (1, has_left)):
                    @pl.when(also)
                    def _():
                        drained(cycles * tiles, csend.at[2 * way + q])

        for way, there in ((0, has_right), (1, has_left)):
            @pl.when(there)
            def _():
                drained(cycles * tiles * 2 * cx, ysend.at[way])
                drained(tiles * cx, vsend.at[2 + way])

        early = dd_sum(weighted(table, shared(0), range(2 * s - LATE)))
        reduced = dd_eliminate((early[0] + table[2 * s], early[1]), s - 2)

    with jax.named_scope("solve"):
        weights = dd_finish(table, early, reduced, shared(1))

    with jax.named_scope("combine"):
        @pl.loop(0, cx)
        def _(x):
            for c in range(tiles):
                for y in range(0, cy, 8):
                    pieces = [
                        w * vecs[1 + k, pl.ds(row(x, c, y), 8), :] for k, w in enumerate(weights)
                    ]
                    while len(pieces) > 1:
                        pieces = [sum(pieces[i : i + 2]) for i in range(0, len(pieces), 2)]
                    out[x, y : y + 8, 128 * c : 128 * (c + 1)] = pieces[0]
                    f = pl.ds(flat_row(x, c, y), 8)
                    at = (x * cy + y) * tiles + c
                    flat[pl.ds(at, 8, stride=tiles), :] = base[f, :] + slope[f, :] * pieces[0]

    picks = (pick0, pick1)

    def fetch(peer, pick):
        for part in range(wide):
            for i in range(128):
                pick[pl.ds(128 * part + i, 1), :] = flat[pl.ds(voxel[peer * wide + part, i], 1), :]

    def pass_on(peer, pick):
        for part in range(wide):
            value = pick[128 * part : 128 * (part + 1), :] * mask[peer * wide + part]
            sent[peer, pl.ds(part, 1), :] = jnp.sum(value.T, axis=0, keepdims=True)

    def give(peer):
        pltpu.make_async_remote_copy(
            src_ref=sent.at[peer], dst_ref=got.at[gy], send_sem=lsend, recv_sem=lrecv.at[gy],
            device_id=(gx, peer), device_id_type=mesh_id,
        ).start()

    def peer_at(step):
        return flipped(gy, n_gy - 1 - step, n_gy)

    with jax.named_scope("gather"):
        fetch(peer_at(0), picks[0])

        @pl.loop(0, n_gy // 2 - 1)
        def _(i):
            pass_on(peer_at(2 * i), picks[0])
            fetch(peer_at(2 * i + 1), picks[1])
            give(peer_at(2 * i))
            pass_on(peer_at(2 * i + 1), picks[1])
            fetch(peer_at(2 * i + 2), picks[0])
            give(peer_at(2 * i + 1))

        pass_on(peer_at(n_gy - 2), picks[0])
        fetch(gy, picks[1])
        give(peer_at(n_gy - 2))
        pass_on(gy, picks[1])
        got[gy] = sent[gy]

    own = tally.shape[0]

    def tallied(peer, first):
        spots = [target[pl.ds(peer * wide + part, 1), :] for part in range(wide)]
        values = [got[peer, part : part + 1, :] for part in range(wide)]
        for start in range(0, own, 128):
            found = []
            for r in range(start, start + 128, 8):
                total_ = zeros8 if first else tally[r : r + 8, :]
                for spot, value in zip(spots, values):
                    total_ = total_ + jnp.where(spot == sub8 + r, value, 0.0)
                found.append((r, total_))
            for r, total_ in found:
                tally[r : r + 8, :] = total_

    with jax.named_scope("links"):
        tallied(gy, True)
        drained(2 * (total - 1), rsend)

        @pl.loop(0, n_gy - 1)
        def _(step):
            peer = flipped(gy, n_gy - 1 - step, n_gy)
            pltpu.make_async_copy(got.at[peer], got.at[peer], lrecv.at[peer]).wait()
            tallied(peer, False)

        for start in range(0, own, 128):
            particle[0, :, start : start + 128] = jnp.sum(
                tally[start : start + 128, :].T, axis=0, keepdims=True
            )
        drained((n_gy - 1) * wide, lsend)


def kept(x):
    return pltpu.with_memory_space_constraint(x, pltpu.HBM)


def shards(sizes, source, voxel_phase, lin_potential, link_voxel, link_count, link_target):
    cx, cy, cz = source.shape
    total = sizes[0] * sizes[1]
    s = ITERS
    tiles = cz // 128
    voxels = cx * cy * tiles
    padded = (cx + 4) * tiles * (cy + PAD) + 8
    cycles = s // 2
    places = link_voxel[0, 0].reshape(-1, 128)
    peers = link_count.shape[2]
    slots = link_voxel.shape[2]
    groups = slots // 128
    whole = pl.BlockSpec(memory_space=pltpu.VMEM)
    far = pl.BlockSpec(memory_space=pltpu.HBM)
    found, sums = pl.pallas_call(
        functools.partial(kernel, sizes),
        out_shape=(
            jax.ShapeDtypeStruct(source.shape, F32),
            jax.ShapeDtypeStruct((1, 1, PART_DEV), F32),
        ),
        in_specs=[far] * 7,
        out_specs=(whole, whole),
        scratch_shapes=[
            pltpu.VMEM((tiles, cx, cy, 128), F32),
            pltpu.VMEM((tiles, cx, cy, 128), jnp.int32),
            pltpu.VMEM((tiles, cx, cy, 128), F32),
            pltpu.VMEM((2 * s + 1, ROWS, 128), F32),
            pltpu.VMEM((groups, 128), jnp.int32),
            pltpu.SMEM((groups, 128), jnp.int32),
            pltpu.VMEM((groups, 128), jnp.int32),
            pltpu.SMEM((peers,), jnp.int32),
            pltpu.VMEM((groups, 128), jnp.int32),
            pltpu.VMEM((s + 2, padded, 128), F32),
            pltpu.VMEM((voxels, 128), F32),
            pltpu.VMEM((tiles * (cx + 2) * cy, 128), F32),
            pltpu.VMEM((voxels, 128), F32),
            pltpu.VMEM((voxels, 128), F32),
            pltpu.VMEM((cycles, tiles, 2, 2 * cx, 128), F32),
            pltpu.VMEM((cycles, tiles, 2, 2 * cx + 8, 128), F32),
            pltpu.VMEM((2, tiles, cx, 128), F32),
            pltpu.VMEM((2, tiles, cx, 128), F32),
            pltpu.VMEM((2, tiles, cx, 128), F32),
            pltpu.VMEM((groups, 128, 128), F32),
            pltpu.VMEM((2 * s * 8, 128), F32),
            pltpu.VMEM((2, 1, 128), F32),
            pltpu.VMEM((2, total, 128), F32),
            pltpu.VMEM((groups // peers * 128, 128), F32),
            pltpu.VMEM((groups // peers * 128, 128), F32),
            pltpu.VMEM((voxels, 128), F32),
            pltpu.VMEM((peers, groups // peers, 128), F32),
            pltpu.VMEM((peers, groups // peers, 128), F32),
            pltpu.VMEM((PART_DEV, 128), F32),
            pltpu.SemaphoreType.DMA((tiles + 3,)),
            pltpu.SemaphoreType.DMA((2,)),
            pltpu.SemaphoreType.DMA((2,)),
            pltpu.SemaphoreType.DMA((4,)),
            pltpu.SemaphoreType.DMA((2, tiles, 2)),
            pltpu.SemaphoreType.DMA((4,)),
            pltpu.SemaphoreType.DMA((tiles + 1,)),
            pltpu.SemaphoreType.DMA,
            pltpu.SemaphoreType.DMA((2,)),
            pltpu.SemaphoreType.DMA,
            pltpu.SemaphoreType.DMA((peers,)),
        ],
        compiler_params=pltpu.CompilerParams(
            collective_id=0, has_side_effects=True, vmem_limit_bytes=52 * 2**20
        ),
    )(
        kept(source), kept(voxel_phase), kept(lin_potential), kept(jnp.asarray(gram_map())),
        kept(places), kept(link_count[0, 0]), kept(link_target[0, 0].reshape(groups, 128)),
    )
    return pl.pallas_call(
        last_kernel,
        out_shape=(
            jax.ShapeDtypeStruct(source.shape, F32),
            jax.ShapeDtypeStruct((1, 1, PART_DEV), F32),
        ),
        in_specs=[pl.BlockSpec(memory_space=pl.ANY)] * 2,
        out_specs=(far, far),
        scratch_shapes=[pltpu.SemaphoreType.DMA((2,))],
        compiler_params=pltpu.CompilerParams(vmem_limit_bytes=2 * 2**20),
    )(found, sums)


def solution(mesh):
    spec = P("gx", "gy", None)
    return jax.shard_map(
        functools.partial(shards, (mesh.shape["gx"], mesh.shape["gy"])),
        mesh=mesh,
        in_specs=(spec,) * 6,
        out_specs=(spec, spec),
        check_vma=False,
    )
```

```python
import functools

import jax
import jax.numpy as jnp
import numpy as np
from jax import lax
from jax.experimental import pallas as pl
from jax.experimental.pallas import tpu as pltpu
from jax.sharding import PartitionSpec as P

ITERS = 12
PART_DEV = 512
ROWS = 16
RHS = 15
LATE = 4
PAD = 8
LOW = 64
F32 = jnp.float32


def gram_map():
    s = ITERS
    n = 2 * s

    def unit(at):
        out = np.zeros(n)
        out[at] = 1.0
        return out

    m = []
    for k in range(s):
        m.append(2 * unit(2 * k) - unit(0))
        m.append(2 * unit(2 * k + 1) - unit(1))

    def entry(j, k):
        a, b = j + k, abs(j - k)
        return 0.5 * (
            m[a] - 0.5 * (m[a + 1] + m[abs(a - 1)]) + m[b] - 0.5 * (m[b + 1] + m[abs(b - 1)])
        )

    table = np.zeros((n, ROWS, 128))
    for j in range(s):
        table[:, j, RHS] = m[j]
        for k in range(s):
            table[:, j, k] = entry(j, k)
    extra = np.zeros((ROWS, 128))
    for i, m in enumerate(range(n - LATE, n)):
        extra[:, RHS + 1 + 2 * i : RHS + 3 + 2 * i] = table[m][:, s - 2 : s]
    return np.concatenate([table, extra[None]]).astype(np.float32)


def two_sum(a, b):
    s = a + b
    t = s - a
    return s, (a - (s - t)) + (b - t)


def quick_two_sum(a, b):
    s = a + b
    return s, b - (s - a)


def split(a):
    c = 4097.0 * a
    hi = c - (c - a)
    return hi, a - hi


def two_prod(a, b):
    p = a * b
    ah, al = split(a)
    bh, bl = split(b)
    return p, ((ah * bh - p) + ah * bl + al * bh) + al * bl


def dd_add(a, b):
    s, e = two_sum(a[0], b[0])
    return quick_two_sum(s, e + (a[1] + b[1]))


def dd_mul(a, b):
    p, e = two_prod(a[0], b[0])
    return quick_two_sum(p, e + (a[0] * b[1] + a[1] * b[0]))


def dd_inverse(a):
    x = 1.0 / a[0]
    p, e = two_prod(a[0], x)
    r = (1.0 - p) - e - a[1] * x
    return quick_two_sum(x, x * r)


def dd_minus(a, b):
    return dd_add(a, (-b[0], -b[1]))


def dd_sum(terms):
    while len(terms) > 1:
        terms = [
            dd_add(terms[i], terms[i + 1]) if i + 1 < len(terms) else terms[i]
            for i in range(0, len(terms), 2)
        ]
    return terms[0]


def lane_column(matrix, j):
    return tuple(jnp.broadcast_to(m[:, j : j + 1], m.shape) for m in matrix)


def full_row(matrix, j, rows=ROWS):
    return tuple(jnp.broadcast_to(m[j : j + 1, :], (rows, 128)) for m in matrix)


def weighted(table, every, numbers):
    terms = []
    for m in numbers:
        hi, lo = (jnp.broadcast_to(p[0:1, m : m + 1], (ROWS, 128)) for p in every)
        terms.append((table[m] * hi, table[m] * lo))
    return terms


def dd_eliminate(matrix, count):
    rows = lax.broadcasted_iota(jnp.int32, (ROWS, 128), 0)

    def eliminate(a, j, by, inverse):
        scaled = dd_mul(full_row(a, j), inverse)
        less = dd_minus(a, dd_mul(by, scaled))
        return tuple(jnp.where(rows == j, r, m) for r, m in zip(scaled, less))

    for j in range(0, count, 2):
        one, two = lane_column(matrix, j), lane_column(matrix, j + 1)
        inverse = dd_inverse(full_row(one, j))
        two = eliminate(two, j, one, inverse)
        matrix = eliminate(matrix, j, one, inverse)
        matrix = eliminate(matrix, j + 1, two, dd_inverse(full_row(two, j + 1)))
    return matrix


def dd_finish(table, early, reduced, every):
    u = ITERS - 2
    rows = lax.broadcasted_iota(jnp.int32, (ROWS, 128), 0)
    lanes = lax.broadcasted_iota(jnp.int32, (ROWS, 128), 1)
    last_two = (lanes == u) | (lanes == u + 1)
    late = range(2 * ITERS - LATE, 2 * ITERS)
    matrix = dd_sum([early] + weighted(table, every, late))
    terms = [reduced]
    for i, m in enumerate(late):
        value = tuple(
            jnp.where(last_two, jnp.broadcast_to(p[0:1, m : m + 1], (ROWS, 128)), 0.0) for p in every
        )
        moved = tuple(pltpu.roll(p, 128 - (RHS + 1 + 2 * i - u), 1) for p in reduced)
        terms.append(dd_mul(value, moved))
    x = dd_sum(terms)
    schur = []
    for a in range(2):
        product = dd_mul(lane_column(matrix, u + a), x)
        product = tuple(jnp.where(rows < u, p, 0.0) for p in product)
        total = dd_add(tuple(p[0:8, :] for p in product), tuple(p[8:16, :] for p in product))
        for shift in (4, 2, 1):
            total = dd_add(total, tuple(pltpu.roll(p, shift, 0) for p in total))
        schur.append(dd_minus(full_row(matrix, u + a, 8), total))
    (s00, s01, r0), (s10, s11, r1) = (
        [lane_column(row, j) for j in (u, u + 1, RHS)] for row in schur
    )
    over = dd_inverse(dd_minus(dd_mul(s00, s11), dd_mul(s01, s10)))
    c0 = dd_mul(dd_minus(dd_mul(r0, s11), dd_mul(r1, s01)), over)
    c1 = dd_mul(dd_minus(dd_mul(r1, s00), dd_mul(r0, s10)), over)
    rest = dd_minus(
        dd_minus(lane_column(x, RHS), dd_mul(lane_column(x, u), full_row(c0, 0))),
        dd_mul(lane_column(x, u + 1), full_row(c1, 0)),
    )
    return [full_row(rest, j, 8)[0] for j in range(u)] + [c0[0], c1[0]]


def partners(index, size):
    if size & (size - 1):
        return [lax.rem(index + m, size) for m in range(size)]
    out = [0]
    bit = 1
    while bit < size:
        same = lax.rem(index // bit, 2) * bit
        out = [o + same for o in out] + [o + (bit - same) for o in out]
        bit *= 2
    return out


def flipped(index, m, size):
    if size & (size - 1):
        return lax.rem(index + m, size)
    out, bit = 0, 1
    while bit < size:
        out = out + lax.rem(index // bit + m // bit, 2) * bit
        bit *= 2
    return out


def last_kernel(found, sums, out, particle, sems):
    pieces = [
        pltpu.make_async_copy(found, out, sems.at[0]),
        pltpu.make_async_copy(sums, particle, sems.at[1]),
    ]
    for copy in pieces:
        copy.start()
    for copy in pieces:
        copy.wait()


def kernel(
    sizes, source_hbm, phase_hbm, potential_hbm, map_hbm, places_hbm, count_hbm, target_hbm,
    out, particle,
    source, phase, potential, table, lines, voxel, places, count, target, vecs, diag, inv, base, slope, ybuf, hin,
    pinv, hinv, hodd, mask, dots, mine, parts, pick0, pick1, flat, sent, got, tally,
    isem, xsend, ysend, csend, hrecv, vsend, vrecv, rsend, rrecv, lsend, lrecv,
):
    n_gx, n_gy = sizes
    total = n_gx * n_gy
    cx, cy, cz = source_hbm.shape
    tiles = cz // 128
    pitch = cy + PAD
    block = (cx + 4) * pitch
    s = ITERS
    cycles = s // 2
    gx, gy = lax.axis_index("gx"), lax.axis_index("gy")
    me = gx * n_gy + gy
    mesh_id = pl.DeviceIdType.MESH

    barrier = pltpu.get_barrier_semaphore()

    gy_of = partners(gy, n_gy)
    gx_of = partners(gx, n_gx)

    def everyone(act):
        for m in reversed(range(n_gy)):
            for q in reversed(range(n_gx)):
                if m or q:
                    act(gx_of[q], gy_of[m])


    loads = []
    for c in range(tiles):
        for src, dst in (
            (potential_hbm, potential), (phase_hbm, phase), (source_hbm, source)
        ):
            loads.append(
                pltpu.make_async_copy(
                    src.at[:, :, pl.ds(128 * c, 128)], dst.at[c], isem.at[c]
                )
            )
    extra = [
        pltpu.make_async_copy(map_hbm, table, isem.at[tiles]),
        pltpu.make_async_copy(places_hbm, places, isem.at[tiles]),
        pltpu.make_async_copy(count_hbm, count, isem.at[tiles + 1]),
        pltpu.make_async_copy(target_hbm, target, isem.at[tiles]),
    ]
    for copy in loads[:3]:
        copy.start()
    everyone(
        lambda to_gx, to_gy: pl.semaphore_signal(
            barrier, inc=1, device_id=(to_gx, to_gy), device_id_type=mesh_id
        )
    )
    for copy in loads[3:] + extra:
        copy.start()

    has_up, has_down = gx < n_gx - 1, gx > 0
    has_right, has_left = gy < n_gy - 1, gy > 0
    up_gx, down_gx = jnp.minimum(gx + 1, n_gx - 1), jnp.maximum(gx - 1, 0)
    right_gy, left_gy = jnp.minimum(gy + 1, n_gy - 1), jnp.maximum(gy - 1, 0)

    def row(x, c, y):
        return c * block + (x + 2) * pitch + PAD + y

    def inv_row(x, c, y):
        return (c * (cx + 2) + x + 1) * cy + y

    def flat_row(x, c, y):
        return (c * cx + x) * cy + y

    def drained(rows, sem):
        ref = vecs.at[0, pl.ds(0, rows), :]
        pltpu.make_async_copy(ref, ref, sem).wait()

    def counts(one, other, size):
        if size < 3:
            return [(size - 1, None)]
        both = one & other
        return [(1, jnp.logical_not(both)), (2, both)]

    x_counts = counts(has_up, has_down, n_gx)
    y_counts = counts(has_right, has_left, n_gy)

    def taken(sem, rows):
        for a, so_many_x in x_counts:
            for b, so_many_y in y_counts:
                if not rows(a, b):
                    continue
                there = [t for t in (so_many_x, so_many_y) if t is not None]
                if there:
                    pl.when(functools.reduce(jnp.logical_and, there))(
                        functools.partial(drained, rows(a, b), sem)
                    )
                else:
                    drained(rows(a, b), sem)

    near, low_corner, high_corner = cx, 2 * cx + 1, 2 * cx
    zeros8 = jnp.zeros((8, 128), F32)
    zero_row = jnp.zeros((1, 128), F32)

    sides = ((0, 0, 1), (1, cy - 1, cy - 2))

    def pack_rows(j, c):
        k = 2 * j + 1
        for side, y1, y2 in sides:
            for x in range(0, cx, 8):
                ybuf[j, c, side, pl.ds(near + x, 8), :] = (
                    vecs[k, pl.ds(row(x, c, y1), 8, stride=pitch), :]
                )
                ybuf[j, c, side, pl.ds(x, 8), :] = vecs[k, pl.ds(row(x, c, y2), 8, stride=pitch), :]

    def xcopy(j, c, way, layer):
        up = way == 0
        return pltpu.make_async_remote_copy(
            src_ref=vecs.at[2 * j + 1, pl.ds(row(cx - 1 - layer if up else layer, c, 0), cy), :],
            dst_ref=vecs.at[2 * j + 1, pl.ds(row(-1 - layer if up else cx + layer, c, 0), cy), :],
            send_sem=xsend.at[way], recv_sem=hrecv.at[lax.rem(j, 2), c, layer],
            device_id=(up_gx if up else down_gx, gy), device_id_type=mesh_id,
        )

    def ycopy(j, c, way):
        right = way == 0
        return pltpu.make_async_remote_copy(
            src_ref=ybuf.at[j, c, 1 if right else 0],
            dst_ref=hin.at[j, c, 0 if right else 1, pl.ds(0, 2 * cx), :],
            send_sem=ysend.at[way], recv_sem=hrecv.at[lax.rem(j, 2), c, 0],
            device_id=(gx, right_gy if right else left_gy), device_id_type=mesh_id,
        )

    def ccopy(j, c, xway, yway):
        up, right = xway == 0, yway == 0
        q = 2 * xway + yway
        return pltpu.make_async_remote_copy(
            src_ref=vecs.at[
                2 * j + 1, pl.ds(row(cx - 1 if up else 0, c, cy - 1 if right else 0), 1), :
            ],
            dst_ref=hin.at[j, c, 0 if right else 1, pl.ds(low_corner if up else high_corner, 1), :],
            send_sem=csend.at[q], recv_sem=hrecv.at[lax.rem(j, 2), c, 1],
            device_id=(up_gx if up else down_gx, right_gy if right else left_gy),
            device_id_type=mesh_id,
        )

    def vcopy(c, way):
        up = way == 0
        return pltpu.make_async_remote_copy(
            src_ref=inv.at[pl.ds(inv_row(cx - 1 if up else 0, c, 0), cy), :],
            dst_ref=inv.at[pl.ds(inv_row(-1 if up else cx, c, 0), cy), :],
            send_sem=vsend.at[way], recv_sem=vrecv.at[c],
            device_id=(up_gx if up else down_gx, gy), device_id_type=mesh_id,
        )

    def hcopy(way):
        right = way == 0
        return pltpu.make_async_remote_copy(
            src_ref=pinv.at[1 if right else 0], dst_ref=hinv.at[0 if right else 1],
            send_sem=vsend.at[2 + way], recv_sem=vrecv.at[tiles],
            device_id=(gx, right_gy if right else left_gy), device_id_type=mesh_id,
        )

    for c in range(tiles):
        drained(3 * cx * cy, isem.at[c])

        @pl.loop(0, cx)
        def _(x):
            found = []
            for y in range(0, cy, 8):
                at = potential[c, x, y : y + 8, :]
                rising = jnp.exp(0.4 * at)
                falling = jnp.exp(-0.6 * at)
                label = phase[c, x, y : y + 8, :]
                rate = jnp.where(label == 1, 0.3, jnp.where(label == 2, 0.08, 0.02)).astype(F32)
                bend = 0.4 * rising + 0.6 * falling
                d = 6.0 + rate * bend
                i = 1.0 / d
                found.append((y, rising - falling, bend, d, i, source[c, x, y : y + 8, :] * i))
            for y, level, bend, d, i, v in found:
                f = pl.ds(flat_row(x, c, y), 8)
                base[f, :] = level
                slope[f, :] = bend
                diag[f, :] = d
                inv[pl.ds(inv_row(x, c, y), 8), :] = i
                vecs[1, pl.ds(row(x, c, y), 8), :] = v

        pack_rows(0, c)
        for side, y, _ in sides:
            for x in range(0, cx, 8):
                pinv[side, c, pl.ds(x, 8), :] = inv[pl.ds(inv_row(x, c, y), 8, stride=cy), :]

    def launch_x(j, c, more):
        for way, there in ((0, has_up), (1, has_down)):
            @pl.when(there & more)
            def _():
                pl.when(has_right)(ccopy(j, c, way, 0).start)
                pl.when(has_left)(ccopy(j, c, way, 1).start)
                xcopy(j, c, way, 0).start()
                xcopy(j, c, way, 1).start()

    def launch_y(j, c, more):
        pl.when(has_right & more)(ycopy(j, c, 0).start)
        pl.when(has_left & more)(ycopy(j, c, 1).start)

    def landed_near(j, c):
        taken(hrecv.at[lax.rem(j, 2), c, 0], lambda a, b: a * cy + b * 2 * cx)

    def landed_far(j, c):
        taken(hrecv.at[lax.rem(j, 2), c, 1], lambda a, b: a * (cy + b))

        @pl.when(j == 0)
        def _():
            taken(vrecv.at[c], lambda a, b: a * cy)

    with jax.named_scope("barrier"):
        pl.semaphore_wait(barrier, total - 1)

    always = gx >= 0
    pl.when(has_right)(hcopy(0).start)
    pl.when(has_left)(hcopy(1).start)
    for c in range(tiles):
        launch_x(0, c, always)
        launch_y(0, c, always)
        pl.when(has_up)(vcopy(c, 0).start)
        pl.when(has_down)(vcopy(c, 1).start)

    groups = places.shape[0]
    wide = groups // n_gy
    drained(table.shape[0] * ROWS + 2 * groups, isem.at[tiles])
    pltpu.make_async_copy(count_hbm, count, isem.at[tiles + 1]).wait()
    lines[...] = places[...] >> 7
    scalar_lines = pltpu.make_async_copy(lines, voxel, isem.at[tiles + 2])
    scalar_lines.start()

    @pl.loop(-1, cx + 1)
    def _(x):
        for c in range(tiles):
            for y in range(0, cy, 8):
                vecs[0, pl.ds(row(x, c, y), 8), :] = zeros8

    @pl.loop(0, cycles)
    def _(j):
        @pl.loop(0, cx + 1)
        def _(x):
            for c in range(tiles):
                vecs[2 * j + 1, pl.ds(row(x, c, -PAD), 8), :] = zeros8

    hodd[...] = jnp.zeros(hodd.shape, F32)
    for beyond, x in ((gx == 0, -1), (gx == n_gx - 1, cx)):
        @pl.when(beyond)
        def _():
            for c in range(tiles):
                for y in range(0, cy, 8):
                    inv[pl.ds(inv_row(x, c, y), 8), :] = zeros8

            @pl.loop(0, cycles)
            def _(j):
                for c in range(tiles):
                    first = row(-2 if x < 0 else cx, c, 0)
                    for y in range(0, pitch + cy, 8):
                        vecs[2 * j + 1, pl.ds(first + y, 8), :] = zeros8
                    for side in range(2):
                        hin[j, c, side, pl.ds(low_corner if x < 0 else high_corner, 1), :] = zero_row

    for beyond, side in ((gy == 0, 0), (gy == n_gy - 1, 1)):
        @pl.when(beyond)
        def _():
            hinv[side] = jnp.zeros(hinv.shape[1:], F32)

            @pl.loop(0, cycles)
            def _(j):
                for c in range(tiles):
                    hin[j, c, side] = jnp.zeros(hin.shape[3:], F32)

    def build_masks():
        @pl.loop(0, n_gy)
        def _(peer):
            live = count[peer]
            lanes = lax.broadcasted_iota(jnp.int32, (128, 128), 1)
            rows = lax.broadcasted_iota(jnp.int32, (128, 128), 0)
            for part in range(wide):
                at = (places[pl.ds(peer * wide + part, 1), :] & 127).astype(F32)
                at = jnp.broadcast_to(at, (128, 128)).T
                mask[peer * wide + part] = jnp.where(
                    (lanes.astype(F32) == at) & (rows + 128 * part < live), 0.5, 0.0
                )

    lane8 = lax.broadcasted_iota(jnp.int32, (8, 128), 1)
    sub8 = lax.broadcasted_iota(jnp.int32, (8, 128), 0)
    first_lane, last_lane = lane8 == 0, lane8 == 127

    def beside(v, before, after):
        z = pltpu.roll(jnp.where(last_lane, before, v), 1, 1)
        return z + pltpu.roll(jnp.where(first_lane, after, v), 127, 1)

    def sweep(k, runs, scale, carry, more=lambda: ()):
        centers = {}

        def center(run, c, start, o, y):
            if (run, o, y) not in centers:
                centers[run, o, y] = vecs[k, pl.ds(row(start + o, c, y), 8), :]
            return centers[run, o, y]

        found = []
        for run, (c, start, offsets, counted) in enumerate(runs):
            for y in range(0, cy, 8):
                for o in offsets:
                    r = row(start + o, c, y)
                    v = center(run, c, start, o, y)
                    before = vecs[k, pl.ds(r - block, 8), :] if c > 0 else 0.0
                    after = vecs[k, pl.ds(r + block, 8), :] if c < tiles - 1 else 0.0
                    n = vecs[k, pl.ds(r - 1, 8), :] + vecs[k, pl.ds(r + 1, 8), :]
                    n = n + (center(run, c, start, o - 1, y) + center(run, c, start, o + 1, y))
                    n = n + beside(v, before, after)
                    i = inv[pl.ds(inv_row(start + o, c, y), 8), :]
                    new = (scale * i) * n - vecs[k - 1, pl.ds(r, 8), :]
                    if counted:
                        w = diag[pl.ds(flat_row(start + o, c, y), 8), :] * v
                        carry = (carry[0] + w * v, carry[1] + w * new)
                    found.append((r, new))
        others = more()
        for r, new in found:
            vecs[k + 1, pl.ds(r, 8), :] = new
        for store in others:
            store()
        return carry

    def inner(k, c, first, last, scale, carry):
        group = max(g for g in range(1, 8) if (last - first) % g == 0)

        def some(i, a):
            return sweep(k, [(c, group * i + first, range(group), True)], scale, a)

        return lax.fori_loop(0, (last - first) // group, some, carry)

    def rows_beyond(j, c, scale):
        k = 2 * j + 1
        stores = []
        for side, beyond in ((0, -1), (1, cy)):
            for x in range(0, cx, 8):
                at = pl.ds(near + x, 8)
                h = hin[j, c, side, at, :]
                before = hin[j, c - 1, side, at, :] if c > 0 else 0.0
                after = hin[j, c + 1, side, at, :] if c < tiles - 1 else 0.0
                lower = hin[j, c, side, pl.ds(near + x - 1, 8), :]
                if x == 0:
                    corner = hin[j, c, side, pl.ds(low_corner, 1), :]
                    lower = jnp.where(sub8 == 0, corner, lower)
                upper = hin[j, c, side, pl.ds(near + x + 1, 8), :]
                n = (lower + upper) + (hin[j, c, side, pl.ds(x, 8), :] + ybuf[j, c, side, at, :])
                n = n + beside(h, before, after)
                old = pl.ds(x, 8)
                new = (scale * hinv[side, c, old, :]) * n - hodd[side, c, old, :]

                def store(side=side, old=old, new=new, line=row(x, c, beyond)):
                    hodd[side, c, old, :] = new
                    vecs[k + 1, pl.ds(line, 8, stride=pitch), :] = new

                stores.append(store)
        return stores

    def outside(j, border, shell, scale, carry):
        k = 2 * j + 1
        runs, more = [], lambda: ()
        if border is not None:
            runs += [(border, 0, (0,), True), (border, cx - 1, (0,), True)]
        if shell is not None:
            for side, y in ((0, -1), (1, cy)):
                for x, at in ((-1, low_corner), (cx, high_corner)):
                    vecs[k, pl.ds(row(x, shell, y), 1), :] = hin[j, shell, side, pl.ds(at, 1), :]
            runs += [(shell, -1, (0,), False), (shell, cx, (0,), False)]
            more = functools.partial(rows_beyond, j, shell, scale)
        carry = sweep(k, runs, scale, carry, more)
        if border is None:
            return carry
        own, cross = carry
        found = []
        for side, y, _ in sides:
            for x in range(0, cx, 8):
                at = pl.ds(near + x, 8)
                h = hin[j, border, side, at, :]
                line = pl.ds(row(x, border, y), 8, stride=pitch)
                fixed = vecs[k + 1, line, :] + (scale * pinv[side, border, pl.ds(x, 8), :]) * h
                cross = cross + (scale * ybuf[j, border, side, at, :]) * h
                found.append((line, fixed))
        for line, fixed in found:
            vecs[k + 1, line, :] = fixed
        return own, cross

    def finish(j, c, carry):
        k = 2 * j + 2
        more = j < cycles - 1
        carry = sweep(k, [(c, 0, (0, 1), True), (c, cx - 2, (0, 1), True)], 2.0, carry)
        launch_x(j + 1, c, more)
        carry = inner(k, c, 2, cx - 2, 2.0, carry)

        @pl.when(more)
        def _():
            pack_rows(j + 1, c)
            launch_y(j + 1, c, always)

        return carry

    def local_sums(numbers):
        sums = []
        for g in numbers:
            level = [dots[pl.ds(64 * g + i, 8, stride=8), :] for i in range(8)]
            level = [two_sum(level[2 * i], level[2 * i + 1]) for i in range(4)]
            sums.append(dd_sum(level))
        for shift in (64, 32, 16, 8, 4, 2, 1):
            sums = [
                dd_add(a, tuple(pltpu.roll(p, shift, 1) for p in a)) for a in sums
            ]
        spread = zeros8
        for g, (hi, lo) in zip(numbers, sums):
            spread = jnp.where(lane8 == sub8 + 8 * g, hi, spread)
            spread = jnp.where(lane8 == sub8 + 8 * g + LOW, lo, spread)
        return jnp.sum(spread, axis=0, keepdims=True)

    def share(which, line):
        mine[which] = line
        parts[which, pl.ds(me, 1), :] = line
        everyone(
            lambda to_gx, to_gy: pltpu.make_async_remote_copy(
                src_ref=mine.at[which], dst_ref=parts.at[which, pl.ds(me, 1), :],
                send_sem=rsend, recv_sem=rrecv.at[which],
                device_id=(to_gx, to_gy), device_id_type=mesh_id,
            ).start()
        )

    def shared(which):
        drained(total - 1, rrecv.at[which])
        level = [parts[which, 8 * i : 8 * i + 8, :] for i in range(total // 8)]
        every = dd_sum([(a, pltpu.roll(a, 128 - LOW, 1)) for a in level])
        for shift in (4, 2, 1):
            every = dd_add(every, tuple(pltpu.roll(p, shift, 0) for p in every))
        return every

    numbers = range(2 * s // 8)
    late_group = (2 * s - LATE) // 8
    dots[pl.ds(8 * (2 * s - LATE), 8 * LATE), :] = jnp.zeros((8 * LATE, 128), F32)

    @pl.loop(0, cycles)
    def _(j):
        with jax.named_scope("cycle"):
            scale = jnp.where(j == 0, 1.0, 2.0).astype(F32)
            first = second = (zeros8, zeros8)
            with jax.named_scope("ainner"):
                for c in range(tiles):
                    first = inner(2 * j + 1, c, 1, cx - 1, scale, first)

            @pl.when(j == cycles - 1)
            def _():
                share(0, local_sums(numbers))

            @pl.when(j == 0)
            def _():
                taken(vrecv.at[tiles], lambda a, b: b * tiles * cx)

            with jax.named_scope("landed"):
                landed_near(j, 0)
            first = outside(j, 0, None, scale, first)
            for c in range(tiles):
                following = c + 1 if c + 1 < tiles else None
                with jax.named_scope("landed"):
                    if following is not None:
                        landed_near(j, following)
                    landed_far(j, c)
                first = outside(j, following, c, scale, first)
                second = finish(j, c, second)
            for i, value in enumerate((*first, *second)):
                dots[pl.ds(pl.multiple_of(32 * j + 8 * i, 8), 8), :] = value

    scalar_lines.wait()

    with jax.named_scope("reduce"):
        share(1, local_sums(numbers[late_group:]))

        build_masks()
        for way, there in ((0, has_up), (1, has_down)):
            @pl.when(there)
            def _():
                drained(cycles * tiles * 2 * cy, xsend.at[way])
                drained(tiles * cy, vsend.at[way])
                for q, also in ((0, has_right), (1, has_left)):
                    @pl.when(also)
                    def _():
                        drained(cycles * tiles, csend.at[2 * way + q])

        for way, there in ((0, has_right), (1, has_left)):
            @pl.when(there)
            def _():
                drained(cycles * tiles * 2 * cx, ysend.at[way])
                drained(tiles * cx, vsend.at[2 + way])

        early = dd_sum(weighted(table, shared(0), range(2 * s - LATE)))
        reduced = dd_eliminate((early[0] + table[2 * s], early[1]), s - 2)

    with jax.named_scope("solve"):
        weights = dd_finish(table, early, reduced, shared(1))

    with jax.named_scope("combine"):
        @pl.loop(0, cx)
        def _(x):
            for c in range(tiles):
                for y in range(0, cy, 8):
                    pieces = [
                        w * vecs[1 + k, pl.ds(row(x, c, y), 8), :] for k, w in enumerate(weights)
                    ]
                    while len(pieces) > 1:
                        pieces = [sum(pieces[i : i + 2]) for i in range(0, len(pieces), 2)]
                    out[x, y : y + 8, 128 * c : 128 * (c + 1)] = pieces[0]
                    f = pl.ds(flat_row(x, c, y), 8)
                    at = (x * cy + y) * tiles + c
                    flat[pl.ds(at, 8, stride=tiles), :] = base[f, :] + slope[f, :] * pieces[0]

    picks = (pick0, pick1)

    def fetch(peer, pick):
        for part in range(wide):
            for i in range(128):
                pick[pl.ds(128 * part + i, 1), :] = flat[pl.ds(voxel[peer * wide + part, i], 1), :]

    def pass_on(peer, pick):
        for part in range(wide):
            value = pick[128 * part : 128 * (part + 1), :] * mask[peer * wide + part]
            sent[peer, pl.ds(part, 1), :] = jnp.sum(value.T, axis=0, keepdims=True)

    def give(peer):
        pltpu.make_async_remote_copy(
            src_ref=sent.at[peer], dst_ref=got.at[gy], send_sem=lsend, recv_sem=lrecv.at[gy],
            device_id=(gx, peer), device_id_type=mesh_id,
        ).start()

    def peer_at(step):
        return flipped(gy, n_gy - 1 - step, n_gy)

    with jax.named_scope("gather"):
        fetch(peer_at(0), picks[0])

        @pl.loop(0, n_gy // 2 - 2)
        def _(i):
            pass_on(peer_at(2 * i), picks[0])
            fetch(peer_at(2 * i + 1), picks[1])
            give(peer_at(2 * i))
            pass_on(peer_at(2 * i + 1), picks[1])
            fetch(peer_at(2 * i + 2), picks[0])
            give(peer_at(2 * i + 1))

        pass_on(peer_at(n_gy - 4), picks[0])
        fetch(peer_at(n_gy - 3), picks[1])
        give(peer_at(n_gy - 4))
        pass_on(peer_at(n_gy - 3), picks[1])
        give(peer_at(n_gy - 3))
        fetch(peer_at(n_gy - 2), picks[0])
        pass_on(peer_at(n_gy - 2), picks[0])
        give(peer_at(n_gy - 2))
        fetch(gy, picks[1])
        pass_on(gy, picks[1])
        got[gy] = sent[gy]

    own = tally.shape[0]

    def tallied(peer, first):
        spots = [target[pl.ds(peer * wide + part, 1), :] for part in range(wide)]
        values = [got[peer, part : part + 1, :] for part in range(wide)]
        for start in range(0, own, 128):
            found = []
            for r in range(start, start + 128, 8):
                total_ = zeros8 if first else tally[r : r + 8, :]
                for spot, value in zip(spots, values):
                    total_ = total_ + jnp.where(spot == sub8 + r, value, 0.0)
                found.append((r, total_))
            for r, total_ in found:
                tally[r : r + 8, :] = total_

    with jax.named_scope("links"):
        tallied(gy, True)
        drained(2 * (total - 1), rsend)

        @pl.loop(0, n_gy - 1)
        def _(step):
            peer = flipped(gy, n_gy - 1 - step, n_gy)
            pltpu.make_async_copy(got.at[peer], got.at[peer], lrecv.at[peer]).wait()
            tallied(peer, False)

        for start in range(0, own, 128):
            particle[0, :, start : start + 128] = jnp.sum(
                tally[start : start + 128, :].T, axis=0, keepdims=True
            )
        drained((n_gy - 1) * wide, lsend)


def kept(x):
    return pltpu.with_memory_space_constraint(x, pltpu.HBM)


def shards(sizes, source, voxel_phase, lin_potential, link_voxel, link_count, link_target):
    cx, cy, cz = source.shape
    total = sizes[0] * sizes[1]
    s = ITERS
    tiles = cz // 128
    voxels = cx * cy * tiles
    padded = (cx + 4) * tiles * (cy + PAD) + 8
    cycles = s // 2
    places = link_voxel[0, 0].reshape(-1, 128)
    peers = link_count.shape[2]
    slots = link_voxel.shape[2]
    groups = slots // 128
    whole = pl.BlockSpec(memory_space=pltpu.VMEM)
    far = pl.BlockSpec(memory_space=pltpu.HBM)
    found, sums = pl.pallas_call(
        functools.partial(kernel, sizes),
        out_shape=(
            jax.ShapeDtypeStruct(source.shape, F32),
            jax.ShapeDtypeStruct((1, 1, PART_DEV), F32),
        ),
        in_specs=[far] * 7,
        out_specs=(whole, whole),
        scratch_shapes=[
            pltpu.VMEM((tiles, cx, cy, 128), F32),
            pltpu.VMEM((tiles, cx, cy, 128), jnp.int32),
            pltpu.VMEM((tiles, cx, cy, 128), F32),
            pltpu.VMEM((2 * s + 1, ROWS, 128), F32),
            pltpu.VMEM((groups, 128), jnp.int32),
            pltpu.SMEM((groups, 128), jnp.int32),
            pltpu.VMEM((groups, 128), jnp.int32),
            pltpu.SMEM((peers,), jnp.int32),
            pltpu.VMEM((groups, 128), jnp.int32),
            pltpu.VMEM((s + 2, padded, 128), F32),
            pltpu.VMEM((voxels, 128), F32),
            pltpu.VMEM((tiles * (cx + 2) * cy, 128), F32),
            pltpu.VMEM((voxels, 128), F32),
            pltpu.VMEM((voxels, 128), F32),
            pltpu.VMEM((cycles, tiles, 2, 2 * cx, 128), F32),
            pltpu.VMEM((cycles, tiles, 2, 2 * cx + 8, 128), F32),
            pltpu.VMEM((2, tiles, cx, 128), F32),
            pltpu.VMEM((2, tiles, cx, 128), F32),
            pltpu.VMEM((2, tiles, cx, 128), F32),
            pltpu.VMEM((groups, 128, 128), F32),
            pltpu.VMEM((2 * s * 8, 128), F32),
            pltpu.VMEM((2, 1, 128), F32),
            pltpu.VMEM((2, total, 128), F32),
            pltpu.VMEM((groups // peers * 128, 128), F32),
            pltpu.VMEM((groups // peers * 128, 128), F32),
            pltpu.VMEM((voxels, 128), F32),
            pltpu.VMEM((peers, groups // peers, 128), F32),
            pltpu.VMEM((peers, groups // peers, 128), F32),
            pltpu.VMEM((PART_DEV, 128), F32),
            pltpu.SemaphoreType.DMA((tiles + 3,)),
            pltpu.SemaphoreType.DMA((2,)),
            pltpu.SemaphoreType.DMA((2,)),
            pltpu.SemaphoreType.DMA((4,)),
            pltpu.SemaphoreType.DMA((2, tiles, 2)),
            pltpu.SemaphoreType.DMA((4,)),
            pltpu.SemaphoreType.DMA((tiles + 1,)),
            pltpu.SemaphoreType.DMA,
            pltpu.SemaphoreType.DMA((2,)),
            pltpu.SemaphoreType.DMA,
            pltpu.SemaphoreType.DMA((peers,)),
        ],
        compiler_params=pltpu.CompilerParams(
            collective_id=0, has_side_effects=True, vmem_limit_bytes=52 * 2**20
        ),
    )(
        kept(source), kept(voxel_phase), kept(lin_potential), kept(jnp.asarray(gram_map())),
        kept(places), kept(link_count[0, 0]), kept(link_target[0, 0].reshape(groups, 128)),
    )
    return pl.pallas_call(
        last_kernel,
        out_shape=(
            jax.ShapeDtypeStruct(source.shape, F32),
            jax.ShapeDtypeStruct((1, 1, PART_DEV), F32),
        ),
        in_specs=[pl.BlockSpec(memory_space=pl.ANY)] * 2,
        out_specs=(far, far),
        scratch_shapes=[pltpu.SemaphoreType.DMA((2,))],
        compiler_params=pltpu.CompilerParams(vmem_limit_bytes=2 * 2**20),
    )(found, sums)


def solution(mesh):
    spec = P("gx", "gy", None)
    return jax.shard_map(
        functools.partial(shards, (mesh.shape["gx"], mesh.shape["gy"])),
        mesh=mesh,
        in_specs=(spec,) * 6,
        out_specs=(spec, spec),
        check_vma=False,
    )
```

```python
import functools

import jax
import jax.numpy as jnp
import numpy as np
from jax import lax
from jax.experimental import pallas as pl
from jax.experimental.pallas import tpu as pltpu
from jax.sharding import PartitionSpec as P

ITERS = 12
PART_DEV = 512
ROWS = 16
RHS = 15
LATE = 4
PAD = 8
LOW = 64
F32 = jnp.float32


def gram_map():
    s = ITERS
    n = 2 * s

    def unit(at):
        out = np.zeros(n)
        out[at] = 1.0
        return out

    m = []
    for k in range(s):
        m.append(2 * unit(2 * k) - unit(0))
        m.append(2 * unit(2 * k + 1) - unit(1))

    def entry(j, k):
        a, b = j + k, abs(j - k)
        return 0.5 * (
            m[a] - 0.5 * (m[a + 1] + m[abs(a - 1)]) + m[b] - 0.5 * (m[b + 1] + m[abs(b - 1)])
        )

    table = np.zeros((n, ROWS, 128))
    for j in range(s):
        table[:, j, RHS] = m[j]
        for k in range(s):
            table[:, j, k] = entry(j, k)
    extra = np.zeros((ROWS, 128))
    for i, m in enumerate(range(n - LATE, n)):
        extra[:, RHS + 1 + 2 * i : RHS + 3 + 2 * i] = table[m][:, s - 2 : s]
    return np.concatenate([table, extra[None]]).astype(np.float32)


def two_sum(a, b):
    s = a + b
    t = s - a
    return s, (a - (s - t)) + (b - t)


def quick_two_sum(a, b):
    s = a + b
    return s, b - (s - a)


def split(a):
    c = 4097.0 * a
    hi = c - (c - a)
    return hi, a - hi


def two_prod(a, b):
    p = a * b
    ah, al = split(a)
    bh, bl = split(b)
    return p, ((ah * bh - p) + ah * bl + al * bh) + al * bl


def dd_add(a, b):
    s, e = two_sum(a[0], b[0])
    return quick_two_sum(s, e + (a[1] + b[1]))


def loose_add(a, b):
    s, e = two_sum(a[0], b[0])
    return s, e + (a[1] + b[1])


def dd_mul(a, b):
    p, e = two_prod(a[0], b[0])
    return quick_two_sum(p, e + (a[0] * b[1] + a[1] * b[0]))


def dd_inverse(a):
    x = 1.0 / a[0]
    p, e = two_prod(a[0], x)
    r = (1.0 - p) - e - a[1] * x
    return quick_two_sum(x, x * r)


def dd_minus(a, b):
    return dd_add(a, (-b[0], -b[1]))


def dd_sum(terms):
    while len(terms) > 1:
        terms = [
            loose_add(terms[i], terms[i + 1]) if i + 1 < len(terms) else terms[i]
            for i in range(0, len(terms), 2)
        ]
    return quick_two_sum(*terms[0])


def lane_column(matrix, j):
    return tuple(jnp.broadcast_to(m[:, j : j + 1], m.shape) for m in matrix)


def full_row(matrix, j, rows=ROWS):
    return tuple(jnp.broadcast_to(m[j : j + 1, :], (rows, 128)) for m in matrix)


def weighted(table, every, numbers):
    terms = []
    for m in numbers:
        hi, lo = (jnp.broadcast_to(p[0:1, m : m + 1], (ROWS, 128)) for p in every)
        terms.append((table[m] * hi, table[m] * lo))
    return terms


def dd_eliminate(matrix, count):
    rows = lax.broadcasted_iota(jnp.int32, (ROWS, 128), 0)

    def eliminate(a, j, by, inverse):
        scaled = dd_mul(full_row(a, j), inverse)
        less = dd_minus(a, dd_mul(by, scaled))
        return tuple(jnp.where(rows == j, r, m) for r, m in zip(scaled, less))

    for j in range(0, count, 2):
        one, two = lane_column(matrix, j), lane_column(matrix, j + 1)
        inverse = dd_inverse(full_row(one, j))
        two = eliminate(two, j, one, inverse)
        matrix = eliminate(matrix, j, one, inverse)
        matrix = eliminate(matrix, j + 1, two, dd_inverse(full_row(two, j + 1)))
    return matrix


def dd_finish(table, early, reduced, every):
    u = ITERS - 2
    rows = lax.broadcasted_iota(jnp.int32, (ROWS, 128), 0)
    lanes = lax.broadcasted_iota(jnp.int32, (ROWS, 128), 1)
    last_two = (lanes == u) | (lanes == u + 1)
    late = range(2 * ITERS - LATE, 2 * ITERS)
    matrix = dd_sum([early] + weighted(table, every, late))
    terms = [reduced]
    for i, m in enumerate(late):
        value = tuple(
            jnp.where(last_two, jnp.broadcast_to(p[0:1, m : m + 1], (ROWS, 128)), 0.0) for p in every
        )
        moved = tuple(pltpu.roll(p, 128 - (RHS + 1 + 2 * i - u), 1) for p in reduced)
        terms.append(dd_mul(value, moved))
    x = dd_sum(terms)
    schur = []
    for a in range(2):
        product = dd_mul(lane_column(matrix, u + a), x)
        product = tuple(jnp.where(rows < u, p, 0.0) for p in product)
        total = dd_add(tuple(p[0:8, :] for p in product), tuple(p[8:16, :] for p in product))
        for shift in (4, 2, 1):
            total = dd_add(total, tuple(pltpu.roll(p, shift, 0) for p in total))
        schur.append(dd_minus(full_row(matrix, u + a, 8), total))
    (s00, s01, r0), (s10, s11, r1) = (
        [lane_column(row, j) for j in (u, u + 1, RHS)] for row in schur
    )
    over = dd_inverse(dd_minus(dd_mul(s00, s11), dd_mul(s01, s10)))
    c0 = dd_mul(dd_minus(dd_mul(r0, s11), dd_mul(r1, s01)), over)
    c1 = dd_mul(dd_minus(dd_mul(r1, s00), dd_mul(r0, s10)), over)
    rest = dd_minus(
        dd_minus(lane_column(x, RHS), dd_mul(lane_column(x, u), full_row(c0, 0))),
        dd_mul(lane_column(x, u + 1), full_row(c1, 0)),
    )
    return [full_row(rest, j, 8)[0] for j in range(u)] + [c0[0], c1[0]]


def partners(index, size):
    if size & (size - 1):
        return [lax.rem(index + m, size) for m in range(size)]
    out = [0]
    bit = 1
    while bit < size:
        same = lax.rem(index // bit, 2) * bit
        out = [o + same for o in out] + [o + (bit - same) for o in out]
        bit *= 2
    return out


def flipped(index, m, size):
    if size & (size - 1):
        return lax.rem(index + m, size)
    out, bit = 0, 1
    while bit < size:
        out = out + lax.rem(index // bit + m // bit, 2) * bit
        bit *= 2
    return out


def last_kernel(found, sums, out, particle, sems):
    pieces = [
        pltpu.make_async_copy(found, out, sems.at[0]),
        pltpu.make_async_copy(sums, particle, sems.at[1]),
    ]
    for copy in pieces:
        copy.start()
    for copy in pieces:
        copy.wait()


def kernel(
    sizes, source_hbm, phase_hbm, potential_hbm, map_hbm, places_hbm, count_hbm, target_hbm,
    out, particle,
    source, phase, potential, table, lines, voxel, places, count, target, vecs, diag, inv, base, slope, ybuf, hin,
    pinv, hinv, hodd, mask, dots, mine, parts, pick0, pick1, flat, sent, got, tally,
    isem, xsend, ysend, csend, hrecv, vsend, vrecv, rsend, rrecv, lsend, lrecv,
):
    n_gx, n_gy = sizes
    total = n_gx * n_gy
    cx, cy, cz = source_hbm.shape
    tiles = cz // 128
    pitch = cy + PAD
    block = (cx + 4) * pitch
    s = ITERS
    cycles = s // 2
    gx, gy = lax.axis_index("gx"), lax.axis_index("gy")
    me = gx * n_gy + gy
    mesh_id = pl.DeviceIdType.MESH

    barrier = pltpu.get_barrier_semaphore()

    gy_of = partners(gy, n_gy)
    gx_of = partners(gx, n_gx)

    def everyone(act):
        for m in reversed(range(n_gy)):
            for q in reversed(range(n_gx)):
                if m or q:
                    act(gx_of[q], gy_of[m])


    loads = []
    for c in range(tiles):
        for src, dst in (
            (potential_hbm, potential), (phase_hbm, phase), (source_hbm, source)
        ):
            loads.append(
                pltpu.make_async_copy(
                    src.at[:, :, pl.ds(128 * c, 128)], dst.at[c], isem.at[c]
                )
            )
    extra = [
        pltpu.make_async_copy(map_hbm, table, isem.at[tiles]),
        pltpu.make_async_copy(places_hbm, places, isem.at[tiles]),
        pltpu.make_async_copy(count_hbm, count, isem.at[tiles + 1]),
        pltpu.make_async_copy(target_hbm, target, isem.at[tiles]),
    ]
    for copy in loads[:3]:
        copy.start()
    everyone(
        lambda to_gx, to_gy: pl.semaphore_signal(
            barrier, inc=1, device_id=(to_gx, to_gy), device_id_type=mesh_id
        )
    )
    for copy in loads[3:] + extra:
        copy.start()

    has_up, has_down = gx < n_gx - 1, gx > 0
    has_right, has_left = gy < n_gy - 1, gy > 0
    up_gx, down_gx = jnp.minimum(gx + 1, n_gx - 1), jnp.maximum(gx - 1, 0)
    right_gy, left_gy = jnp.minimum(gy + 1, n_gy - 1), jnp.maximum(gy - 1, 0)

    def row(x, c, y):
        return c * block + (x + 2) * pitch + PAD + y

    def inv_row(x, c, y):
        return (c * (cx + 2) + x + 1) * cy + y

    def flat_row(x, c, y):
        return (c * cx + x) * cy + y

    def drained(rows, sem):
        ref = vecs.at[0, pl.ds(0, rows), :]
        pltpu.make_async_copy(ref, ref, sem).wait()

    def counts(one, other, size):
        if size < 3:
            return [(size - 1, None)]
        both = one & other
        return [(1, jnp.logical_not(both)), (2, both)]

    x_counts = counts(has_up, has_down, n_gx)
    y_counts = counts(has_right, has_left, n_gy)

    def taken(sem, rows):
        for a, so_many_x in x_counts:
            for b, so_many_y in y_counts:
                if not rows(a, b):
                    continue
                there = [t for t in (so_many_x, so_many_y) if t is not None]
                if there:
                    pl.when(functools.reduce(jnp.logical_and, there))(
                        functools.partial(drained, rows(a, b), sem)
                    )
                else:
                    drained(rows(a, b), sem)

    near, low_corner, high_corner = cx, 2 * cx + 1, 2 * cx
    zeros8 = jnp.zeros((8, 128), F32)
    zero_row = jnp.zeros((1, 128), F32)

    sides = ((0, 0, 1), (1, cy - 1, cy - 2))

    def pack_rows(j, c):
        k = 2 * j + 1
        for side, y1, y2 in sides:
            for x in range(0, cx, 8):
                ybuf[j, c, side, pl.ds(near + x, 8), :] = (
                    vecs[k, pl.ds(row(x, c, y1), 8, stride=pitch), :]
                )
                ybuf[j, c, side, pl.ds(x, 8), :] = vecs[k, pl.ds(row(x, c, y2), 8, stride=pitch), :]

    def xcopy(j, c, way, layer):
        up = way == 0
        return pltpu.make_async_remote_copy(
            src_ref=vecs.at[2 * j + 1, pl.ds(row(cx - 1 - layer if up else layer, c, 0), cy), :],
            dst_ref=vecs.at[2 * j + 1, pl.ds(row(-1 - layer if up else cx + layer, c, 0), cy), :],
            send_sem=xsend.at[way], recv_sem=hrecv.at[lax.rem(j, 2), c, layer],
            device_id=(up_gx if up else down_gx, gy), device_id_type=mesh_id,
        )

    def ycopy(j, c, way):
        right = way == 0
        return pltpu.make_async_remote_copy(
            src_ref=ybuf.at[j, c, 1 if right else 0],
            dst_ref=hin.at[j, c, 0 if right else 1, pl.ds(0, 2 * cx), :],
            send_sem=ysend.at[way], recv_sem=hrecv.at[lax.rem(j, 2), c, 0],
            device_id=(gx, right_gy if right else left_gy), device_id_type=mesh_id,
        )

    def ccopy(j, c, xway, yway):
        up, right = xway == 0, yway == 0
        q = 2 * xway + yway
        return pltpu.make_async_remote_copy(
            src_ref=vecs.at[
                2 * j + 1, pl.ds(row(cx - 1 if up else 0, c, cy - 1 if right else 0), 1), :
            ],
            dst_ref=hin.at[j, c, 0 if right else 1, pl.ds(low_corner if up else high_corner, 1), :],
            send_sem=csend.at[q], recv_sem=hrecv.at[lax.rem(j, 2), c, 1],
            device_id=(up_gx if up else down_gx, right_gy if right else left_gy),
            device_id_type=mesh_id,
        )

    def vcopy(c, way):
        up = way == 0
        return pltpu.make_async_remote_copy(
            src_ref=inv.at[pl.ds(inv_row(cx - 1 if up else 0, c, 0), cy), :],
            dst_ref=inv.at[pl.ds(inv_row(-1 if up else cx, c, 0), cy), :],
            send_sem=vsend.at[way], recv_sem=vrecv.at[c],
            device_id=(up_gx if up else down_gx, gy), device_id_type=mesh_id,
        )

    def hcopy(way):
        right = way == 0
        return pltpu.make_async_remote_copy(
            src_ref=pinv.at[1 if right else 0], dst_ref=hinv.at[0 if right else 1],
            send_sem=vsend.at[2 + way], recv_sem=vrecv.at[tiles],
            device_id=(gx, right_gy if right else left_gy), device_id_type=mesh_id,
        )

    for c in range(tiles):
        drained(3 * cx * cy, isem.at[c])

        @pl.loop(0, cx)
        def _(x):
            found = []
            for y in range(0, cy, 8):
                at = potential[c, x, y : y + 8, :]
                rising = jnp.exp(0.4 * at)
                falling = jnp.exp(-0.6 * at)
                label = phase[c, x, y : y + 8, :]
                rate = jnp.where(label == 1, 0.3, jnp.where(label == 2, 0.08, 0.02)).astype(F32)
                bend = 0.4 * rising + 0.6 * falling
                d = 6.0 + rate * bend
                i = 1.0 / d
                found.append((y, rising - falling, bend, d, i, source[c, x, y : y + 8, :] * i))
            for y, level, bend, d, i, v in found:
                f = pl.ds(flat_row(x, c, y), 8)
                base[f, :] = level
                slope[f, :] = bend
                diag[f, :] = d
                inv[pl.ds(inv_row(x, c, y), 8), :] = i
                vecs[1, pl.ds(row(x, c, y), 8), :] = v

        pack_rows(0, c)
        for side, y, _ in sides:
            for x in range(0, cx, 8):
                pinv[side, c, pl.ds(x, 8), :] = inv[pl.ds(inv_row(x, c, y), 8, stride=cy), :]

    def launch_x(j, c, more):
        for way, there in ((0, has_up), (1, has_down)):
            @pl.when(there & more)
            def _():
                pl.when(has_right)(ccopy(j, c, way, 0).start)
                pl.when(has_left)(ccopy(j, c, way, 1).start)
                xcopy(j, c, way, 0).start()
                xcopy(j, c, way, 1).start()

    def launch_y(j, c, more):
        pl.when(has_right & more)(ycopy(j, c, 0).start)
        pl.when(has_left & more)(ycopy(j, c, 1).start)

    def landed_near(j, c):
        taken(hrecv.at[lax.rem(j, 2), c, 0], lambda a, b: a * cy + b * 2 * cx)

    def landed_far(j, c):
        taken(hrecv.at[lax.rem(j, 2), c, 1], lambda a, b: a * (cy + b))

        @pl.when(j == 0)
        def _():
            taken(vrecv.at[c], lambda a, b: a * cy)

    with jax.named_scope("barrier"):
        pl.semaphore_wait(barrier, total - 1)

    always = gx >= 0
    pl.when(has_right)(hcopy(0).start)
    pl.when(has_left)(hcopy(1).start)
    for c in range(tiles):
        launch_x(0, c, always)
        launch_y(0, c, always)
        pl.when(has_up)(vcopy(c, 0).start)
        pl.when(has_down)(vcopy(c, 1).start)

    groups = places.shape[0]
    wide = groups // n_gy
    drained(table.shape[0] * ROWS + 2 * groups, isem.at[tiles])
    pltpu.make_async_copy(count_hbm, count, isem.at[tiles + 1]).wait()
    lines[...] = places[...] >> 7
    scalar_lines = pltpu.make_async_copy(lines, voxel, isem.at[tiles + 2])
    scalar_lines.start()

    @pl.loop(-1, cx + 1)
    def _(x):
        for c in range(tiles):
            for y in range(0, cy, 8):
                vecs[0, pl.ds(row(x, c, y), 8), :] = zeros8

    @pl.loop(0, cycles)
    def _(j):
        @pl.loop(0, cx + 1)
        def _(x):
            for c in range(tiles):
                vecs[2 * j + 1, pl.ds(row(x, c, -PAD), 8), :] = zeros8

    hodd[...] = jnp.zeros(hodd.shape, F32)
    for beyond, x in ((gx == 0, -1), (gx == n_gx - 1, cx)):
        @pl.when(beyond)
        def _():
            for c in range(tiles):
                for y in range(0, cy, 8):
                    inv[pl.ds(inv_row(x, c, y), 8), :] = zeros8

            @pl.loop(0, cycles)
            def _(j):
                for c in range(tiles):
                    first = row(-2 if x < 0 else cx, c, 0)
                    for y in range(0, pitch + cy, 8):
                        vecs[2 * j + 1, pl.ds(first + y, 8), :] = zeros8
                    for side in range(2):
                        hin[j, c, side, pl.ds(low_corner if x < 0 else high_corner, 1), :] = zero_row

    for beyond, side in ((gy == 0, 0), (gy == n_gy - 1, 1)):
        @pl.when(beyond)
        def _():
            hinv[side] = jnp.zeros(hinv.shape[1:], F32)

            @pl.loop(0, cycles)
            def _(j):
                for c in range(tiles):
                    hin[j, c, side] = jnp.zeros(hin.shape[3:], F32)

    def build_masks():
        @pl.loop(0, n_gy)
        def _(peer):
            live = count[peer]
            lanes = lax.broadcasted_iota(jnp.int32, (128, 128), 1)
            rows = lax.broadcasted_iota(jnp.int32, (128, 128), 0)
            for part in range(wide):
                at = (places[pl.ds(peer * wide + part, 1), :] & 127).astype(F32)
                at = jnp.broadcast_to(at, (128, 128)).T
                mask[peer * wide + part] = jnp.where(
                    (lanes.astype(F32) == at) & (rows + 128 * part < live), 0.5, 0.0
                )

    lane8 = lax.broadcasted_iota(jnp.int32, (8, 128), 1)
    sub8 = lax.broadcasted_iota(jnp.int32, (8, 128), 0)
    first_lane, last_lane = lane8 == 0, lane8 == 127

    def beside(v, before, after):
        z = pltpu.roll(jnp.where(last_lane, before, v), 1, 1)
        return z + pltpu.roll(jnp.where(first_lane, after, v), 127, 1)

    def sweep(k, runs, scale, carry, more=lambda: ()):
        centers = {}

        def center(run, c, start, o, y):
            if (run, o, y) not in centers:
                centers[run, o, y] = vecs[k, pl.ds(row(start + o, c, y), 8), :]
            return centers[run, o, y]

        found = []
        for run, (c, start, offsets, counted) in enumerate(runs):
            for y in range(0, cy, 8):
                for o in offsets:
                    r = row(start + o, c, y)
                    v = center(run, c, start, o, y)
                    before = vecs[k, pl.ds(r - block, 8), :] if c > 0 else 0.0
                    after = vecs[k, pl.ds(r + block, 8), :] if c < tiles - 1 else 0.0
                    n = vecs[k, pl.ds(r - 1, 8), :] + vecs[k, pl.ds(r + 1, 8), :]
                    n = n + (center(run, c, start, o - 1, y) + center(run, c, start, o + 1, y))
                    n = n + beside(v, before, after)
                    i = inv[pl.ds(inv_row(start + o, c, y), 8), :]
                    new = (scale * i) * n - vecs[k - 1, pl.ds(r, 8), :]
                    if counted:
                        w = diag[pl.ds(flat_row(start + o, c, y), 8), :] * v
                        carry = (carry[0] + w * v, carry[1] + w * new)
                    found.append((r, new))
        others = more()
        for r, new in found:
            vecs[k + 1, pl.ds(r, 8), :] = new
        for store in others:
            store()
        return carry

    def inner(k, c, first, last, scale, carry):
        group = max(g for g in range(1, 8) if (last - first) % g == 0)

        def some(i, a):
            return sweep(k, [(c, group * i + first, range(group), True)], scale, a)

        return lax.fori_loop(0, (last - first) // group, some, carry)

    def rows_beyond(j, c, scale):
        k = 2 * j + 1
        stores = []
        for side, beyond in ((0, -1), (1, cy)):
            for x in range(0, cx, 8):
                at = pl.ds(near + x, 8)
                h = hin[j, c, side, at, :]
                before = hin[j, c - 1, side, at, :] if c > 0 else 0.0
                after = hin[j, c + 1, side, at, :] if c < tiles - 1 else 0.0
                lower = hin[j, c, side, pl.ds(near + x - 1, 8), :]
                if x == 0:
                    corner = hin[j, c, side, pl.ds(low_corner, 1), :]
                    lower = jnp.where(sub8 == 0, corner, lower)
                upper = hin[j, c, side, pl.ds(near + x + 1, 8), :]
                n = (lower + upper) + (hin[j, c, side, pl.ds(x, 8), :] + ybuf[j, c, side, at, :])
                n = n + beside(h, before, after)
                old = pl.ds(x, 8)
                new = (scale * hinv[side, c, old, :]) * n - hodd[side, c, old, :]

                def store(side=side, old=old, new=new, line=row(x, c, beyond)):
                    hodd[side, c, old, :] = new
                    vecs[k + 1, pl.ds(line, 8, stride=pitch), :] = new

                stores.append(store)
        return stores

    def outside(j, border, shell, scale, carry):
        k = 2 * j + 1
        runs, more = [], lambda: ()
        if border is not None:
            runs += [(border, 0, (0,), True), (border, cx - 1, (0,), True)]
        if shell is not None:
            for side, y in ((0, -1), (1, cy)):
                for x, at in ((-1, low_corner), (cx, high_corner)):
                    vecs[k, pl.ds(row(x, shell, y), 1), :] = hin[j, shell, side, pl.ds(at, 1), :]
            runs += [(shell, -1, (0,), False), (shell, cx, (0,), False)]
            more = functools.partial(rows_beyond, j, shell, scale)
        carry = sweep(k, runs, scale, carry, more)
        if border is None:
            return carry
        own, cross = carry
        found = []
        for side, y, _ in sides:
            for x in range(0, cx, 8):
                at = pl.ds(near + x, 8)
                h = hin[j, border, side, at, :]
                line = pl.ds(row(x, border, y), 8, stride=pitch)
                fixed = vecs[k + 1, line, :] + (scale * pinv[side, border, pl.ds(x, 8), :]) * h
                cross = cross + (scale * ybuf[j, border, side, at, :]) * h
                found.append((line, fixed))
        for line, fixed in found:
            vecs[k + 1, line, :] = fixed
        return own, cross

    def finish(j, c, carry):
        k = 2 * j + 2
        more = j < cycles - 1
        carry = sweep(k, [(c, 0, (0, 1), True), (c, cx - 2, (0, 1), True)], 2.0, carry)
        launch_x(j + 1, c, more)
        carry = inner(k, c, 2, cx - 2, 2.0, carry)

        @pl.when(more)
        def _():
            pack_rows(j + 1, c)
            launch_y(j + 1, c, always)

        return carry

    def local_sums(numbers):
        sums = []
        for g in numbers:
            level = [dots[pl.ds(64 * g + i, 8, stride=8), :] for i in range(8)]
            level = [two_sum(level[2 * i], level[2 * i + 1]) for i in range(4)]
            sums.append(dd_sum(level))
        for shift in (64, 32, 16, 8, 4, 2, 1):
            sums = [
                loose_add(a, tuple(pltpu.roll(p, shift, 1) for p in a)) for a in sums
            ]
        sums = [quick_two_sum(*a) for a in sums]
        spread = zeros8
        for g, (hi, lo) in zip(numbers, sums):
            spread = jnp.where(lane8 == sub8 + 8 * g, hi, spread)
            spread = jnp.where(lane8 == sub8 + 8 * g + LOW, lo, spread)
        return jnp.sum(spread, axis=0, keepdims=True)

    def share(which, line):
        mine[which] = line
        parts[which, pl.ds(me, 1), :] = line
        everyone(
            lambda to_gx, to_gy: pltpu.make_async_remote_copy(
                src_ref=mine.at[which], dst_ref=parts.at[which, pl.ds(me, 1), :],
                send_sem=rsend, recv_sem=rrecv.at[which],
                device_id=(to_gx, to_gy), device_id_type=mesh_id,
            ).start()
        )

    def shared(which):
        drained(total - 1, rrecv.at[which])
        level = [parts[which, 8 * i : 8 * i + 8, :] for i in range(total // 8)]
        every = dd_sum([(a, pltpu.roll(a, 128 - LOW, 1)) for a in level])
        for shift in (4, 2, 1):
            every = loose_add(every, tuple(pltpu.roll(p, shift, 0) for p in every))
        return quick_two_sum(*every)

    numbers = range(2 * s // 8)
    late_group = (2 * s - LATE) // 8
    dots[pl.ds(8 * (2 * s - LATE), 8 * LATE), :] = jnp.zeros((8 * LATE, 128), F32)

    @pl.loop(0, cycles)
    def _(j):
        with jax.named_scope("cycle"):
            scale = jnp.where(j == 0, 1.0, 2.0).astype(F32)
            first = second = (zeros8, zeros8)
            with jax.named_scope("ainner"):
                for c in range(tiles):
                    first = inner(2 * j + 1, c, 1, cx - 1, scale, first)

            pl.when(j == 0)(build_masks)

            @pl.when(j == cycles - 1)
            def _():
                share(0, local_sums(numbers))

            @pl.when(j == 0)
            def _():
                taken(vrecv.at[tiles], lambda a, b: b * tiles * cx)

            with jax.named_scope("landed"):
                landed_near(j, 0)
            first = outside(j, 0, None, scale, first)
            for c in range(tiles):
                following = c + 1 if c + 1 < tiles else None
                with jax.named_scope("landed"):
                    if following is not None:
                        landed_near(j, following)
                    landed_far(j, c)
                first = outside(j, following, c, scale, first)
                second = finish(j, c, second)
            for i, value in enumerate((*first, *second)):
                dots[pl.ds(pl.multiple_of(32 * j + 8 * i, 8), 8), :] = value

    scalar_lines.wait()

    with jax.named_scope("reduce"):
        share(1, local_sums(numbers[late_group:]))

        for way, there in ((0, has_up), (1, has_down)):
            @pl.when(there)
            def _():
                drained(cycles * tiles * 2 * cy, xsend.at[way])
                drained(tiles * cy, vsend.at[way])
                for q, also in ((0, has_right), (1, has_left)):
                    @pl.when(also)
                    def _():
                        drained(cycles * tiles, csend.at[2 * way + q])

        for way, there in ((0, has_right), (1, has_left)):
            @pl.when(there)
            def _():
                drained(cycles * tiles * 2 * cx, ysend.at[way])
                drained(tiles * cx, vsend.at[2 + way])

        early = dd_sum(weighted(table, shared(0), range(2 * s - LATE)))
        reduced = dd_eliminate((early[0] + table[2 * s], early[1]), s - 2)

    with jax.named_scope("solve"):
        weights = dd_finish(table, early, reduced, shared(1))

    with jax.named_scope("combine"):
        @pl.loop(0, cx)
        def _(x):
            for c in range(tiles):
                for y in range(0, cy, 8):
                    pieces = [
                        w * vecs[1 + k, pl.ds(row(x, c, y), 8), :] for k, w in enumerate(weights)
                    ]
                    while len(pieces) > 1:
                        pieces = [sum(pieces[i : i + 2]) for i in range(0, len(pieces), 2)]
                    out[x, y : y + 8, 128 * c : 128 * (c + 1)] = pieces[0]
                    f = pl.ds(flat_row(x, c, y), 8)
                    at = (x * cy + y) * tiles + c
                    flat[pl.ds(at, 8, stride=tiles), :] = base[f, :] + slope[f, :] * pieces[0]

    picks = (pick0, pick1)

    def fetch(peer, pick):
        for part in range(wide):
            for i in range(128):
                pick[pl.ds(128 * part + i, 1), :] = flat[pl.ds(voxel[peer * wide + part, i], 1), :]

    def pass_on(peer, pick):
        for part in range(wide):
            value = pick[128 * part : 128 * (part + 1), :] * mask[peer * wide + part]
            sent[peer, pl.ds(part, 1), :] = jnp.sum(value.T, axis=0, keepdims=True)

    def give(peer):
        pltpu.make_async_remote_copy(
            src_ref=sent.at[peer], dst_ref=got.at[gy], send_sem=lsend, recv_sem=lrecv.at[gy],
            device_id=(gx, peer), device_id_type=mesh_id,
        ).start()

    def peer_at(step):
        return flipped(gy, n_gy - 1 - step, n_gy)

    with jax.named_scope("gather"):
        fetch(peer_at(0), picks[0])

        @pl.loop(0, n_gy // 2 - 2)
        def _(i):
            pass_on(peer_at(2 * i), picks[0])
            fetch(peer_at(2 * i + 1), picks[1])
            give(peer_at(2 * i))
            pass_on(peer_at(2 * i + 1), picks[1])
            fetch(peer_at(2 * i + 2), picks[0])
            give(peer_at(2 * i + 1))

        pass_on(peer_at(n_gy - 4), picks[0])
        fetch(peer_at(n_gy - 3), picks[1])
        give(peer_at(n_gy - 4))
        pass_on(peer_at(n_gy - 3), picks[1])
        give(peer_at(n_gy - 3))
        fetch(peer_at(n_gy - 2), picks[0])
        pass_on(peer_at(n_gy - 2), picks[0])
        give(peer_at(n_gy - 2))
        fetch(gy, picks[1])
        pass_on(gy, picks[1])
        got[gy] = sent[gy]

    own = tally.shape[0]

    def tallied(peer, first):
        spots = [target[pl.ds(peer * wide + part, 1), :] for part in range(wide)]
        values = [got[peer, part : part + 1, :] for part in range(wide)]
        for start in range(0, own, 128):
            found = []
            for r in range(start, start + 128, 8):
                total_ = zeros8 if first else tally[r : r + 8, :]
                for spot, value in zip(spots, values):
                    total_ = total_ + jnp.where(spot == sub8 + r, value, 0.0)
                found.append((r, total_))
            for r, total_ in found:
                tally[r : r + 8, :] = total_

    with jax.named_scope("links"):
        tallied(gy, True)
        drained(2 * (total - 1), rsend)

        @pl.loop(0, n_gy - 1)
        def _(step):
            peer = flipped(gy, n_gy - 1 - step, n_gy)
            pltpu.make_async_copy(got.at[peer], got.at[peer], lrecv.at[peer]).wait()
            tallied(peer, False)

        for start in range(0, own, 128):
            particle[0, :, start : start + 128] = jnp.sum(
                tally[start : start + 128, :].T, axis=0, keepdims=True
            )
        drained((n_gy - 1) * wide, lsend)


def kept(x):
    return pltpu.with_memory_space_constraint(x, pltpu.HBM)


def shards(sizes, source, voxel_phase, lin_potential, link_voxel, link_count, link_target):
    cx, cy, cz = source.shape
    total = sizes[0] * sizes[1]
    s = ITERS
    tiles = cz // 128
    voxels = cx * cy * tiles
    padded = (cx + 4) * tiles * (cy + PAD) + 8
    cycles = s // 2
    places = link_voxel[0, 0].reshape(-1, 128)
    peers = link_count.shape[2]
    slots = link_voxel.shape[2]
    groups = slots // 128
    whole = pl.BlockSpec(memory_space=pltpu.VMEM)
    far = pl.BlockSpec(memory_space=pltpu.HBM)
    found, sums = pl.pallas_call(
        functools.partial(kernel, sizes),
        out_shape=(
            jax.ShapeDtypeStruct(source.shape, F32),
            jax.ShapeDtypeStruct((1, 1, PART_DEV), F32),
        ),
        in_specs=[far] * 7,
        out_specs=(whole, whole),
        scratch_shapes=[
            pltpu.VMEM((tiles, cx, cy, 128), F32),
            pltpu.VMEM((tiles, cx, cy, 128), jnp.int32),
            pltpu.VMEM((tiles, cx, cy, 128), F32),
            pltpu.VMEM((2 * s + 1, ROWS, 128), F32),
            pltpu.VMEM((groups, 128), jnp.int32),
            pltpu.SMEM((groups, 128), jnp.int32),
            pltpu.VMEM((groups, 128), jnp.int32),
            pltpu.SMEM((peers,), jnp.int32),
            pltpu.VMEM((groups, 128), jnp.int32),
            pltpu.VMEM((s + 2, padded, 128), F32),
            pltpu.VMEM((voxels, 128), F32),
            pltpu.VMEM((tiles * (cx + 2) * cy, 128), F32),
            pltpu.VMEM((voxels, 128), F32),
            pltpu.VMEM((voxels, 128), F32),
            pltpu.VMEM((cycles, tiles, 2, 2 * cx, 128), F32),
            pltpu.VMEM((cycles, tiles, 2, 2 * cx + 8, 128), F32),
            pltpu.VMEM((2, tiles, cx, 128), F32),
            pltpu.VMEM((2, tiles, cx, 128), F32),
            pltpu.VMEM((2, tiles, cx, 128), F32),
            pltpu.VMEM((groups, 128, 128), F32),
            pltpu.VMEM((2 * s * 8, 128), F32),
            pltpu.VMEM((2, 1, 128), F32),
            pltpu.VMEM((2, total, 128), F32),
            pltpu.VMEM((groups // peers * 128, 128), F32),
            pltpu.VMEM((groups // peers * 128, 128), F32),
            pltpu.VMEM((voxels, 128), F32),
            pltpu.VMEM((peers, groups // peers, 128), F32),
            pltpu.VMEM((peers, groups // peers, 128), F32),
            pltpu.VMEM((PART_DEV, 128), F32),
            pltpu.SemaphoreType.DMA((tiles + 3,)),
            pltpu.SemaphoreType.DMA((2,)),
            pltpu.SemaphoreType.DMA((2,)),
            pltpu.SemaphoreType.DMA((4,)),
            pltpu.SemaphoreType.DMA((2, tiles, 2)),
            pltpu.SemaphoreType.DMA((4,)),
            pltpu.SemaphoreType.DMA((tiles + 1,)),
            pltpu.SemaphoreType.DMA,
            pltpu.SemaphoreType.DMA((2,)),
            pltpu.SemaphoreType.DMA,
            pltpu.SemaphoreType.DMA((peers,)),
        ],
        compiler_params=pltpu.CompilerParams(
            collective_id=0, has_side_effects=True, vmem_limit_bytes=52 * 2**20
        ),
    )(
        kept(source), kept(voxel_phase), kept(lin_potential), kept(jnp.asarray(gram_map())),
        kept(places), kept(link_count[0, 0]), kept(link_target[0, 0].reshape(groups, 128)),
    )
    return pl.pallas_call(
        last_kernel,
        out_shape=(
            jax.ShapeDtypeStruct(source.shape, F32),
            jax.ShapeDtypeStruct((1, 1, PART_DEV), F32),
        ),
        in_specs=[pl.BlockSpec(memory_space=pl.ANY)] * 2,
        out_specs=(far, far),
        scratch_shapes=[pltpu.SemaphoreType.DMA((2,))],
        compiler_params=pltpu.CompilerParams(vmem_limit_bytes=2 * 2**20),
    )(found, sums)


def solution(mesh):
    spec = P("gx", "gy", None)
    return jax.shard_map(
        functools.partial(shards, (mesh.shape["gx"], mesh.shape["gy"])),
        mesh=mesh,
        in_specs=(spec,) * 6,
        out_specs=(spec, spec),
        check_vma=False,
    )
```

```python
import functools

import jax
import jax.numpy as jnp
import numpy as np
from jax import lax
from jax.experimental import pallas as pl
from jax.experimental.pallas import tpu as pltpu
from jax.sharding import PartitionSpec as P

ITERS = 12
PART_DEV = 512
ROWS = 16
RHS = 15
LATE = 4
PAD = 8
LOW = 64
F32 = jnp.float32


def gram_map():
    s = ITERS
    n = 2 * s

    def unit(at):
        out = np.zeros(n)
        out[at] = 1.0
        return out

    m = []
    for k in range(s):
        m.append(2 * unit(2 * k) - unit(0))
        m.append(2 * unit(2 * k + 1) - unit(1))

    def entry(j, k):
        a, b = j + k, abs(j - k)
        return 0.5 * (
            m[a] - 0.5 * (m[a + 1] + m[abs(a - 1)]) + m[b] - 0.5 * (m[b + 1] + m[abs(b - 1)])
        )

    table = np.zeros((n, ROWS, 128))
    for j in range(s):
        table[:, j, RHS] = m[j]
        for k in range(s):
            table[:, j, k] = entry(j, k)
    extra = np.zeros((ROWS, 128))
    for i, m in enumerate(range(n - LATE, n)):
        extra[:, RHS + 1 + 2 * i : RHS + 3 + 2 * i] = table[m][:, s - 2 : s]
    return np.concatenate([table, extra[None]]).astype(np.float32)


def two_sum(a, b):
    s = a + b
    t = s - a
    return s, (a - (s - t)) + (b - t)


def quick_two_sum(a, b):
    s = a + b
    return s, b - (s - a)


def split(a):
    c = 4097.0 * a
    hi = c - (c - a)
    return hi, a - hi


def two_prod(a, b):
    p = a * b
    ah, al = split(a)
    bh, bl = split(b)
    return p, ((ah * bh - p) + ah * bl + al * bh) + al * bl


def dd_add(a, b):
    s, e = two_sum(a[0], b[0])
    return quick_two_sum(s, e + (a[1] + b[1]))


def loose_add(a, b):
    s, e = two_sum(a[0], b[0])
    return s, e + (a[1] + b[1])


def dd_mul(a, b):
    p, e = two_prod(a[0], b[0])
    return quick_two_sum(p, e + (a[0] * b[1] + a[1] * b[0]))


def dd_inverse(a):
    x = 1.0 / a[0]
    p, e = two_prod(a[0], x)
    r = (1.0 - p) - e - a[1] * x
    return quick_two_sum(x, x * r)


def dd_minus(a, b):
    return dd_add(a, (-b[0], -b[1]))


def dd_sum(terms):
    while len(terms) > 1:
        terms = [
            loose_add(terms[i], terms[i + 1]) if i + 1 < len(terms) else terms[i]
            for i in range(0, len(terms), 2)
        ]
    return quick_two_sum(*terms[0])


def lane_column(matrix, j):
    return tuple(jnp.broadcast_to(m[:, j : j + 1], m.shape) for m in matrix)


def full_row(matrix, j, rows=ROWS):
    return tuple(jnp.broadcast_to(m[j : j + 1, :], (rows, 128)) for m in matrix)


def weighted(table, every, numbers):
    terms = []
    for m in numbers:
        hi, lo = (jnp.broadcast_to(p[0:1, m : m + 1], (ROWS, 128)) for p in every)
        terms.append((table[m] * hi, table[m] * lo))
    return terms


def dd_eliminate(matrix, count):
    rows = lax.broadcasted_iota(jnp.int32, (ROWS, 128), 0)

    def eliminate(a, j, by, inverse):
        scaled = dd_mul(full_row(a, j), inverse)
        less = dd_minus(a, dd_mul(by, scaled))
        return tuple(jnp.where(rows == j, r, m) for r, m in zip(scaled, less))

    for j in range(0, count, 2):
        one, two = lane_column(matrix, j), lane_column(matrix, j + 1)
        inverse = dd_inverse(full_row(one, j))
        two = eliminate(two, j, one, inverse)
        matrix = eliminate(matrix, j, one, inverse)
        matrix = eliminate(matrix, j + 1, two, dd_inverse(full_row(two, j + 1)))
    return matrix


def dd_finish(table, early, reduced, every):
    u = ITERS - 2
    rows = lax.broadcasted_iota(jnp.int32, (ROWS, 128), 0)
    lanes = lax.broadcasted_iota(jnp.int32, (ROWS, 128), 1)
    last_two = (lanes == u) | (lanes == u + 1)
    late = range(2 * ITERS - LATE, 2 * ITERS)
    matrix = dd_sum([early] + weighted(table, every, late))
    terms = [reduced]
    for i, m in enumerate(late):
        value = tuple(
            jnp.where(last_two, jnp.broadcast_to(p[0:1, m : m + 1], (ROWS, 128)), 0.0) for p in every
        )
        moved = tuple(pltpu.roll(p, 128 - (RHS + 1 + 2 * i - u), 1) for p in reduced)
        terms.append(dd_mul(value, moved))
    x = dd_sum(terms)
    schur = []
    for a in range(2):
        product = dd_mul(lane_column(matrix, u + a), x)
        product = tuple(jnp.where(rows < u, p, 0.0) for p in product)
        total = dd_add(tuple(p[0:8, :] for p in product), tuple(p[8:16, :] for p in product))
        for shift in (4, 2, 1):
            total = dd_add(total, tuple(pltpu.roll(p, shift, 0) for p in total))
        schur.append(dd_minus(full_row(matrix, u + a, 8), total))
    (s00, s01, r0), (s10, s11, r1) = (
        [lane_column(row, j) for j in (u, u + 1, RHS)] for row in schur
    )
    over = dd_inverse(dd_minus(dd_mul(s00, s11), dd_mul(s01, s10)))
    c0 = dd_mul(dd_minus(dd_mul(r0, s11), dd_mul(r1, s01)), over)
    c1 = dd_mul(dd_minus(dd_mul(r1, s00), dd_mul(r0, s10)), over)
    rest = dd_minus(
        dd_minus(lane_column(x, RHS), dd_mul(lane_column(x, u), full_row(c0, 0))),
        dd_mul(lane_column(x, u + 1), full_row(c1, 0)),
    )
    return [full_row(rest, j, 8)[0] for j in range(u)] + [c0[0], c1[0]]


def partners(index, size):
    if size & (size - 1):
        return [lax.rem(index + m, size) for m in range(size)]
    out = [0]
    bit = 1
    while bit < size:
        same = lax.rem(index // bit, 2) * bit
        out = [o + same for o in out] + [o + (bit - same) for o in out]
        bit *= 2
    return out


def flipped(index, m, size):
    if size & (size - 1):
        return lax.rem(index + m, size)
    out, bit = 0, 1
    while bit < size:
        out = out + lax.rem(index // bit + m // bit, 2) * bit
        bit *= 2
    return out


def last_kernel(found, sums, out, particle, sems):
    pieces = [
        pltpu.make_async_copy(found, out, sems.at[0]),
        pltpu.make_async_copy(sums, particle, sems.at[1]),
    ]
    for copy in pieces:
        copy.start()
    for copy in pieces:
        copy.wait()


def kernel(
    sizes, source_hbm, phase_hbm, potential_hbm, map_hbm, places_hbm, count_hbm, target_hbm,
    out, particle,
    source, phase, potential, table, lines, voxel, places, count, target, vecs, diag, inv, base, slope, ybuf, hin,
    pinv, hinv, hodd, mask, dots, mine, parts, pick0, pick1, flat, sent, got, tally,
    isem, xsend, ysend, csend, hrecv, vsend, vrecv, rsend, rrecv, lsend, lrecv,
):
    n_gx, n_gy = sizes
    total = n_gx * n_gy
    cx, cy, cz = source_hbm.shape
    tiles = cz // 128
    pitch = cy + PAD
    block = (cx + 4) * pitch
    s = ITERS
    cycles = s // 2
    gx, gy = lax.axis_index("gx"), lax.axis_index("gy")
    me = gx * n_gy + gy
    mesh_id = pl.DeviceIdType.MESH

    barrier = pltpu.get_barrier_semaphore()

    gy_of = partners(gy, n_gy)
    gx_of = partners(gx, n_gx)

    def everyone(act):
        for m in reversed(range(n_gy)):
            for q in reversed(range(n_gx)):
                if m or q:
                    act(gx_of[q], gy_of[m])


    loads = []
    for c in range(tiles):
        for src, dst in (
            (potential_hbm, potential), (phase_hbm, phase), (source_hbm, source)
        ):
            loads.append(
                pltpu.make_async_copy(
                    src.at[:, :, pl.ds(128 * c, 128)], dst.at[c], isem.at[c]
                )
            )
    extra = [
        pltpu.make_async_copy(map_hbm, table, isem.at[tiles]),
        pltpu.make_async_copy(places_hbm, places, isem.at[tiles]),
        pltpu.make_async_copy(count_hbm, count, isem.at[tiles + 1]),
        pltpu.make_async_copy(target_hbm, target, isem.at[tiles]),
    ]
    for copy in loads[:3]:
        copy.start()
    everyone(
        lambda to_gx, to_gy: pl.semaphore_signal(
            barrier, inc=1, device_id=(to_gx, to_gy), device_id_type=mesh_id
        )
    )
    for copy in loads[3:] + extra:
        copy.start()

    has_up, has_down = gx < n_gx - 1, gx > 0
    has_right, has_left = gy < n_gy - 1, gy > 0
    up_gx, down_gx = jnp.minimum(gx + 1, n_gx - 1), jnp.maximum(gx - 1, 0)
    right_gy, left_gy = jnp.minimum(gy + 1, n_gy - 1), jnp.maximum(gy - 1, 0)

    def row(x, c, y):
        return c * block + (x + 2) * pitch + PAD + y

    def inv_row(x, c, y):
        return (c * (cx + 2) + x + 1) * cy + y

    def flat_row(x, c, y):
        return (c * cx + x) * cy + y

    def drained(rows, sem):
        ref = vecs.at[0, pl.ds(0, rows), :]
        pltpu.make_async_copy(ref, ref, sem).wait()

    def counts(one, other, size):
        if size < 3:
            return [(size - 1, None)]
        both = one & other
        return [(1, jnp.logical_not(both)), (2, both)]

    x_counts = counts(has_up, has_down, n_gx)
    y_counts = counts(has_right, has_left, n_gy)

    def taken(sem, rows):
        for a, so_many_x in x_counts:
            for b, so_many_y in y_counts:
                if not rows(a, b):
                    continue
                there = [t for t in (so_many_x, so_many_y) if t is not None]
                if there:
                    pl.when(functools.reduce(jnp.logical_and, there))(
                        functools.partial(drained, rows(a, b), sem)
                    )
                else:
                    drained(rows(a, b), sem)

    near, low_corner, high_corner = cx, 2 * cx + 1, 2 * cx
    zeros8 = jnp.zeros((8, 128), F32)
    zero_row = jnp.zeros((1, 128), F32)

    sides = ((0, 0, 1), (1, cy - 1, cy - 2))

    def pack_rows(j, c):
        k = 2 * j + 1
        for side, y1, y2 in sides:
            for x in range(0, cx, 8):
                ybuf[j, c, side, pl.ds(near + x, 8), :] = (
                    vecs[k, pl.ds(row(x, c, y1), 8, stride=pitch), :]
                )
                ybuf[j, c, side, pl.ds(x, 8), :] = vecs[k, pl.ds(row(x, c, y2), 8, stride=pitch), :]

    def xcopy(j, c, way, layer):
        up = way == 0
        return pltpu.make_async_remote_copy(
            src_ref=vecs.at[2 * j + 1, pl.ds(row(cx - 1 - layer if up else layer, c, 0), cy), :],
            dst_ref=vecs.at[2 * j + 1, pl.ds(row(-1 - layer if up else cx + layer, c, 0), cy), :],
            send_sem=xsend.at[way], recv_sem=hrecv.at[lax.rem(j, 2), c, layer],
            device_id=(up_gx if up else down_gx, gy), device_id_type=mesh_id,
        )

    def ycopy(j, c, way):
        right = way == 0
        return pltpu.make_async_remote_copy(
            src_ref=ybuf.at[j, c, 1 if right else 0],
            dst_ref=hin.at[j, c, 0 if right else 1, pl.ds(0, 2 * cx), :],
            send_sem=ysend.at[way], recv_sem=hrecv.at[lax.rem(j, 2), c, 0],
            device_id=(gx, right_gy if right else left_gy), device_id_type=mesh_id,
        )

    def ccopy(j, c, xway, yway):
        up, right = xway == 0, yway == 0
        q = 2 * xway + yway
        return pltpu.make_async_remote_copy(
            src_ref=vecs.at[
                2 * j + 1, pl.ds(row(cx - 1 if up else 0, c, cy - 1 if right else 0), 1), :
            ],
            dst_ref=hin.at[j, c, 0 if right else 1, pl.ds(low_corner if up else high_corner, 1), :],
            send_sem=csend.at[q], recv_sem=hrecv.at[lax.rem(j, 2), c, 1],
            device_id=(up_gx if up else down_gx, right_gy if right else left_gy),
            device_id_type=mesh_id,
        )

    def vcopy(c, way):
        up = way == 0
        return pltpu.make_async_remote_copy(
            src_ref=inv.at[pl.ds(inv_row(cx - 1 if up else 0, c, 0), cy), :],
            dst_ref=inv.at[pl.ds(inv_row(-1 if up else cx, c, 0), cy), :],
            send_sem=vsend.at[way], recv_sem=vrecv.at[c],
            device_id=(up_gx if up else down_gx, gy), device_id_type=mesh_id,
        )

    def hcopy(way):
        right = way == 0
        return pltpu.make_async_remote_copy(
            src_ref=pinv.at[1 if right else 0], dst_ref=hinv.at[0 if right else 1],
            send_sem=vsend.at[2 + way], recv_sem=vrecv.at[tiles],
            device_id=(gx, right_gy if right else left_gy), device_id_type=mesh_id,
        )

    for c in range(tiles):
        drained(3 * cx * cy, isem.at[c])

        @pl.loop(0, cx)
        def _(x):
            found = []
            for y in range(0, cy, 8):
                at = potential[c, x, y : y + 8, :]
                rising = jnp.exp(0.4 * at)
                falling = jnp.exp(-0.6 * at)
                label = phase[c, x, y : y + 8, :]
                rate = jnp.where(label == 1, 0.3, jnp.where(label == 2, 0.08, 0.02)).astype(F32)
                bend = 0.4 * rising + 0.6 * falling
                d = 6.0 + rate * bend
                i = 1.0 / d
                found.append((y, rising - falling, bend, d, i, source[c, x, y : y + 8, :] * i))
            for y, level, bend, d, i, v in found:
                f = pl.ds(flat_row(x, c, y), 8)
                base[f, :] = level
                slope[f, :] = bend
                diag[f, :] = d
                inv[pl.ds(inv_row(x, c, y), 8), :] = i
                vecs[1, pl.ds(row(x, c, y), 8), :] = v

        pack_rows(0, c)
        for side, y, _ in sides:
            for x in range(0, cx, 8):
                pinv[side, c, pl.ds(x, 8), :] = inv[pl.ds(inv_row(x, c, y), 8, stride=cy), :]

    def launch_x(j, c, more):
        for way, there in ((0, has_up), (1, has_down)):
            @pl.when(there & more)
            def _():
                pl.when(has_right)(ccopy(j, c, way, 0).start)
                pl.when(has_left)(ccopy(j, c, way, 1).start)
                xcopy(j, c, way, 0).start()
                xcopy(j, c, way, 1).start()

    def launch_y(j, c, more):
        pl.when(has_right & more)(ycopy(j, c, 0).start)
        pl.when(has_left & more)(ycopy(j, c, 1).start)

    def landed_near(j, c):
        taken(hrecv.at[lax.rem(j, 2), c, 0], lambda a, b: a * cy + b * 2 * cx)

    def landed_far(j, c):
        taken(hrecv.at[lax.rem(j, 2), c, 1], lambda a, b: a * (cy + b))

        @pl.when(j == 0)
        def _():
            taken(vrecv.at[c], lambda a, b: a * cy)

    with jax.named_scope("barrier"):
        pl.semaphore_wait(barrier, total - 1)

    always = gx >= 0
    for c in range(tiles):
        launch_x(0, c, always)
        launch_y(0, c, always)
        pl.when(has_up)(vcopy(c, 0).start)
        pl.when(has_down)(vcopy(c, 1).start)
        if c == 0:
            pl.when(has_right)(hcopy(0).start)
            pl.when(has_left)(hcopy(1).start)

    groups = places.shape[0]
    wide = groups // n_gy
    drained(table.shape[0] * ROWS + 2 * groups, isem.at[tiles])
    pltpu.make_async_copy(count_hbm, count, isem.at[tiles + 1]).wait()
    lines[...] = places[...] >> 7
    scalar_lines = pltpu.make_async_copy(lines, voxel, isem.at[tiles + 2])
    scalar_lines.start()

    @pl.loop(-1, cx + 1)
    def _(x):
        for c in range(tiles):
            for y in range(0, cy, 8):
                vecs[0, pl.ds(row(x, c, y), 8), :] = zeros8

    @pl.loop(0, cycles)
    def _(j):
        @pl.loop(0, cx + 1)
        def _(x):
            for c in range(tiles):
                vecs[2 * j + 1, pl.ds(row(x, c, -PAD), 8), :] = zeros8

    hodd[...] = jnp.zeros(hodd.shape, F32)
    for beyond, x in ((gx == 0, -1), (gx == n_gx - 1, cx)):
        @pl.when(beyond)
        def _():
            for c in range(tiles):
                for y in range(0, cy, 8):
                    inv[pl.ds(inv_row(x, c, y), 8), :] = zeros8

            @pl.loop(0, cycles)
            def _(j):
                for c in range(tiles):
                    first = row(-2 if x < 0 else cx, c, 0)
                    for y in range(0, pitch + cy, 8):
                        vecs[2 * j + 1, pl.ds(first + y, 8), :] = zeros8
                    for side in range(2):
                        hin[j, c, side, pl.ds(low_corner if x < 0 else high_corner, 1), :] = zero_row

    for beyond, side in ((gy == 0, 0), (gy == n_gy - 1, 1)):
        @pl.when(beyond)
        def _():
            hinv[side] = jnp.zeros(hinv.shape[1:], F32)

            @pl.loop(0, cycles)
            def _(j):
                for c in range(tiles):
                    hin[j, c, side] = jnp.zeros(hin.shape[3:], F32)

    def build_masks():
        @pl.loop(0, n_gy)
        def _(peer):
            live = count[peer]
            lanes = lax.broadcasted_iota(jnp.int32, (128, 128), 1)
            rows = lax.broadcasted_iota(jnp.int32, (128, 128), 0)
            for part in range(wide):
                at = (places[pl.ds(peer * wide + part, 1), :] & 127).astype(F32)
                at = jnp.broadcast_to(at, (128, 128)).T
                mask[peer * wide + part] = jnp.where(
                    (lanes.astype(F32) == at) & (rows + 128 * part < live), 0.5, 0.0
                )

    lane8 = lax.broadcasted_iota(jnp.int32, (8, 128), 1)
    sub8 = lax.broadcasted_iota(jnp.int32, (8, 128), 0)
    first_lane, last_lane = lane8 == 0, lane8 == 127

    def beside(v, before, after):
        z = pltpu.roll(jnp.where(last_lane, before, v), 1, 1)
        return z + pltpu.roll(jnp.where(first_lane, after, v), 127, 1)

    def sweep(k, runs, scale, carry, more=lambda: ()):
        centers = {}

        def center(run, c, start, o, y):
            if (run, o, y) not in centers:
                centers[run, o, y] = vecs[k, pl.ds(row(start + o, c, y), 8), :]
            return centers[run, o, y]

        found = []
        for run, (c, start, offsets, counted) in enumerate(runs):
            for y in range(0, cy, 8):
                for o in offsets:
                    r = row(start + o, c, y)
                    v = center(run, c, start, o, y)
                    before = vecs[k, pl.ds(r - block, 8), :] if c > 0 else 0.0
                    after = vecs[k, pl.ds(r + block, 8), :] if c < tiles - 1 else 0.0
                    n = vecs[k, pl.ds(r - 1, 8), :] + vecs[k, pl.ds(r + 1, 8), :]
                    n = n + (center(run, c, start, o - 1, y) + center(run, c, start, o + 1, y))
                    n = n + beside(v, before, after)
                    i = inv[pl.ds(inv_row(start + o, c, y), 8), :]
                    new = (scale * i) * n - vecs[k - 1, pl.ds(r, 8), :]
                    if counted:
                        w = diag[pl.ds(flat_row(start + o, c, y), 8), :] * v
                        carry = (carry[0] + w * v, carry[1] + w * new)
                    found.append((r, new))
        others = more()
        for r, new in found:
            vecs[k + 1, pl.ds(r, 8), :] = new
        for store in others:
            store()
        return carry

    def inner(k, c, first, last, scale, carry):
        group = max(g for g in range(1, 8) if (last - first) % g == 0)

        def some(i, a):
            return sweep(k, [(c, group * i + first, range(group), True)], scale, a)

        return lax.fori_loop(0, (last - first) // group, some, carry)

    def rows_beyond(j, c, scale):
        k = 2 * j + 1
        stores = []
        for side, beyond in ((0, -1), (1, cy)):
            for x in range(0, cx, 8):
                at = pl.ds(near + x, 8)
                h = hin[j, c, side, at, :]
                before = hin[j, c - 1, side, at, :] if c > 0 else 0.0
                after = hin[j, c + 1, side, at, :] if c < tiles - 1 else 0.0
                lower = hin[j, c, side, pl.ds(near + x - 1, 8), :]
                if x == 0:
                    corner = hin[j, c, side, pl.ds(low_corner, 1), :]
                    lower = jnp.where(sub8 == 0, corner, lower)
                upper = hin[j, c, side, pl.ds(near + x + 1, 8), :]
                n = (lower + upper) + (hin[j, c, side, pl.ds(x, 8), :] + ybuf[j, c, side, at, :])
                n = n + beside(h, before, after)
                old = pl.ds(x, 8)
                new = (scale * hinv[side, c, old, :]) * n - hodd[side, c, old, :]

                def store(side=side, old=old, new=new, line=row(x, c, beyond)):
                    hodd[side, c, old, :] = new
                    vecs[k + 1, pl.ds(line, 8, stride=pitch), :] = new

                stores.append(store)
        return stores

    def outside(j, border, shell, scale, carry):
        k = 2 * j + 1
        runs, more = [], lambda: ()
        if border is not None:
            runs += [(border, 0, (0,), True), (border, cx - 1, (0,), True)]
        if shell is not None:
            for side, y in ((0, -1), (1, cy)):
                for x, at in ((-1, low_corner), (cx, high_corner)):
                    vecs[k, pl.ds(row(x, shell, y), 1), :] = hin[j, shell, side, pl.ds(at, 1), :]
            runs += [(shell, -1, (0,), False), (shell, cx, (0,), False)]
            more = functools.partial(rows_beyond, j, shell, scale)
        carry = sweep(k, runs, scale, carry, more)
        if border is None:
            return carry
        own, cross = carry
        found = []
        for side, y, _ in sides:
            for x in range(0, cx, 8):
                at = pl.ds(near + x, 8)
                h = hin[j, border, side, at, :]
                line = pl.ds(row(x, border, y), 8, stride=pitch)
                fixed = vecs[k + 1, line, :] + (scale * pinv[side, border, pl.ds(x, 8), :]) * h
                cross = cross + (scale * ybuf[j, border, side, at, :]) * h
                found.append((line, fixed))
        for line, fixed in found:
            vecs[k + 1, line, :] = fixed
        return own, cross

    def finish(j, c, carry):
        k = 2 * j + 2
        more = j < cycles - 1
        carry = sweep(k, [(c, 0, (0, 1), True), (c, cx - 2, (0, 1), True)], 2.0, carry)
        launch_x(j + 1, c, more)
        carry = inner(k, c, 2, cx - 2, 2.0, carry)

        @pl.when(more)
        def _():
            pack_rows(j + 1, c)
            launch_y(j + 1, c, always)

        return carry

    def local_sums(numbers):
        sums = []
        for g in numbers:
            level = [dots[pl.ds(64 * g + i, 8, stride=8), :] for i in range(8)]
            level = [two_sum(level[2 * i], level[2 * i + 1]) for i in range(4)]
            sums.append(dd_sum(level))
        for shift in (64, 32, 16, 8, 4, 2, 1):
            sums = [
                loose_add(a, tuple(pltpu.roll(p, shift, 1) for p in a)) for a in sums
            ]
        sums = [quick_two_sum(*a) for a in sums]
        spread = zeros8
        for g, (hi, lo) in zip(numbers, sums):
            spread = jnp.where(lane8 == sub8 + 8 * g, hi, spread)
            spread = jnp.where(lane8 == sub8 + 8 * g + LOW, lo, spread)
        return jnp.sum(spread, axis=0, keepdims=True)

    def share(which, line):
        mine[which] = line
        parts[which, pl.ds(me, 1), :] = line
        everyone(
            lambda to_gx, to_gy: pltpu.make_async_remote_copy(
                src_ref=mine.at[which], dst_ref=parts.at[which, pl.ds(me, 1), :],
                send_sem=rsend, recv_sem=rrecv.at[which],
                device_id=(to_gx, to_gy), device_id_type=mesh_id,
            ).start()
        )

    def shared(which):
        drained(total - 1, rrecv.at[which])
        level = [parts[which, 8 * i : 8 * i + 8, :] for i in range(total // 8)]
        every = dd_sum([(a, pltpu.roll(a, 128 - LOW, 1)) for a in level])
        for shift in (4, 2, 1):
            every = loose_add(every, tuple(pltpu.roll(p, shift, 0) for p in every))
        return quick_two_sum(*every)

    numbers = range(2 * s // 8)
    late_group = (2 * s - LATE) // 8
    dots[pl.ds(8 * (2 * s - LATE), 8 * LATE), :] = jnp.zeros((8 * LATE, 128), F32)

    @pl.loop(0, cycles)
    def _(j):
        with jax.named_scope("cycle"):
            scale = jnp.where(j == 0, 1.0, 2.0).astype(F32)
            first = second = (zeros8, zeros8)
            with jax.named_scope("ainner"):
                for c in range(tiles):
                    first = inner(2 * j + 1, c, 1, cx - 1, scale, first)

            pl.when(j == 0)(build_masks)

            @pl.when(j == cycles - 1)
            def _():
                share(0, local_sums(numbers))

            @pl.when(j == 0)
            def _():
                taken(vrecv.at[tiles], lambda a, b: b * tiles * cx)

            with jax.named_scope("landed"):
                landed_near(j, 0)
            first = outside(j, 0, None, scale, first)
            for c in range(tiles):
                following = c + 1 if c + 1 < tiles else None
                with jax.named_scope("landed"):
                    if following is not None:
                        landed_near(j, following)
                    landed_far(j, c)
                first = outside(j, following, c, scale, first)
                second = finish(j, c, second)
            for i, value in enumerate((*first, *second)):
                dots[pl.ds(pl.multiple_of(32 * j + 8 * i, 8), 8), :] = value

    scalar_lines.wait()

    with jax.named_scope("reduce"):
        share(1, local_sums(numbers[late_group:]))

        for way, there in ((0, has_up), (1, has_down)):
            @pl.when(there)
            def _():
                drained(cycles * tiles * 2 * cy, xsend.at[way])
                drained(tiles * cy, vsend.at[way])
                for q, also in ((0, has_right), (1, has_left)):
                    @pl.when(also)
                    def _():
                        drained(cycles * tiles, csend.at[2 * way + q])

        for way, there in ((0, has_right), (1, has_left)):
            @pl.when(there)
            def _():
                drained(cycles * tiles * 2 * cx, ysend.at[way])
                drained(tiles * cx, vsend.at[2 + way])

        early = dd_sum(weighted(table, shared(0), range(2 * s - LATE)))
        reduced = dd_eliminate((early[0] + table[2 * s], early[1]), s - 2)

    with jax.named_scope("solve"):
        weights = dd_finish(table, early, reduced, shared(1))

    with jax.named_scope("combine"):
        @pl.loop(0, cx)
        def _(x):
            for c in range(tiles):
                for y in range(0, cy, 8):
                    pieces = [
                        w * vecs[1 + k, pl.ds(row(x, c, y), 8), :] for k, w in enumerate(weights)
                    ]
                    while len(pieces) > 1:
                        pieces = [sum(pieces[i : i + 2]) for i in range(0, len(pieces), 2)]
                    out[x, y : y + 8, 128 * c : 128 * (c + 1)] = pieces[0]
                    f = pl.ds(flat_row(x, c, y), 8)
                    at = (x * cy + y) * tiles + c
                    flat[pl.ds(at, 8, stride=tiles), :] = base[f, :] + slope[f, :] * pieces[0]

    picks = (pick0, pick1)

    def fetch(peer, pick):
        for part in range(wide):
            for i in range(128):
                pick[pl.ds(128 * part + i, 1), :] = flat[pl.ds(voxel[peer * wide + part, i], 1), :]

    def pass_on(peer, pick):
        for part in range(wide):
            value = pick[128 * part : 128 * (part + 1), :] * mask[peer * wide + part]
            sent[peer, pl.ds(part, 1), :] = jnp.sum(value.T, axis=0, keepdims=True)

    def give(peer):
        pltpu.make_async_remote_copy(
            src_ref=sent.at[peer], dst_ref=got.at[gy], send_sem=lsend, recv_sem=lrecv.at[gy],
            device_id=(gx, peer), device_id_type=mesh_id,
        ).start()

    def peer_at(step):
        return flipped(gy, n_gy - 1 - step, n_gy)

    with jax.named_scope("gather"):
        fetch(peer_at(0), picks[0])

        @pl.loop(0, n_gy // 2 - 2)
        def _(i):
            pass_on(peer_at(2 * i), picks[0])
            fetch(peer_at(2 * i + 1), picks[1])
            give(peer_at(2 * i))
            pass_on(peer_at(2 * i + 1), picks[1])
            fetch(peer_at(2 * i + 2), picks[0])
            give(peer_at(2 * i + 1))

        pass_on(peer_at(n_gy - 4), picks[0])
        fetch(peer_at(n_gy - 3), picks[1])
        give(peer_at(n_gy - 4))
        pass_on(peer_at(n_gy - 3), picks[1])
        give(peer_at(n_gy - 3))
        fetch(peer_at(n_gy - 2), picks[0])
        pass_on(peer_at(n_gy - 2), picks[0])
        give(peer_at(n_gy - 2))
        fetch(gy, picks[1])
        pass_on(gy, picks[1])
        got[gy] = sent[gy]

    own = tally.shape[0]

    def tallied(peer, first):
        spots = [target[pl.ds(peer * wide + part, 1), :] for part in range(wide)]
        values = [got[peer, part : part + 1, :] for part in range(wide)]
        for start in range(0, own, 128):
            found = []
            for r in range(start, start + 128, 8):
                total_ = zeros8 if first else tally[r : r + 8, :]
                for spot, value in zip(spots, values):
                    total_ = total_ + jnp.where(spot == sub8 + r, value, 0.0)
                found.append((r, total_))
            for r, total_ in found:
                tally[r : r + 8, :] = total_

    with jax.named_scope("links"):
        tallied(gy, True)
        drained(2 * (total - 1), rsend)

        @pl.loop(0, n_gy - 1)
        def _(step):
            peer = flipped(gy, n_gy - 1 - step, n_gy)
            pltpu.make_async_copy(got.at[peer], got.at[peer], lrecv.at[peer]).wait()
            tallied(peer, False)

        for start in range(0, own, 128):
            particle[0, :, start : start + 128] = jnp.sum(
                tally[start : start + 128, :].T, axis=0, keepdims=True
            )
        drained((n_gy - 1) * wide, lsend)


def kept(x):
    return pltpu.with_memory_space_constraint(x, pltpu.HBM)


def shards(sizes, source, voxel_phase, lin_potential, link_voxel, link_count, link_target):
    cx, cy, cz = source.shape
    total = sizes[0] * sizes[1]
    s = ITERS
    tiles = cz // 128
    voxels = cx * cy * tiles
    padded = (cx + 4) * tiles * (cy + PAD) + 8
    cycles = s // 2
    places = link_voxel[0, 0].reshape(-1, 128)
    peers = link_count.shape[2]
    slots = link_voxel.shape[2]
    groups = slots // 128
    whole = pl.BlockSpec(memory_space=pltpu.VMEM)
    far = pl.BlockSpec(memory_space=pltpu.HBM)
    found, sums = pl.pallas_call(
        functools.partial(kernel, sizes),
        out_shape=(
            jax.ShapeDtypeStruct(source.shape, F32),
            jax.ShapeDtypeStruct((1, 1, PART_DEV), F32),
        ),
        in_specs=[far] * 7,
        out_specs=(whole, whole),
        scratch_shapes=[
            pltpu.VMEM((tiles, cx, cy, 128), F32),
            pltpu.VMEM((tiles, cx, cy, 128), jnp.int32),
            pltpu.VMEM((tiles, cx, cy, 128), F32),
            pltpu.VMEM((2 * s + 1, ROWS, 128), F32),
            pltpu.VMEM((groups, 128), jnp.int32),
            pltpu.SMEM((groups, 128), jnp.int32),
            pltpu.VMEM((groups, 128), jnp.int32),
            pltpu.SMEM((peers,), jnp.int32),
            pltpu.VMEM((groups, 128), jnp.int32),
            pltpu.VMEM((s + 2, padded, 128), F32),
            pltpu.VMEM((voxels, 128), F32),
            pltpu.VMEM((tiles * (cx + 2) * cy, 128), F32),
            pltpu.VMEM((voxels, 128), F32),
            pltpu.VMEM((voxels, 128), F32),
            pltpu.VMEM((cycles, tiles, 2, 2 * cx, 128), F32),
            pltpu.VMEM((cycles, tiles, 2, 2 * cx + 8, 128), F32),
            pltpu.VMEM((2, tiles, cx, 128), F32),
            pltpu.VMEM((2, tiles, cx, 128), F32),
            pltpu.VMEM((2, tiles, cx, 128), F32),
            pltpu.VMEM((groups, 128, 128), F32),
            pltpu.VMEM((2 * s * 8, 128), F32),
            pltpu.VMEM((2, 1, 128), F32),
            pltpu.VMEM((2, total, 128), F32),
            pltpu.VMEM((groups // peers * 128, 128), F32),
            pltpu.VMEM((groups // peers * 128, 128), F32),
            pltpu.VMEM((voxels, 128), F32),
            pltpu.VMEM((peers, groups // peers, 128), F32),
            pltpu.VMEM((peers, groups // peers, 128), F32),
            pltpu.VMEM((PART_DEV, 128), F32),
            pltpu.SemaphoreType.DMA((tiles + 3,)),
            pltpu.SemaphoreType.DMA((2,)),
            pltpu.SemaphoreType.DMA((2,)),
            pltpu.SemaphoreType.DMA((4,)),
            pltpu.SemaphoreType.DMA((2, tiles, 2)),
            pltpu.SemaphoreType.DMA((4,)),
            pltpu.SemaphoreType.DMA((tiles + 1,)),
            pltpu.SemaphoreType.DMA,
            pltpu.SemaphoreType.DMA((2,)),
            pltpu.SemaphoreType.DMA,
            pltpu.SemaphoreType.DMA((peers,)),
        ],
        compiler_params=pltpu.CompilerParams(
            collective_id=0, has_side_effects=True, vmem_limit_bytes=52 * 2**20
        ),
    )(
        kept(source), kept(voxel_phase), kept(lin_potential), kept(jnp.asarray(gram_map())),
        kept(places), kept(link_count[0, 0]), kept(link_target[0, 0].reshape(groups, 128)),
    )
    return pl.pallas_call(
        last_kernel,
        out_shape=(
            jax.ShapeDtypeStruct(source.shape, F32),
            jax.ShapeDtypeStruct((1, 1, PART_DEV), F32),
        ),
        in_specs=[pl.BlockSpec(memory_space=pl.ANY)] * 2,
        out_specs=(far, far),
        scratch_shapes=[pltpu.SemaphoreType.DMA((2,))],
        compiler_params=pltpu.CompilerParams(vmem_limit_bytes=2 * 2**20),
    )(found, sums)


def solution(mesh):
    spec = P("gx", "gy", None)
    return jax.shard_map(
        functools.partial(shards, (mesh.shape["gx"], mesh.shape["gy"])),
        mesh=mesh,
        in_specs=(spec,) * 6,
        out_specs=(spec, spec),
        check_vma=False,
    )
```
